32 devices in a mesh: fsdp: 4 (over z), ctx: 4 (over y, core), tp: 2 (over x).
Axes of the slice: x: 2, y: 2, z: 4, core: 2. Of those that a mesh axis runs over, the one named last changes fastest.
Arguments:
- layer_input: bfloat16 [4, 2048, 768], P('fsdp', 'ctx'), may hold values from -6 to 6
- cotangent: bfloat16 [4, 2048, 768], P('fsdp', 'ctx'), may hold values from -6 to 6
- segments: int32 [4, 2048], P('fsdp'), may hold values from 0 to 2047, as said below
- slot_order: int32 [4, 8], P('fsdp'), may hold values from 0 to 7, as said below
- first_gain: bfloat16 [768], P(('fsdp', 'ctx')), may hold values from 0.25 to 1.75
- first_shift: bfloat16 [768], P(('fsdp', 'ctx')), may hold values from -3 to 3
- project_weight: bfloat16 [768, 3, 768], P(('fsdp', 'ctx'), None, 'tp'), may hold values from -0.21875 to 0.21875
- project_bias: bfloat16 [2, 768], P(None, 'tp'), may hold values from -4 to 4
- output_weight: bfloat16 [768, 768], P('tp', ('fsdp', 'ctx')), may hold values from -1.5 to 1.5
- output_bias: bfloat16 [768], P(('fsdp', 'ctx')), may hold values from -3 to 3
- second_gain: bfloat16 [768], P(('fsdp', 'ctx')), may hold values from 0.25 to 1.75
- second_shift: bfloat16 [768], P(('fsdp', 'ctx')), may hold values from -3 to 3
- expand_weight: bfloat16 [768, 3072], P(('fsdp', 'ctx'), 'tp'), may hold values from -0.21875 to 0.21875
- expand_bias: bfloat16 [3072], P('tp'), may hold values from -4 to 4
- shrink_weight: bfloat16 [3072, 768], P('tp', ('fsdp', 'ctx')), may hold values from -0.109375 to 0.109375
- shrink_bias: bfloat16 [768], P(('fsdp', 'ctx')), may hold values from -3 to 3
Outputs:
- layer_output: bfloat16 [4, 2048, 768], P('fsdp', 'ctx')
- input_delta: float32 [4, 2048, 768], P('fsdp', 'ctx')
- first_gain_delta: float32 [768], P(('fsdp', 'ctx'))
- first_shift_delta: float32 [768], P(('fsdp', 'ctx'))
- project_weight_delta: float32 [768, 3, 768], P(('fsdp', 'ctx'), None, 'tp')
- project_bias_delta: float32 [2, 768], P(None, 'tp')
- output_weight_delta: float32 [768, 768], P('tp', ('fsdp', 'ctx'))
- output_bias_delta: float32 [768], P(('fsdp', 'ctx'))
- second_gain_delta: float32 [768], P(('fsdp', 'ctx'))
- second_shift_delta: float32 [768], P(('fsdp', 'ctx'))
- expand_weight_delta: float32 [768, 3072], P(('fsdp', 'ctx'), 'tp')
- expand_bias_delta: float32 [3072], P('tp')
- shrink_weight_delta: float32 [3072, 768], P('tp', ('fsdp', 'ctx'))
- shrink_bias_delta: float32 [768], P(('fsdp', 'ctx'))
The draws below stay inside these ranges and needn't reach their ends.
Inputs may be any that keep to these rules, and one draw needn't show every extreme that they name: `segments`: taken in the order of positions (slot s of a sequence holds the 256 positions from slot_order[s] * 256 on), the sequence is cut into documents that follow one another; every token's segment number is the position of its document's last token; a document spans at most 800 positions and at least 60 unless it ends its sequence; every sequence has one document of exactly 800. `slot_order`: each row is a permutation.
All inputs are finite; a program needn't handle non-finite values.
Results may differ from the reference program's by a relative error of at most 0.02.
Values may be sent and summed in bfloat16 or wider, within the bound.
A program may use at most 128 MiB of HBM per device.

```python
import jax
import jax.numpy as jnp
from jax import lax

D = 768
HEADS = 12
HEAD_DIM = 64
FF = 3072
HALF = 256
DOC_MOST = 800
DOC_LEAST = 60
LENGTH = 2048
SEQS = 4
N_CTX = 4


def layout_tables(key):
    base = jax.random.fold_in(key, 41)
    order_keys = jax.random.split(jax.random.fold_in(base, 1), SEQS)
    orders = jax.vmap(lambda single: jax.random.permutation(single, 2 * N_CTX))(order_keys).astype(jnp.int32)
    count = LENGTH // DOC_LEAST + 2
    lengths = jax.random.randint(jax.random.fold_in(base, 2), (SEQS, count), DOC_LEAST, DOC_MOST + 1)
    chosen = jax.random.randint(jax.random.fold_in(base, 3), (SEQS, 1), 0, 2)
    lengths = jnp.where(jnp.arange(count)[None, :] == chosen, DOC_MOST, lengths).astype(jnp.int32)
    bounds = jnp.cumsum(lengths, axis=1).astype(jnp.int32)
    places = jnp.arange(LENGTH).astype(jnp.int32)
    numbers = jax.vmap(lambda edges: jnp.searchsorted(edges, places, side='right'))(bounds).astype(jnp.int32)
    ends = (jnp.minimum(bounds, LENGTH) - 1).astype(jnp.int32)
    labels = jnp.take_along_axis(ends, numbers, axis=1).astype(jnp.int32)
    anchor = orders[:, places // HALF] * HALF + (places % HALF)[None, :]
    segments = jnp.take_along_axis(labels, anchor, axis=1).astype(jnp.int32)
    return (orders, segments)


def draw_segments(key, part):
    return layout_tables(key)[1]


def draw_slot_order(key, part):
    return layout_tables(key)[0]


def block_levels(own_key, shape, shards, least, largest):
    level, own = 1.0, jax.random.fold_in(own_key, 6)
    for dim, shards_of in shards:
        draws = jnp.exp(jax.random.uniform(jax.random.fold_in(own, dim), (shards_of,), jnp.float32, least / len(shards), largest / len(shards)))
        level = level * jnp.repeat(draws, shape[dim] // shards_of).reshape([-1 if axis == dim else 1 for axis in range(len(shape))])
    return level


def noise(stream_key, shape, scale, reach, pieces=(), held_as=jnp.bfloat16):
    level = block_levels(stream_key, shape, pieces, -0.22, 0.18) if pieces else 1.0
    values = jax.random.normal(stream_key, shape, jnp.float32) * scale * level
    return jnp.minimum(jnp.maximum(values, -reach), reach).astype(held_as)


def setup_inputs(seed: int = 0) -> dict:
    splits = jax.random.split(jax.random.key(seed), 17)
    return {
        "layer_input": noise(splits[0], (SEQS, LENGTH, D), 1.0, 6.0, ((0, 4), (1, 4))),
        "cotangent": noise(splits[1], (SEQS, LENGTH, D), 1.0, 6.0, ((0, 4), (1, 4))),
        "segments": draw_segments(jax.random.fold_in(splits[16], 71), 0),
        "slot_order": draw_slot_order(jax.random.fold_in(splits[16], 71), 0),
        "first_gain": jnp.clip(1.0 + 0.15 * jax.random.normal(splits[4], (D,), jnp.float32), 0.25, 1.75).astype(jnp.bfloat16),
        "first_shift": noise(splits[5], (D,), 0.3, 3.0, ((0, 16),)),
        "project_weight": noise(splits[6], (D, 3, D), D ** -0.5, 0.21875, ((0, 16), (2, 2))),
        "project_bias": noise(splits[7], (2, D), 0.5, 4.0, ((1, 2),)),
        "output_weight": noise(splits[8], (D, D), (HEAD_DIM // 4) ** -0.5, 1.5, ((0, 2), (1, 16))),
        "output_bias": noise(splits[9], (D,), 0.3, 3.0, ((0, 16),)),
        "second_gain": jnp.clip(1.0 + 0.15 * jax.random.normal(splits[10], (D,), jnp.float32), 0.25, 1.75).astype(jnp.bfloat16),
        "second_shift": noise(splits[11], (D,), 0.3, 3.0, ((0, 16),)),
        "expand_weight": noise(splits[12], (D, FF), D ** -0.5, 0.21875, ((0, 16), (1, 2))),
        "expand_bias": noise(splits[13], (FF,), 0.5, 4.0, ((0, 2),)),
        "shrink_weight": noise(splits[14], (FF, D), FF ** -0.5, 0.109375, ((0, 2), (1, 16))),
        "shrink_bias": noise(splits[15], (D,), 0.3, 3.0, ((0, 16),)),
    }


@jax.custom_vjp
def low(v):
    return lax.optimization_barrier(v.astype(jnp.bfloat16)).astype(jnp.float32)

@jax.custom_vjp
def low_back(v):
    return v

def low_keep(v):
    return (low(v), None)

def low_pass(kept, grad):
    return (grad,)

def back_keep(v):
    return (v, None)

def back_low(kept, grad):
    return (low(grad),)
low.defvjp(low_keep, low_pass)
low_back.defvjp(back_keep, back_low)
EPSILON = 1e-05
SCALE = 0.125
NEGATIVE = -1000000000.0
HIGH = lax.Precision.HIGHEST

def product(left, right):
    return jnp.dot(left, right, precision=HIGH, preferred_element_type=jnp.float32)

def normalize(rows, gain, shift):
    mean = lax.optimization_barrier(jnp.mean(rows, axis=-1, keepdims=True))
    centred = rows - mean
    spread = lax.optimization_barrier(jnp.mean(centred * centred, axis=-1, keepdims=True))
    return centred * lax.rsqrt(spread + EPSILON) * gain + shift

def sequence_layer(params, rows, allowed):
    first_gain, first_shift, project_weight, project_bias, output_weight, output_bias, second_gain, second_shift, expand_weight, expand_bias, shrink_weight, shrink_bias = params
    normed = low(normalize(rows, first_gain, first_shift))
    mixed = product(normed, project_weight.reshape(D, 3 * D)).reshape(LENGTH, 3, D)
    queries = low_back(low(mixed[:, 0] + project_bias[0])).reshape(LENGTH, HEADS, HEAD_DIM)
    keys = low_back(low(mixed[:, 1])).reshape(LENGTH, HEADS, HEAD_DIM)
    values = low_back(low(mixed[:, 2] + project_bias[1])).reshape(LENGTH, HEADS, HEAD_DIM)
    scores = jnp.einsum('qhd,khd->hqk', queries, keys, precision=HIGH) * SCALE
    scores = low_back(jnp.where(allowed[None], scores, NEGATIVE))
    top = lax.optimization_barrier(jnp.max(scores, axis=-1, keepdims=True))
    raised = jnp.exp(scores - top)
    chance = low(raised / lax.optimization_barrier(jnp.sum(raised, axis=-1, keepdims=True)))
    attended = jnp.einsum('hqk,khd->qhd', chance, values, precision=HIGH).reshape(LENGTH, D)
    attended = low_back(low(attended))
    middle = rows + low_back(product(attended, output_weight)) + output_bias
    normed_two = low(normalize(middle, second_gain, second_shift))
    before = low_back(product(normed_two, expand_weight) + expand_bias)
    active = low(jax.nn.gelu(before, approximate=True))
    return middle + low_back(product(active, shrink_weight)) + shrink_bias

def reference(layer_input, cotangent, segments, slot_order, first_gain, first_shift, project_weight, project_bias, output_weight, output_bias, second_gain, second_shift, expand_weight, expand_bias, shrink_weight, shrink_bias):
    params = (first_gain.astype(jnp.float32), first_shift.astype(jnp.float32), project_weight.astype(jnp.float32), project_bias.astype(jnp.float32), output_weight.astype(jnp.float32), output_bias.astype(jnp.float32), second_gain.astype(jnp.float32), second_shift.astype(jnp.float32), expand_weight.astype(jnp.float32), expand_bias.astype(jnp.float32), shrink_weight.astype(jnp.float32), shrink_bias.astype(jnp.float32))
    places = jnp.arange(LENGTH).astype(jnp.int32)

    def one_sequence(totals, item):
        rows, slope, numbers, order = item
        position = order[places // HALF] * HALF + places % HALF
        allowed = (numbers[:, None] == numbers[None, :]) & (position[None, :] <= position[:, None])
        result, pull = jax.vjp(lambda weights, inputs: sequence_layer(weights, inputs, allowed), params, rows)
        weight_slopes, input_slope = pull(slope)
        totals = jax.tree.map(lambda left, right: left + right, totals, weight_slopes)
        return (totals, (result.astype(jnp.bfloat16), input_slope))
    zeros = jax.tree.map(jnp.zeros_like, params)
    totals, outputs = lax.scan(one_sequence, zeros, (layer_input.astype(jnp.float32), cotangent.astype(jnp.float32), segments, slot_order))
    return (outputs[0], outputs[1], totals[0], totals[1], totals[2], totals[3], totals[4], totals[5], totals[6], totals[7], totals[8], totals[9], totals[10], totals[11])
```

```python
from functools import partial

import jax
import jax.numpy as jnp
from jax import lax
from jax.experimental import pallas as pl
from jax.experimental.pallas import tpu as pltpu
from jax.sharding import PartitionSpec as P

HEAD_DIM = 64


EPSILON = 1e-05
SCALE = 0.125
NEGATIVE = -1000000000.0
TILE = 512
GELU_A = 0.7978845608028654
GELU_B = 0.044715


def contract_rows(left, right):
    return lax.dot_general(
        left, right, (((0,), (0,)), ((), ())), preferred_element_type=jnp.float32
    )


def times_transpose(left, right):
    return lax.dot_general(
        left, right, (((1,), (1,)), ((), ())), preferred_element_type=jnp.float32
    )


def normalize_parts(rows):
    mean = jnp.mean(rows, axis=-1, keepdims=True)
    centred = rows - mean
    spread = jnp.mean(centred * centred, axis=-1, keepdims=True)
    inverse = lax.rsqrt(spread + EPSILON)
    return (centred * inverse, inverse)


def norm_backward(upstream, unit, inverse, gain):
    scaled = upstream * gain
    back = inverse * (
        scaled
        - jnp.mean(scaled, axis=-1, keepdims=True)
        - unit * jnp.mean(scaled * unit, axis=-1, keepdims=True)
    )
    return (back, jnp.sum(upstream * unit, axis=0), jnp.sum(upstream, axis=0))


def split_pairs(array, pairs):
    seqs, count, width = array.shape
    span = width // pairs
    return (
        array.reshape(seqs, count, pairs, span)
        .transpose(0, 2, 1, 3)
        .reshape(seqs * pairs, count, span)
    )


def join_pairs(array, seqs):
    items, count, span = array.shape
    pairs = items // seqs
    return (
        array.reshape(seqs, pairs, count, span)
        .transpose(0, 2, 1, 3)
        .reshape(seqs, count, pairs * span)
    )


def masked_scores(query_heads, key_heads, query_place, query_group, key_place, key_group):
    scores = (
        jnp.einsum("qhd,khd->hqk", query_heads, key_heads, preferred_element_type=jnp.float32)
        * SCALE
    )
    allowed = (query_group[:, None] == key_group[None, :]) & (
        key_place[None, :] <= query_place[:, None]
    )
    return jnp.where(allowed[None], scores, NEGATIVE)


def attend_forward(
    queries, keys_all, values_all, query_places, query_groups, key_places, key_groups, pairs
):
    seqs, rows, width = queries.shape
    length = keys_all.shape[1]
    span = width // pairs
    tile = min(TILE, rows)

    def one_item(item):
        query_part, key_part, value_part, index = item
        which = index // pairs
        query_place = lax.dynamic_index_in_dim(query_places, which, 0, keepdims=False)
        query_group = lax.dynamic_index_in_dim(query_groups, which, 0, keepdims=False)
        key_place = lax.dynamic_index_in_dim(key_places, which, 0, keepdims=False)
        key_group = lax.dynamic_index_in_dim(key_groups, which, 0, keepdims=False)
        key_heads = key_part.reshape(length, 2, span // 2)
        value_heads = value_part.reshape(length, 2, span // 2)
        results, tops, totals = ([], [], [])
        query_heads = query_part.reshape(tile, 2, span // 2)
        scores = masked_scores(
            query_heads, key_heads, query_place, query_group, key_place, key_group
        )
        top = jnp.max(scores, axis=-1)
        raised = jnp.exp(scores - top[..., None])
        total = jnp.sum(raised, axis=-1)
        chance = (raised / total[..., None]).astype(jnp.bfloat16)
        mixed = jnp.einsum("hqk,khd->qhd", chance, value_heads, preferred_element_type=jnp.float32)
        results.append(mixed.reshape(tile, span).astype(jnp.bfloat16))
        tops.append(top)
        totals.append(total)
        return (
            jnp.concatenate(results, axis=0),
            jnp.concatenate(tops, axis=1),
            jnp.concatenate(totals, axis=1),
        )

    items = (
        split_pairs(queries, pairs),
        split_pairs(keys_all, pairs),
        split_pairs(values_all, pairs),
        jnp.arange(seqs * pairs, dtype=jnp.int32),
    )
    mixed, tops, totals = lax.map(one_item, items)
    return (join_pairs(mixed, seqs), tops, totals)


def attend_backward(
    queries,
    keys_all,
    values_all,
    attended_slope,
    tops,
    totals,
    query_places,
    query_groups,
    key_places,
    key_groups,
    pairs,
):
    seqs, rows, width = queries.shape
    length = keys_all.shape[1]
    span = width // pairs
    tile = min(TILE, rows)

    def one_item(item):
        query_part, key_part, value_part, slope_part, top, total, index = item
        which = index // pairs
        query_place = lax.dynamic_index_in_dim(query_places, which, 0, keepdims=False)
        query_group = lax.dynamic_index_in_dim(query_groups, which, 0, keepdims=False)
        key_place = lax.dynamic_index_in_dim(key_places, which, 0, keepdims=False)
        key_group = lax.dynamic_index_in_dim(key_groups, which, 0, keepdims=False)
        key_heads = key_part.reshape(length, 2, span // 2)
        value_heads = value_part.reshape(length, 2, span // 2)
        key_total = jnp.zeros((length, 2, span // 2), jnp.float32)
        value_total = jnp.zeros((length, 2, span // 2), jnp.float32)
        query_heads = query_part.reshape(tile, 2, span // 2)
        slope_heads = slope_part.reshape(tile, 2, span // 2)
        scores = masked_scores(
            query_heads, key_heads, query_place, query_group, key_place, key_group
        )
        chance = jnp.exp(scores - top[:, 0:tile, None]) / total[:, 0:tile, None]
        chance_low = chance.astype(jnp.bfloat16)
        value_total = value_total + jnp.einsum(
            "hqk,qhd->khd", chance_low, slope_heads, preferred_element_type=jnp.float32
        )
        pulled = jnp.einsum(
            "qhd,khd->hqk", slope_heads, value_heads, preferred_element_type=jnp.float32
        )
        score_slope = (chance * (pulled - jnp.sum(chance * pulled, axis=-1, keepdims=True))).astype(
            jnp.bfloat16
        )
        query_step = (
            jnp.einsum("hqk,khd->qhd", score_slope, key_heads, preferred_element_type=jnp.float32)
            * SCALE
        )
        query_results = [query_step.reshape(tile, span).astype(jnp.bfloat16)]
        key_total = (
            key_total
            + jnp.einsum(
                "hqk,qhd->khd", score_slope, query_heads, preferred_element_type=jnp.float32
            )
            * SCALE
        )
        return (
            jnp.concatenate(query_results, axis=0),
            key_total.reshape(length, span),
            value_total.reshape(length, span),
        )

    items = (
        split_pairs(queries, pairs),
        split_pairs(keys_all, pairs),
        split_pairs(values_all, pairs),
        split_pairs(attended_slope, pairs),
        tops,
        totals,
        jnp.arange(seqs * pairs, dtype=jnp.int32),
    )
    query_slope, key_part, value_part = lax.map(one_item, items)
    return (join_pairs(query_slope, seqs), join_pairs(key_part, seqs), join_pairs(value_part, seqs))


def on_device(
    layer_input,
    cotangent,
    segments,
    slot_order,
    first_gain,
    first_shift,
    project_weight,
    project_bias,
    output_weight,
    output_bias,
    second_gain,
    second_shift,
    expand_weight,
    expand_bias,
    shrink_weight,
    shrink_bias,
):
    seqs, rows, model_width = layer_input.shape
    count = seqs * rows
    half = rows // 2
    length = rows * lax.axis_size("ctx")
    begin = lax.axis_index("ctx") * rows
    local_width = project_weight.shape[2]
    pairs = local_width // (2 * HEAD_DIM)
    (
        gain_one,
        shift_one,
        project_full,
        output_full,
        out_bias,
        gain_two,
        shift_two,
        expand_full,
        shrink_full,
        shrink_add,
    ) = (
        lax.all_gather(first_gain, ("fsdp", "ctx"), axis=0, tiled=True),
        lax.all_gather(first_shift, ("fsdp", "ctx"), axis=0, tiled=True),
        lax.all_gather(project_weight, ("fsdp", "ctx"), axis=0, tiled=True),
        lax.all_gather(output_weight, ("fsdp", "ctx"), axis=1, tiled=True),
        lax.all_gather(output_bias, ("fsdp", "ctx"), axis=0, tiled=True),
        lax.all_gather(second_gain, ("fsdp", "ctx"), axis=0, tiled=True),
        lax.all_gather(second_shift, ("fsdp", "ctx"), axis=0, tiled=True),
        lax.all_gather(expand_weight, ("fsdp", "ctx"), axis=0, tiled=True),
        lax.all_gather(shrink_weight, ("fsdp", "ctx"), axis=1, tiled=True),
        lax.all_gather(shrink_bias, ("fsdp", "ctx"), axis=0, tiled=True),
    )
    offsets = jnp.arange(half, dtype=jnp.int32)
    key_places = (slot_order[:, :, None] * half + offsets[None, None, :]).reshape(seqs, length)
    query_places = lax.dynamic_slice_in_dim(key_places, begin, rows, 1)
    query_groups = lax.dynamic_slice_in_dim(segments, begin, rows, 1)
    inputs = layer_input.reshape(count, model_width).astype(jnp.float32)
    unit_one, inverse_one = normalize_parts(inputs)
    normed_one = (unit_one * gain_one.astype(jnp.float32) + shift_one.astype(jnp.float32)).astype(
        jnp.bfloat16
    )
    project_flat = project_full.reshape(model_width, 3 * local_width)
    mixed = jnp.dot(normed_one, project_flat, preferred_element_type=jnp.float32).reshape(
        count, 3, local_width
    )
    bias_pair = project_bias.astype(jnp.float32)
    queries = (mixed[:, 0] + bias_pair[0]).astype(jnp.bfloat16).reshape(seqs, rows, local_width)
    keys = mixed[:, 1].astype(jnp.bfloat16).reshape(seqs, rows, local_width)
    values = (mixed[:, 2] + bias_pair[1]).astype(jnp.bfloat16).reshape(seqs, rows, local_width)
    keys_all, values_all = (
        lax.all_gather(keys, "ctx", axis=1, tiled=True),
        lax.all_gather(values, "ctx", axis=1, tiled=True),
    )
    attended, tops, totals = attend_forward(
        queries, keys_all, values_all, query_places, query_groups, key_places, segments, pairs
    )
    attended_flat = attended.reshape(count, local_width)
    branch = lax.psum(jnp.dot(attended_flat, output_full, preferred_element_type=jnp.float32), "tp")
    middle = inputs + branch + out_bias.astype(jnp.float32)
    unit_two, inverse_two = normalize_parts(middle)
    normed_two = (unit_two * gain_two.astype(jnp.float32) + shift_two.astype(jnp.float32)).astype(
        jnp.bfloat16
    )
    before = jnp.dot(
        normed_two, expand_full, preferred_element_type=jnp.float32
    ) + expand_bias.astype(jnp.float32)
    active_value, gelu_pull = jax.vjp(partial(jax.nn.gelu, approximate=True), before)
    active = active_value.astype(jnp.bfloat16)
    feed = lax.psum(
        jnp.dot(active, shrink_full, preferred_element_type=jnp.float32).astype(jnp.bfloat16), "tp"
    ).astype(jnp.float32)
    layer_output = (
        (middle + feed + shrink_add.astype(jnp.float32))
        .astype(jnp.bfloat16)
        .reshape(seqs, rows, model_width)
    )
    gain_back, project_again, output_back, gain_two_back, expand_back, shrink_back = (
        lax.all_gather(first_gain, ("fsdp", "ctx"), axis=0, tiled=True),
        lax.all_gather(project_weight, ("fsdp", "ctx"), axis=0, tiled=True),
        lax.all_gather(output_weight, ("fsdp", "ctx"), axis=1, tiled=True),
        lax.all_gather(second_gain, ("fsdp", "ctx"), axis=0, tiled=True),
        lax.all_gather(expand_weight, ("fsdp", "ctx"), axis=0, tiled=True),
        lax.all_gather(shrink_weight, ("fsdp", "ctx"), axis=1, tiled=True),
    )
    project_back = project_again.reshape(model_width, 3 * local_width)
    slope = cotangent.reshape(count, model_width).astype(jnp.float32)
    shrink_bias_delta = jnp.sum(slope, axis=0)
    slope_low = slope.astype(jnp.bfloat16)
    shrink_weight_delta = contract_rows(active, slope_low)
    active_slope = times_transpose(slope_low, shrink_back)
    before_slope = gelu_pull(active_slope)[0].astype(jnp.bfloat16)
    expand_bias_delta = jnp.sum(before_slope.astype(jnp.float32), axis=0)
    expand_weight_delta = contract_rows(normed_two, before_slope)
    normed_two_slope = lax.psum(
        times_transpose(before_slope, expand_back).astype(jnp.bfloat16), "tp"
    ).astype(jnp.float32)
    back_two, gain_two_delta, shift_two_delta = norm_backward(
        normed_two_slope, unit_two, inverse_two, gain_two_back.astype(jnp.float32)
    )
    middle_slope = slope + back_two
    output_bias_delta = jnp.sum(middle_slope, axis=0)
    middle_low = middle_slope.astype(jnp.bfloat16)
    output_weight_delta = contract_rows(attended_flat, middle_low)
    attended_slope = (
        times_transpose(middle_low, output_back)
        .astype(jnp.bfloat16)
        .reshape(seqs, rows, local_width)
    )
    query_slope, key_part, value_part = attend_backward(
        queries,
        keys_all,
        values_all,
        attended_slope,
        tops,
        totals,
        query_places,
        query_groups,
        key_places,
        segments,
        pairs,
    )
    key_slope, value_slope = (
        lax.psum_scatter(
            key_part.astype(jnp.bfloat16), "ctx", scatter_dimension=1, tiled=True
        ).astype(jnp.float32),
        lax.psum_scatter(
            value_part.astype(jnp.bfloat16), "ctx", scatter_dimension=1, tiled=True
        ).astype(jnp.float32),
    )
    key_low = key_slope.astype(jnp.bfloat16)
    value_low = value_slope.astype(jnp.bfloat16)
    project_slope = jnp.stack([query_slope, key_low, value_low], axis=2).reshape(
        count, 3 * local_width
    )
    project_weight_delta = contract_rows(normed_one, project_slope).reshape(
        model_width, 3, local_width
    )
    project_bias_delta = jnp.stack(
        [
            jnp.sum(query_slope.reshape(count, local_width).astype(jnp.float32), axis=0),
            jnp.sum(value_low.reshape(count, local_width).astype(jnp.float32), axis=0),
        ]
    )
    normed_one_slope = lax.psum(
        times_transpose(project_slope, project_back).astype(jnp.bfloat16), "tp"
    ).astype(jnp.float32)
    back_one, gain_one_delta, shift_one_delta = norm_backward(
        normed_one_slope, unit_one, inverse_one, gain_back.astype(jnp.float32)
    )
    input_delta = (middle_slope + back_one).reshape(seqs, rows, model_width)
    (
        part_gain_one,
        part_shift_one,
        part_project,
        part_output,
        part_out_bias,
        part_gain_two,
        part_shift_two,
        part_expand,
        part_shrink,
        part_shrink_bias,
    ) = (
        lax.psum_scatter(
            gain_one_delta.astype(jnp.bfloat16), "fsdp", scatter_dimension=0, tiled=True
        ).astype(jnp.float32),
        lax.psum_scatter(
            shift_one_delta.astype(jnp.bfloat16), "fsdp", scatter_dimension=0, tiled=True
        ).astype(jnp.float32),
        lax.psum_scatter(
            project_weight_delta.astype(jnp.bfloat16), "fsdp", scatter_dimension=0, tiled=True
        ).astype(jnp.float32),
        lax.psum_scatter(
            output_weight_delta.astype(jnp.bfloat16), "fsdp", scatter_dimension=1, tiled=True
        ).astype(jnp.float32),
        lax.psum_scatter(
            output_bias_delta.astype(jnp.bfloat16), "fsdp", scatter_dimension=0, tiled=True
        ).astype(jnp.float32),
        lax.psum_scatter(
            gain_two_delta.astype(jnp.bfloat16), "fsdp", scatter_dimension=0, tiled=True
        ).astype(jnp.float32),
        lax.psum_scatter(
            shift_two_delta.astype(jnp.bfloat16), "fsdp", scatter_dimension=0, tiled=True
        ).astype(jnp.float32),
        lax.psum_scatter(
            expand_weight_delta.astype(jnp.bfloat16), "fsdp", scatter_dimension=0, tiled=True
        ).astype(jnp.float32),
        lax.psum_scatter(
            shrink_weight_delta.astype(jnp.bfloat16), "fsdp", scatter_dimension=1, tiled=True
        ).astype(jnp.float32),
        lax.psum_scatter(
            shrink_bias_delta.astype(jnp.bfloat16), "fsdp", scatter_dimension=0, tiled=True
        ).astype(jnp.float32),
    )
    shares = (
        lax.psum_scatter(
            part_gain_one.astype(jnp.bfloat16), "ctx", scatter_dimension=0, tiled=True
        ).astype(jnp.float32),
        lax.psum_scatter(
            part_shift_one.astype(jnp.bfloat16), "ctx", scatter_dimension=0, tiled=True
        ).astype(jnp.float32),
        lax.psum_scatter(
            part_project.astype(jnp.bfloat16), "ctx", scatter_dimension=0, tiled=True
        ).astype(jnp.float32),
        lax.psum_scatter(
            part_output.astype(jnp.bfloat16), "ctx", scatter_dimension=1, tiled=True
        ).astype(jnp.float32),
        lax.psum_scatter(
            part_out_bias.astype(jnp.bfloat16), "ctx", scatter_dimension=0, tiled=True
        ).astype(jnp.float32),
        lax.psum_scatter(
            part_gain_two.astype(jnp.bfloat16), "ctx", scatter_dimension=0, tiled=True
        ).astype(jnp.float32),
        lax.psum_scatter(
            part_shift_two.astype(jnp.bfloat16), "ctx", scatter_dimension=0, tiled=True
        ).astype(jnp.float32),
        lax.psum_scatter(
            part_expand.astype(jnp.bfloat16), "ctx", scatter_dimension=0, tiled=True
        ).astype(jnp.float32),
        lax.psum_scatter(
            part_shrink.astype(jnp.bfloat16), "ctx", scatter_dimension=1, tiled=True
        ).astype(jnp.float32),
        lax.psum_scatter(
            part_shrink_bias.astype(jnp.bfloat16), "ctx", scatter_dimension=0, tiled=True
        ).astype(jnp.float32),
    )
    bias_sums = lax.psum((project_bias_delta, expand_bias_delta), ("fsdp", "ctx"))
    return (
        layer_output,
        input_delta,
        shares[0],
        shares[1],
        shares[2],
        bias_sums[0],
        shares[3],
        shares[4],
        shares[5],
        shares[6],
        shares[7],
        bias_sums[1],
        shares[8],
        shares[9],
    )


MESH = pl.DeviceIdType.MESH
VMEM_BYTES = 62 * 1024 * 1024


def dot_nn(left, right):
    return lax.dot_general(
        left, right, (((1,), (0,)), ((), ())), preferred_element_type=jnp.float32
    )


def dot_nt(left, right):
    return lax.dot_general(
        left, right, (((1,), (1,)), ((), ())), preferred_element_type=jnp.float32
    )


def remote(source, target, send, receive, device):
    return pltpu.make_async_remote_copy(
        src_ref=source,
        dst_ref=target,
        send_sem=send,
        recv_sem=receive,
        device_id=device,
        device_id_type=MESH,
    )


def aligned(index, size, unit=16):
    return pl.ds(pl.multiple_of(index * size, unit), size)


class Place:
    def __init__(self, line):
        self.line = line
        self.f = lax.axis_index("fsdp")
        self.c = lax.axis_index("ctx")
        self.t = lax.axis_index("tp")
        self.core_bit = lax.rem(self.c, 2)
        self.row_bit = self.c // 2
        self.core = self.c + 1 - 2 * self.core_bit
        self.row = lax.rem(self.c + 2, 4)
        self.core_device = (self.f, self.core, self.t)
        self.row_device = (self.f, self.row, self.t)
        self.tp_device = (self.f, self.c, 1 - self.t)

    def line_device(self, f):
        return (f, self.c, self.t)

    def greet(self, tp, line):
        barrier = pltpu.get_barrier_semaphore()
        count = 2
        pl.semaphore_signal(barrier, 1, device_id=self.core_device, device_id_type=MESH)
        pl.semaphore_signal(barrier, 1, device_id=self.row_device, device_id_type=MESH)
        if tp:
            pl.semaphore_signal(barrier, 1, device_id=self.tp_device, device_id_type=MESH)
            count += 1
        if line:
            for step in range(1, self.line):
                pl.semaphore_signal(
                    barrier,
                    1,
                    device_id=self.line_device(lax.rem(self.f + step, self.line)),
                    device_id_type=MESH,
                )
            count += self.line - 1
        pl.semaphore_wait(barrier, count)


class Scatter:
    def __init__(self, place, group, shard, sems, core=None, row=None, line=None):
        self.place, self.group, self.shard = place, group, shard
        self.core_send, self.core_recv, self.row_send, self.row_recv, self.line_send, self.line_recv = sems
        self.core, self.row, self.line = core, row, line

    def core_copies(self):
        full, landed, _ = self.core
        at = self.place
        copies = []
        for f in range(at.line):
            for y in range(2):
                index = f * 2 + y
                copies.append(
                    remote(
                        full.at[aligned(f * 4 + 2 * y + 1 - at.core_bit, self.shard), :],
                        landed.at[pl.ds(index * self.shard, self.shard), :],
                        self.core_send.at[self.group, index],
                        self.core_recv.at[self.group, index],
                        at.core_device,
                    )
                )
        return copies

    def row_copies(self):
        summed, landed, _ = self.row
        at = self.place
        return [
            remote(
                summed.at[aligned(f * 2 + 1 - at.row_bit, self.shard), :],
                landed.at[pl.ds(f * self.shard, self.shard), :],
                self.row_send.at[self.group, f],
                self.row_recv.at[self.group, f],
                at.row_device,
            )
            for f in range(at.line)
        ]

    def line_copies(self):
        summed, landed, _ = self.line
        at = self.place
        copies = []
        for step in range(1, at.line):
            target = lax.rem(at.f + step, at.line)
            copies.append(
                remote(
                    summed.at[aligned(target, self.shard), :],
                    landed.at[pl.ds((step - 1) * self.shard, self.shard), :],
                    self.line_send.at[self.group, step],
                    self.line_recv.at[self.group, step],
                    at.line_device(target),
                )
            )
        return copies

    def start(self, stage):
        for copy in getattr(self, stage + "_copies")():
            copy.start()

    def core_finish(self):
        full, landed, summed = self.core
        at = self.place
        for index, copy in enumerate(self.core_copies()):
            copy.wait_recv()
            f, y = index // 2, index % 2
            own = full[aligned(f * 4 + 2 * y + at.core_bit, self.shard), :]
            other = landed[index * self.shard : (index + 1) * self.shard, :]
            summed[index * self.shard : (index + 1) * self.shard, :] = (
                own.astype(jnp.float32) + other.astype(jnp.float32)
            ).astype(summed.dtype)

    def row_finish(self):
        summed, landed, result = self.row
        at = self.place
        for f, copy in enumerate(self.row_copies()):
            copy.wait_recv()
            own = summed[aligned(f * 2 + at.row_bit, self.shard), :]
            other = landed[f * self.shard : (f + 1) * self.shard, :]
            result[f * self.shard : (f + 1) * self.shard, :] = (
                own.astype(jnp.float32) + other.astype(jnp.float32)
            ).astype(result.dtype)

    def line_finish(self):
        summed, landed, result = self.line
        at = self.place
        total = summed[aligned(at.f, self.shard), :].astype(jnp.float32)
        for step, copy in enumerate(self.line_copies()):
            copy.wait_recv()
            total = total + landed[step * self.shard : (step + 1) * self.shard, :].astype(jnp.float32)
        result[...] = total

    def drain(self, *stages):
        for stage in stages:
            for copy in getattr(self, stage + "_copies")():
                copy.wait_send()


def gather_kernel(
    line,
    x_ref,
    pv_own,
    wo_own,
    we_own,
    ws_own,
    bias_ref,
    q_ref,
    kv_ref,
    pv_ref,
    wo_ref,
    we_ref,
    ws_ref,
    vec_ref,
    unit,
    normed,
    line_send,
    line_recv,
    row_send,
    row_recv,
    core_send,
    core_recv,
    kv_send,
    kv_recv,
):
    at = Place(line)
    shard = pv_own.shape[0]
    rows, width = q_ref.shape
    half = rows // 2
    groups = (
        (pv_own, pv_ref, True),
        (wo_own, wo_ref, True),
        (we_own, we_ref, False),
        (ws_own, ws_ref, False),
    )

    def block(group, f, ctx):
        return aligned(f * 4 + ctx if groups[group][2] else f, shard)

    def line_copy(group, f, way, own=False):
        mine, full, _ = groups[group]
        part = full.at[block(group, f, at.c), :]
        return remote(
            mine if own else part,
            part,
            line_send.at[group, (way + 1) // 2, f],
            line_recv.at[group, f],
            at.line_device(at.f + way),
        )

    def row_copy(group, f, own=False):
        mine, full, _ = groups[group]
        part = full.at[block(group, f, at.c), :]
        return remote(
            mine if own else part, part, row_send.at[group, f], row_recv.at[group, f], at.row_device
        )

    def core_copy(group, f, other, own=False):
        mine, full, _ = groups[group]
        part = full.at[block(group, f, at.row if other else at.c), :]
        return remote(
            mine if own else part,
            part,
            core_send.at[group, f, other],
            core_recv.at[group, f, other],
            at.core_device,
        )

    def each(step, action):
        if step == 0:
            action(at.f, 0)
            return

        @pl.when(at.f - step >= 0)
        def _():
            action(at.f - step, 1)

        @pl.when(at.f + step < line)
        def _():
            action(at.f + step, -1)

    def can_pass(way):
        return at.f < line - 1 if way > 0 else at.f > 0

    def start(group):
        mine, full, spread = groups[group]
        for way in (1, -1):

            @pl.when(can_pass(way))
            def _(way=way):
                line_copy(group, at.f, way, own=True).start()

        if spread:
            row_copy(group, at.f, own=True).start()
            core_copy(group, at.f, 0, own=True).start()
        full[block(group, at.f, at.c), :] = mine[...]

    def arrive_line(group, f, way):
        line_copy(group, f, 1).wait_recv()

        @pl.when(can_pass(way))
        def _():
            line_copy(group, f, way).start()

        if groups[group][2]:
            row_copy(group, f).start()
            core_copy(group, f, 0).start()

    def arrive_row(group, f):
        row_copy(group, f).wait_recv()
        core_copy(group, f, 1).start()

    def advance(group):
        spread = groups[group][2]
        for step in range(1, line):
            each(step, lambda f, way: arrive_line(group, f, way))
            if spread:
                each(step - 1, lambda f, way: arrive_row(group, f))
        if spread:
            each(line - 1, lambda f, way: arrive_row(group, f))

    def finish(group):
        if groups[group][2]:
            for f in range(line):
                for other in (0, 1):
                    core_copy(group, f, other).wait_recv()

    def drain(group):
        for step in range(line):
            for way in (1, -1):
                source = at.f - step * way

                @pl.when((source >= 0) & (source < line) & can_pass(way))
                def _(source=source, way=way):
                    line_copy(group, source, way).wait_send()

        if groups[group][2]:
            for f in range(line):
                row_copy(group, f).wait_send()
                for other in (0, 1):
                    core_copy(group, f, other).wait_send()

    def kv_row(part):
        here = kv_ref.at[aligned(at.c * 2 + part, half), :]
        return remote(here, here, kv_send.at[0, part], kv_recv.at[0, part], at.row_device)

    def kv_core(part, other):
        here = kv_ref.at[aligned((at.row if other else at.c) * 2 + part, half), :]
        return remote(
            here, here, kv_send.at[1 + other, part], kv_recv.at[1 + other, part], at.core_device
        )

    at.greet(tp=False, line=True)
    start(0)

    @pl.loop(0, 4)
    def _(part):
        these = aligned(part, rows // 4)
        unit[these, :] = normalize_parts(x_ref[these, :].astype(jnp.float32))[0]

    advance(0)
    for group in (1, 2, 3):
        start(group)
    finish(0)
    tile = pv_ref.shape[1] - 3 * width
    vec_ref[...] = pv_ref[:, 3 * width :].astype(jnp.float32).T[0:8, :]
    gain, shift = vec_ref[0:1, :], vec_ref[1:2, :]

    @pl.loop(0, 4)
    def _(part):
        these = aligned(part, rows // 4)
        normed[these, :] = (unit[these, :] * gain + shift).astype(jnp.bfloat16)

    for part in range(2):
        left = normed[part * half : (part + 1) * half, :]
        here = aligned(at.c * 2 + part, half)
        for piece in range(2):
            columns = slice((1 + piece) * width, (2 + piece) * width)
            kv_ref[here, piece * width : (piece + 1) * width] = (
                dot_nn(left, pv_ref[:, columns]) + bias_ref[:, columns]
            ).astype(jnp.bfloat16)
        kv_row(part).start()
        kv_core(part, 0).start()
    for part in range(2):
        these = slice(part * half, (part + 1) * half)
        q_ref[these, :] = (
            dot_nn(normed[these, :], pv_ref[:, 0:width]) + bias_ref[:, 0:width]
        ).astype(jnp.bfloat16)
    advance(1)
    advance(2)
    kv_row(0).wait_recv()
    kv_core(0, 1).start()
    advance(3)
    kv_row(1).wait_recv()
    kv_core(1, 1).start()
    for group in (1, 2, 3):
        finish(group)
    for part in range(2):
        for other in range(2):
            kv_core(part, other).wait_recv()
    for group in range(4):
        drain(group)
    for part in range(2):
        kv_row(part).wait_send()
        for other in range(2):
            kv_core(part, other).wait_send()


def lanes_of(pair_head, shape):
    lane = lax.broadcasted_iota(jnp.int32, shape, 1)
    return (lane // HEAD_DIM) == pair_head


def split_heads(source, store, scale):
    rows, width = source.shape
    for pair in range(width // 128):
        both = source[:, pair * 128 : (pair + 1) * 128].astype(jnp.float32) * scale
        for side in range(2):
            store[2 * pair + side, :, :] = jnp.where(
                lanes_of(side, both.shape), both, 0.0
            ).astype(jnp.bfloat16)


def slot_mask(bias, seg_ref, order_ref, query_slot, key_slot, half):
    query_seg = seg_ref[:, aligned(query_slot, half, 128)].astype(jnp.float32)
    key_seg = seg_ref[:, aligned(key_slot, half, 128)].astype(jnp.float32)
    key_part = jnp.broadcast_to(key_seg, (128, half)).T
    key_full = jnp.concatenate([key_part] * (half // 128), axis=1)
    shape = (half, half)
    key_place = order_ref[0, key_slot] * half + lax.broadcasted_iota(jnp.int32, shape, 0)
    query_place = order_ref[0, query_slot] * half + lax.broadcasted_iota(jnp.int32, shape, 1)
    allowed = (key_full == query_seg) & (key_place <= query_place)
    bias[...] = jnp.where(allowed, 0.0, NEGATIVE)


def slot_needed(last_ref, order_ref, query_slot, key_slot, half):
    query_block, key_block = order_ref[0, query_slot], order_ref[0, key_slot]
    reaches = last_ref[0, key_slot * half + half - 1] >= query_block * half
    return (key_block == query_block) | ((key_block < query_block) & reaches)


def attend_kernel(
    q_ref, kv_ref, seg_ref, last_ref, order_ref, out_ref, mixed_ref, lse_ref, heads, bias, top, total
):
    rows, width = q_ref.shape
    half = rows // 2
    slots = kv_ref.shape[0] // half
    first = lax.axis_index("ctx") * 2
    split_heads(q_ref, heads, SCALE)
    top[...] = jnp.full_like(top, NEGATIVE)
    total[...] = jnp.zeros_like(total)
    mixed_ref[...] = jnp.zeros_like(mixed_ref)
    for part in range(2):
        these = slice(part * half, (part + 1) * half)

        @pl.loop(0, slots)
        def _(slot, part=part, these=these):
            @pl.when(slot_needed(last_ref, order_ref, first + part, slot, half))
            def _():
                slot_mask(bias, seg_ref, order_ref, first + part, slot, half)
                keys = aligned(slot, half)
                for head in range(width // HEAD_DIM):
                    pair, side = head // 2, head % 2
                    scores = (
                        dot_nt(kv_ref[keys, pair * 128 : (pair + 1) * 128], heads[head, these, :])
                        + bias[...]
                    )
                    before = top[head : head + 1, these]
                    after = jnp.maximum(before, jnp.max(scores, axis=0, keepdims=True))
                    raised = jnp.exp(scores - after)
                    fade = jnp.exp(before - after)
                    top[head : head + 1, these] = after
                    total[head : head + 1, these] = total[head : head + 1, these] * fade + jnp.sum(
                        raised, axis=0, keepdims=True
                    )
                    value = kv_ref[keys, width + pair * 128 : width + (pair + 1) * 128].T
                    spot = slice(head * HEAD_DIM, (head + 1) * HEAD_DIM)
                    mixed_ref[spot, these] = mixed_ref[spot, these] * fade + dot_nn(
                        value[side * HEAD_DIM : (side + 1) * HEAD_DIM, :],
                        raised.astype(jnp.bfloat16),
                    )

    for head in range(width // HEAD_DIM):
        spot = slice(head * HEAD_DIM, (head + 1) * HEAD_DIM)
        mixed_ref[spot, :] = mixed_ref[spot, :] / total[head : head + 1, :]
    for pair in range(width // 128):
        span = slice(pair * 128, (pair + 1) * 128)
        out_ref[:, span] = mixed_ref[span, :].T.astype(jnp.bfloat16)
    lse_ref[...] = top[...] + jnp.log(total[...])


def attend_back_kernel(
    q_ref,
    kv_ref,
    slope_ref,
    mixed_ref,
    lse_ref,
    seg_ref,
    last_ref,
    order_ref,
    dq_ref,
    dkv_ref,
    heads,
    slopes,
    bias,
    delta,
    dq_sum,
    dkv_sum,
):
    rows, width = q_ref.shape
    half = rows // 2
    slots = kv_ref.shape[0] // half
    first = lax.axis_index("ctx") * 2
    split_heads(q_ref, heads, SCALE)
    split_heads(slope_ref, slopes, 1.0)
    dq_sum[...] = jnp.zeros_like(dq_sum)
    for pair in range(width // 128):
        span = slice(pair * 128, (pair + 1) * 128)
        product = slope_ref[:, span].astype(jnp.float32).T * mixed_ref[span, :]
        for side in range(2):
            head = 2 * pair + side
            delta[head : head + 1, :] = jnp.sum(
                product[side * HEAD_DIM : (side + 1) * HEAD_DIM, :], axis=0, keepdims=True
            )

    @pl.loop(0, slots)
    def _(slot):
        keys = aligned(slot, half)
        dkv_sum[...] = jnp.zeros_like(dkv_sum)
        for part in range(2):
            these = slice(part * half, (part + 1) * half)

            @pl.when(slot_needed(last_ref, order_ref, first + part, slot, half))
            def _(part=part, these=these):
                slot_mask(bias, seg_ref, order_ref, first + part, slot, half)
                for pair in range(width // 128):
                    span = slice(pair * 128, (pair + 1) * 128)
                    value_span = slice(width + pair * 128, width + (pair + 1) * 128)
                    key = kv_ref[keys, span]
                    value = kv_ref[keys, value_span]
                    key_turned = key.T
                    for side in range(2):
                        head = 2 * pair + side
                        scores = dot_nt(key, heads[head, these, :]) + bias[...]
                        chance = jnp.exp(scores - lse_ref[head : head + 1, these])
                        pulled = dot_nt(value, slopes[head, these, :])
                        slope = (chance * (pulled - delta[head : head + 1, these])).astype(
                            jnp.bfloat16
                        )
                        dkv_sum[:, value_span] += dot_nn(
                            chance.astype(jnp.bfloat16), slopes[head, these, :]
                        )
                        dkv_sum[:, span] += dot_nn(slope, heads[head, these, :])
                        spot = slice(head * HEAD_DIM, (head + 1) * HEAD_DIM)
                        dq_sum[spot, these] += dot_nn(
                            key_turned[side * HEAD_DIM : (side + 1) * HEAD_DIM, :], slope
                        )

        dkv_ref[keys, :] = dkv_sum[...].astype(jnp.bfloat16)

    for pair in range(width // 128):
        span = slice(pair * 128, (pair + 1) * 128)
        dq_ref[:, span] = (dq_sum[span, :] * SCALE).T.astype(jnp.bfloat16)


def gelu_both(v):
    square = v * v
    inner = GELU_A * v * (1.0 + GELU_B * square)
    bent = jnp.tanh(inner)
    lifted = 0.5 * (1.0 + bent)
    slope = lifted + 0.5 * v * (1.0 - bent * bent) * (GELU_A * (1.0 + 3.0 * GELU_B * square))
    return (v * lifted, slope)


def middle_kernel(
    line,
    att_ref,
    x_ref,
    ct_ref,
    wo_ref,
    we_part,
    ws_part,
    vec_ref,
    bias_ref,
    mid_ref,
    mids_ref,
    att_slope_ref,
    feed_ref,
    shrink_ref,
    expand_ref,
    go_ref,
    vsum_ref,
    bsum_ref,
    we,
    ws,
    out_send,
    out_land,
    up_send,
    up_land,
    normed,
    active,
    before_slope,
    turned,
    gs,
    ge,
    gs_land,
    ge_land,
    gs_sum,
    gs_land2,
    row_send,
    row_recv,
    core_send,
    core_recv,
    tp_send,
    tp_recv,
    *sems,
):
    at = Place(line)
    shard = we_part.shape[0] // line
    rows, model = x_ref.shape
    hidden = we.shape[1]
    pieces = 4
    some = rows // pieces
    groups = ((we_part, we), (ws_part, ws))

    def row_copy(group, f):
        part, full = groups[group]
        return remote(
            part.at[pl.ds(f * shard, shard), :],
            full.at[aligned(f * 4 + at.c, shard), :],
            row_send.at[group, f],
            row_recv.at[group, f],
            at.row_device,
        )

    def core_copy(group, f, other):
        part, full = groups[group]
        there = full.at[aligned(f * 4 + (at.row if other else at.c), shard), :]
        return remote(
            there if other else part.at[pl.ds(f * shard, shard), :],
            there,
            core_send.at[group, f, other],
            core_recv.at[group, f, other],
            at.core_device,
        )

    def tp_copy(kind, piece):
        source, target = ((out_send, out_land), (up_send, up_land))[kind]
        these = aligned(piece, some)
        return remote(
            source.at[these, :],
            target.at[these, :],
            tp_send.at[kind, piece],
            tp_recv.at[kind, piece],
            at.tp_device,
        )

    shrink = Scatter(
        at, 0, shard, sems, core=(gs, gs_land, gs_sum), row=(gs_sum, gs_land2, shrink_ref)
    )
    expand = Scatter(at, 1, shard, sems, core=(ge, ge_land, expand_ref))

    at.greet(tp=True, line=False)
    for group in range(2):
        for f in range(line):
            row_copy(group, f).start()
    for group in range(2):
        part, full = groups[group]
        for f in range(line):
            core_copy(group, f, 0).start()
            full[aligned(f * 4 + at.c, shard), :] = part[f * shard : (f + 1) * shard, :]

    @pl.loop(0, pieces)
    def _(piece):
        these = aligned(piece, some)
        out_send[these, :] = dot_nt(att_ref[these, :], wo_ref[...]).astype(jnp.bfloat16)
        tp_copy(0, piece).start()

    for group in range(2):
        for f in range(line):
            row_copy(group, f).wait_recv()
            core_copy(group, f, 1).start()
    for group in range(2):
        for f in range(line):
            for other in range(2):
                core_copy(group, f, other).wait_recv()
    out_bias, gain, shift = vec_ref[2:3, :], vec_ref[3:4, :], vec_ref[4:5, :]

    @pl.loop(0, pieces)
    def _(piece):
        these = aligned(piece, some)
        tp_copy(0, piece).wait_recv()
        branch = out_send[these, :].astype(jnp.float32) + out_land[these, :].astype(jnp.float32)
        middle = x_ref[these, :].astype(jnp.float32) + branch + out_bias
        mid_ref[these, :] = middle
        unit, _ = normalize_parts(middle)
        low = (unit * gain + shift).astype(jnp.bfloat16)
        normed[these, :] = low
        for column in range(0, hidden, 512):
            span = slice(column, column + 512)
            value, slope = gelu_both(dot_nn(low, we[:, span]) + bias_ref[:, span])
            active[these, span] = value.astype(jnp.bfloat16)
            before_slope[these, span] = (dot_nn(ct_ref[these, :], ws[:, span]) * slope).astype(
                jnp.bfloat16
            )
        up_send[these, :] = dot_nt(before_slope[these, :], we[...]).astype(jnp.bfloat16)
        tp_copy(1, piece).start()

    turned[...] = ct_ref[...].T
    for column in range(0, hidden, 512):
        span = slice(column, column + 512)
        gs[:, span] = dot_nn(turned[...], active[:, span]).astype(jnp.bfloat16)
    shrink.start("core")
    turned[...] = normed[...].T
    for column in range(0, hidden, 512):
        span = slice(column, column + 512)
        ge[:, span] = dot_nn(turned[...], before_slope[:, span]).astype(jnp.bfloat16)
    expand.start("core")
    shrink.core_finish()
    shrink.start("row")

    @pl.loop(0, pieces)
    def _(piece):
        these = aligned(piece, some)
        feed_ref[these, :] = dot_nt(active[these, :], ws[...]).astype(jnp.bfloat16)

    bsum_ref[...] = jnp.sum(before_slope[...].astype(jnp.float32), axis=0, keepdims=True)
    expand.core_finish()
    vsum_ref[...] = jnp.zeros_like(vsum_ref)

    @pl.loop(0, pieces)
    def _(piece):
        these = aligned(piece, some)
        tp_copy(1, piece).wait_recv()
        upstream = up_send[these, :].astype(jnp.float32) + up_land[these, :].astype(jnp.float32)
        unit, inverse = normalize_parts(mid_ref[these, :])
        back, gain_delta, shift_delta = norm_backward(upstream, unit, inverse, gain)
        slope = ct_ref[these, :].astype(jnp.float32)
        middle_slope = slope + back
        mids_ref[these, :] = middle_slope
        vsum_ref[2:3, :] += jnp.sum(middle_slope, axis=0, keepdims=True)
        vsum_ref[3:4, :] += gain_delta[None]
        vsum_ref[4:5, :] += shift_delta[None]
        vsum_ref[5:6, :] += jnp.sum(slope, axis=0, keepdims=True)
        low = middle_slope.astype(jnp.bfloat16)
        normed[these, :] = low
        att_slope_ref[these, :] = dot_nn(low, wo_ref[...]).astype(jnp.bfloat16)

    turned[...] = normed[...].T
    go_ref[...] = dot_nn(turned[...], att_ref[...]).astype(jnp.bfloat16)
    shrink.row_finish()
    for group in range(2):
        for f in range(line):
            row_copy(group, f).wait_send()
            for other in range(2):
                core_copy(group, f, other).wait_send()
    for kind in range(2):
        for piece in range(pieces):
            tp_copy(kind, piece).wait_send()
    shrink.drain("core", "row")
    expand.drain("core")


def last_kernel(
    line,
    dq_ref,
    dkv_ref,
    x_ref,
    pv_ref,
    mids_ref,
    mid_ref,
    feed_ref,
    ts_ref,
    se_ref,
    go_ref,
    vec_ref,
    vsum_ref,
    bsum_ref,
    out_ref,
    delta_ref,
    gs_out,
    ge_out,
    go_out,
    gp_out,
    gv_out,
    bias_out,
    kv_land,
    kv_pass,
    kv_land2,
    kv_low,
    back,
    down_send,
    down_land,
    feed_land,
    normed,
    turned,
    vec_sum,
    te,
    te_land,
    go_land,
    go_sum,
    go_land2,
    to,
    gp,
    gp_land,
    gp_sum,
    gp_land2,
    tp_part,
    gv,
    gv_land,
    gv_sum,
    gv_land2,
    tv,
    zs,
    ze,
    zo,
    zp,
    zv,
    bias_pack,
    bias_land,
    bias_line,
    kv_send,
    kv_recv,
    tp_send,
    tp_recv,
    bias_send,
    bias_recv,
    *sems,
):
    at = Place(line)
    rows, width = dq_ref.shape
    half = rows // 2
    shard = ts_ref.shape[0] // line
    pieces = 4
    some = rows // pieces
    hidden = ts_ref.shape[1]

    shrink = Scatter(at, 0, shard, sems, line=(ts_ref, zs, gs_out))
    expand = Scatter(at, 1, shard, sems, row=(se_ref, te_land, te), line=(te, ze, ge_out))
    output = Scatter(
        at,
        2,
        shard,
        sems,
        core=(go_ref, go_land, go_sum),
        row=(go_sum, go_land2, to),
        line=(to, zo, go_out),
    )
    project = Scatter(
        at,
        3,
        shard,
        sems,
        core=(gp, gp_land, gp_sum),
        row=(gp_sum, gp_land2, tp_part),
        line=(tp_part, zp, gp_out),
    )
    vector = Scatter(
        at,
        4,
        shard,
        sems,
        core=(gv, gv_land, gv_sum),
        row=(gv_sum, gv_land2, tv),
        line=(tv, zv, gv_out),
    )

    def kv_core(y, part):
        return remote(
            dkv_ref.at[aligned((2 * y + 1 - at.core_bit) * 2 + part, half), :],
            kv_land.at[aligned(y * 2 + part, half), :],
            kv_send.at[0, y, part],
            kv_recv.at[0, y, part],
            at.core_device,
        )

    def kv_row(part):
        return remote(
            kv_pass.at[pl.ds(part * half, half), :],
            kv_land2.at[pl.ds(part * half, half), :],
            kv_send.at[1, 0, part],
            kv_recv.at[1, 0, part],
            at.row_device,
        )

    def tp_copy(kind, piece):
        source, target = ((feed_ref, feed_land), (down_send, down_land))[kind]
        these = aligned(piece, some)
        return remote(
            source.at[these, :],
            target.at[these, :],
            tp_send.at[kind, piece],
            tp_recv.at[kind, piece],
            at.tp_device,
        )

    at.greet(tp=True, line=True)
    far, near = 1 - at.row_bit, at.row_bit
    for y in (far, near):
        for part in range(2):
            kv_core(y, part).start()
    for piece in range(pieces):
        tp_copy(0, piece).start()
    shrink.start("line")
    output.start("core")
    for part in range(2):
        kv_core(far, part).wait_recv()
        mine = dkv_ref[aligned((2 * far + at.core_bit) * 2 + part, half), :].astype(jnp.float32)
        landed = kv_land[aligned(far * 2 + part, half), :].astype(jnp.float32)
        kv_pass[part * half : (part + 1) * half, :] = (mine + landed).astype(jnp.bfloat16)
        kv_row(part).start()
    expand.start("row")
    output.core_finish()
    output.start("row")
    gain, shift = vec_ref[0:1, :], vec_ref[1:2, :]

    @pl.loop(0, pieces)
    def _(piece):
        these = aligned(piece, some)
        unit, _ = normalize_parts(x_ref[these, :].astype(jnp.float32))
        normed[these, :] = (unit * gain + shift).astype(jnp.bfloat16)
        back[these, :] = dot_nt(dq_ref[these, :], pv_ref[:, 0:width])

    turned[...] = normed[...].T
    gp[:, 0:width] = dot_nn(turned[...], dq_ref[...]).astype(jnp.bfloat16)
    shrink_bias = vec_ref[5:6, :]

    @pl.loop(0, pieces)
    def _(piece):
        these = aligned(piece, some)
        tp_copy(0, piece).wait_recv()
        feed = (
            feed_ref[these, :].astype(jnp.float32) + feed_land[these, :].astype(jnp.float32)
        ).astype(jnp.bfloat16)
        out_ref[these, :] = (mid_ref[these, :] + feed.astype(jnp.float32) + shrink_bias).astype(
            jnp.bfloat16
        )

    for part in range(2):
        kv_core(near, part).wait_recv()
        kv_row(part).wait_recv()
        these = slice(part * half, (part + 1) * half)
        total = dkv_ref[aligned(at.c * 2 + part, half), :].astype(jnp.float32)
        total = total + kv_land[aligned(near * 2 + part, half), :].astype(jnp.float32)
        total = total + kv_land2[these, :].astype(jnp.float32)
        kv_low[these, :] = total.astype(jnp.bfloat16)
        for step in range(pieces // 2):
            piece = part * (pieces // 2) + step
            these = slice(piece * some, (piece + 1) * some)
            down_send[these, :] = (
                back[these, :] + dot_nt(kv_low[these, :], pv_ref[:, width : 3 * width])
            ).astype(jnp.bfloat16)
            tp_copy(1, piece).start()
    for piece in range(2):
        span = slice((1 + piece) * width, (2 + piece) * width)
        gp[:, span] = dot_nn(
            turned[...], kv_low[:, piece * width : (piece + 1) * width]
        ).astype(jnp.bfloat16)
    project.start("core")
    bias_row = jnp.concatenate(
        [
            bsum_ref[...],
            jnp.sum(dq_ref[...].astype(jnp.float32), axis=0, keepdims=True),
            jnp.sum(kv_low[:, width:].astype(jnp.float32), axis=0, keepdims=True),
        ],
        axis=1,
    )
    bias_pack[...] = jnp.zeros_like(bias_pack)
    for index in range(bias_row.shape[1] // 128):
        bias_pack[0, index : index + 1, :] = bias_row[:, index * 128 : (index + 1) * 128]

    def bias_copy(stage):
        device = (at.core_device, at.row_device)[stage]
        return remote(
            bias_pack.at[stage],
            bias_land.at[stage],
            bias_send.at[0, stage],
            bias_recv.at[0, stage],
            device,
        )

    def bias_line_copy(step):
        target = lax.rem(at.f + step, line)
        return remote(
            bias_pack.at[2],
            bias_line.at[at.f],
            bias_send.at[1, step],
            bias_recv.at[1, step],
            at.line_device(target),
        )

    bias_copy(0).start()
    expand.row_finish()
    expand.start("line")
    output.row_finish()
    output.start("line")
    project.core_finish()
    project.start("row")
    bias_copy(0).wait_recv()
    bias_pack[1, :, :] = bias_pack[0, :, :] + bias_land[0, :, :]
    bias_copy(1).start()
    shrink.line_finish()
    bias_copy(1).wait_recv()
    bias_pack[2, :, :] = bias_pack[1, :, :] + bias_land[1, :, :]
    for step in range(1, line):
        bias_line_copy(step).start()
    vec_sum[...] = jnp.zeros_like(vec_sum)
    vec_sum[0:8, :] = vsum_ref[...]

    @pl.loop(0, pieces)
    def _(piece):
        these = aligned(piece, some)
        tp_copy(1, piece).wait_recv()
        upstream = down_send[these, :].astype(jnp.float32) + down_land[these, :].astype(jnp.float32)
        unit, inverse = normalize_parts(x_ref[these, :].astype(jnp.float32))
        slope, gain_delta, shift_delta = norm_backward(upstream, unit, inverse, gain)
        delta_ref[these, :] = mids_ref[these, :] + slope
        vec_sum[0:1, :] += gain_delta[None]
        vec_sum[1:2, :] += shift_delta[None]

    gv[...] = vec_sum[...].T.astype(jnp.bfloat16)
    vector.start("core")
    project.row_finish()
    project.start("line")
    vector.core_finish()
    vector.start("row")
    expand.line_finish()
    output.line_finish()
    vector.row_finish()
    vector.start("line")
    for step in range(1, line):
        source = lax.rem(at.f + line - step, line)
        remote(
            bias_pack.at[2],
            bias_line.at[source],
            bias_send.at[1, step],
            bias_recv.at[1, step],
            at.row_device,
        ).wait_recv()
    bias_line[at.f, :, :] = bias_pack[2, :, :]
    total = bias_line[0, :, :]
    for f in range(1, line):
        total = total + bias_line[f, :, :]
    bias_out[...] = total
    project.line_finish()
    vector.line_finish()
    for y in range(2):
        for part in range(2):
            kv_core(y, part).wait_send()
    for part in range(2):
        kv_row(part).wait_send()
    for kind in range(2):
        for piece in range(pieces):
            tp_copy(kind, piece).wait_send()
    for stage in range(2):
        bias_copy(stage).wait_send()
    for step in range(1, line):
        bias_line_copy(step).wait_send()
    shrink.drain("line")
    expand.drain("row", "line")
    output.drain("core", "row", "line")
    project.drain("core", "row", "line")
    vector.drain("core", "row", "line")


def whole(count, space=None):
    return [pl.BlockSpec(memory_space=space or pltpu.VMEM)] * count


def call(kernel, outs, scratch, args, spaces=None, identity=None):
    params = dict(vmem_limit_bytes=VMEM_BYTES)
    if identity is not None:
        params.update(collective_id=identity, has_side_effects=True)
    return pl.pallas_call(
        kernel,
        out_shape=[jax.ShapeDtypeStruct(shape, dtype) for shape, dtype in outs],
        in_specs=spaces or whole(len(args)),
        out_specs=whole(len(outs)),
        scratch_shapes=scratch,
        compiler_params=pltpu.CompilerParams(**params),
    )(*args)


def buffers(*shapes):
    return [pltpu.VMEM(shape, dtype) for shape, dtype in shapes]


def dma(*shape):
    return pltpu.SemaphoreType.DMA(shape)


def scatter_sems(count, line):
    return [dma(count, n) for n in (2 * line, 2 * line, line, line, line, line)]


def by_kernels(
    layer_input,
    cotangent,
    segments,
    slot_order,
    first_gain,
    first_shift,
    project_weight,
    project_bias,
    output_weight,
    output_bias,
    second_gain,
    second_shift,
    expand_weight,
    expand_bias,
    shrink_weight,
    shrink_bias,
):
    low, full = jnp.bfloat16, jnp.float32
    line = lax.axis_size("fsdp")
    _, rows, model = layer_input.shape
    length = segments.shape[1]
    slots = slot_order.shape[1]
    shard, _, width = project_weight.shape
    hidden = expand_weight.shape[1]
    count = width // HEAD_DIM
    half = rows // 2
    x = layer_input.reshape(rows, model)
    ct = cotangent.reshape(rows, model)
    vectors = jnp.stack(
        [first_gain, first_shift, output_bias, second_gain, second_shift, shrink_bias], axis=1
    )
    pv_own = jnp.concatenate(
        [project_weight.reshape(shard, 3 * width), jnp.pad(vectors, ((0, 0), (0, 122)))], axis=1
    )
    zero = jnp.zeros((width,), full)
    qkv_bias = jnp.concatenate(
        [project_bias[0].astype(full), zero, project_bias[1].astype(full)]
    ).reshape(1, 3 * width)
    packed = pv_own.shape[1]
    q, kv, pv, wo, we_part, ws_part, vec = call(
        partial(gather_kernel, line),
        [
            ((rows, width), low),
            ((length, 2 * width), low),
            ((model, packed), low),
            ((model, width), low),
            ((line * shard, hidden), low),
            ((line * shard, hidden), low),
            ((8, model), full),
        ],
        buffers(((rows, model), full), ((rows, model), low))
        + [
            dma(4, 2, line),
            dma(4, line),
            dma(2, line),
            dma(2, line),
            dma(2, line, 2),
            dma(2, line, 2),
            dma(3, 2),
            dma(3, 2),
        ],
        (x, pv_own, output_weight.T, expand_weight, shrink_weight.T, qkv_bias),
        identity=0,
    )
    tables = (segments, segments, slot_order)
    table_spaces = whole(1) + whole(2, pltpu.SMEM)
    att, mixed, lse = call(
        attend_kernel,
        [((rows, width), low), ((width, rows), full), ((8, rows), full)],
        buffers(
            ((count, rows, 128), low), ((half, half), full), ((8, rows), full), ((8, rows), full)
        ),
        (q, kv, *tables),
        spaces=whole(2) + table_spaces,
    )
    mid, mids, att_slope, feed, ts, se, go, vsum, bsum = call(
        partial(middle_kernel, line),
        [
            ((rows, model), full),
            ((rows, model), full),
            ((rows, width), low),
            ((rows, model), low),
            ((line * shard, hidden), low),
            ((2 * line * shard, hidden), low),
            ((model, width), low),
            ((8, model), full),
            ((1, hidden), full),
        ],
        buffers(
            ((model, hidden), low),
            ((model, hidden), low),
            ((rows, model), low),
            ((rows, model), low),
            ((rows, model), low),
            ((rows, model), low),
            ((rows, model), low),
            ((rows, hidden), low),
            ((rows, hidden), low),
            ((model, rows), low),
            ((model, hidden), low),
            ((model, hidden), low),
            ((2 * line * shard, hidden), low),
            ((2 * line * shard, hidden), low),
            ((2 * line * shard, hidden), low),
            ((line * shard, hidden), low),
        )
        + [
            dma(2, line),
            dma(2, line),
            dma(2, line, 2),
            dma(2, line, 2),
            dma(2, 4),
            dma(2, 4),
        ]
        + scatter_sems(2, line),
        (att, x, ct, wo, we_part, ws_part, vec, expand_bias.astype(full).reshape(1, hidden)),
        identity=1,
    )
    dq, dkv = call(
        attend_back_kernel,
        [((rows, width), low), ((length, 2 * width), low)],
        buffers(
            ((count, rows, 128), low),
            ((count, rows, 128), low),
            ((half, half), full),
            ((8, rows), full),
            ((width, rows), full),
            ((half, 2 * width), full),
        ),
        (q, kv, att_slope, mixed, lse, *tables),
        spaces=whole(5) + table_spaces,
    )
    two, one = 2 * line * shard, line * shard
    less = one - shard
    bias_rows = -(-(hidden + 2 * width) // 1024) * 8

    def stages(columns, *kinds):
        size = {"full": model, "two": two, "one": one, "less": less}
        return [((size[kind], columns), low) for kind in kinds]

    out, delta, gs, ge, go, gp, gv, biases = call(
        partial(last_kernel, line),
        [
            ((rows, model), low),
            ((rows, model), full),
            ((shard, hidden), full),
            ((shard, hidden), full),
            ((shard, width), full),
            ((shard, 3 * width), full),
            ((shard, 128), full),
            ((bias_rows, 128), full),
        ],
        buffers(
            ((2 * rows, 2 * width), low),
            ((rows, 2 * width), low),
            ((rows, 2 * width), low),
            ((rows, 2 * width), low),
            ((rows, model), full),
            ((rows, model), low),
            ((rows, model), low),
            ((rows, model), low),
            ((rows, model), low),
            ((model, rows), low),
            ((128, model), full),
            *stages(hidden, "one", "one"),
            *stages(width, "two", "two", "one", "one"),
            *stages(3 * width, "full", "two", "two", "one", "one"),
            *stages(128, "full", "two", "two", "one", "one"),
            *stages(hidden, "less", "less"),
            *stages(width, "less"),
            *stages(3 * width, "less"),
            *stages(128, "less"),
            ((3, bias_rows, 128), full),
            ((2, bias_rows, 128), full),
            ((line, bias_rows, 128), full),
        )
        + [dma(2, 2, 2), dma(2, 2, 2), dma(2, 4), dma(2, 4), dma(2, line), dma(2, line)]
        + scatter_sems(5, line),
        (dq, dkv, x, pv, mids, mid, feed, ts, se, go, vec, vsum, bsum),
        identity=2,
    )
    biases = biases.reshape(-1)
    return (
        out.reshape(layer_input.shape),
        delta.reshape(layer_input.shape),
        gv[:, 0],
        gv[:, 1],
        gp.reshape(shard, 3, width),
        biases[hidden : hidden + 2 * width].reshape(2, width),
        go.T,
        gv[:, 2],
        gv[:, 3],
        gv[:, 4],
        ge,
        biases[:hidden],
        gs.T,
        gv[:, 5],
    )


def solution(mesh):
    n_ctx, n_tp = mesh.shape["ctx"], mesh.shape["tp"]

    def choose(layer_input, *others):
        seqs, rows, model = layer_input.shape
        whole_tiles = model % (16 * n_ctx * mesh.shape["fsdp"]) == 0 and rows % 256 == 0
        if seqs == 1 and n_ctx == 4 and n_tp == 2 and whole_tiles:
            return by_kernels(layer_input, *others)
        return on_device(layer_input, *others)

    return jax.shard_map(
        choose,
        mesh=mesh,
        in_specs=(
            P("fsdp", "ctx", None),
            P("fsdp", "ctx", None),
            P("fsdp", None),
            P("fsdp", None),
            P(("fsdp", "ctx")),
            P(("fsdp", "ctx")),
            P(("fsdp", "ctx"), None, "tp"),
            P(None, "tp"),
            P("tp", ("fsdp", "ctx")),
            P(("fsdp", "ctx")),
            P(("fsdp", "ctx")),
            P(("fsdp", "ctx")),
            P(("fsdp", "ctx"), "tp"),
            P("tp"),
            P("tp", ("fsdp", "ctx")),
            P(("fsdp", "ctx")),
        ),
        out_specs=(
            P("fsdp", "ctx", None),
            P("fsdp", "ctx", None),
            P(("fsdp", "ctx")),
            P(("fsdp", "ctx")),
            P(("fsdp", "ctx"), None, "tp"),
            P(None, "tp"),
            P("tp", ("fsdp", "ctx")),
            P(("fsdp", "ctx")),
            P(("fsdp", "ctx")),
            P(("fsdp", "ctx")),
            P(("fsdp", "ctx"), "tp"),
            P("tp"),
            P("tp", ("fsdp", "ctx")),
            P(("fsdp", "ctx")),
        ),
        check_vma=False,
    )
```

```python
from functools import partial

import jax
import jax.numpy as jnp
from jax import lax
from jax.experimental import pallas as pl
from jax.experimental.pallas import tpu as pltpu
from jax.sharding import PartitionSpec as P

HEAD_DIM = 64


EPSILON = 1e-05
SCALE = 0.125
NEGATIVE = -1000000000.0
TILE = 512
GELU_A = 0.7978845608028654
GELU_B = 0.044715


def contract_rows(left, right):
    return lax.dot_general(
        left, right, (((0,), (0,)), ((), ())), preferred_element_type=jnp.float32
    )


def times_transpose(left, right):
    return lax.dot_general(
        left, right, (((1,), (1,)), ((), ())), preferred_element_type=jnp.float32
    )


def normalize_parts(rows):
    mean = jnp.mean(rows, axis=-1, keepdims=True)
    centred = rows - mean
    spread = jnp.mean(centred * centred, axis=-1, keepdims=True)
    inverse = lax.rsqrt(spread + EPSILON)
    return (centred * inverse, inverse)


def norm_backward(upstream, unit, inverse, gain):
    scaled = upstream * gain
    back = inverse * (
        scaled
        - jnp.mean(scaled, axis=-1, keepdims=True)
        - unit * jnp.mean(scaled * unit, axis=-1, keepdims=True)
    )
    return (back, jnp.sum(upstream * unit, axis=0), jnp.sum(upstream, axis=0))


def split_pairs(array, pairs):
    seqs, count, width = array.shape
    span = width // pairs
    return (
        array.reshape(seqs, count, pairs, span)
        .transpose(0, 2, 1, 3)
        .reshape(seqs * pairs, count, span)
    )


def join_pairs(array, seqs):
    items, count, span = array.shape
    pairs = items // seqs
    return (
        array.reshape(seqs, pairs, count, span)
        .transpose(0, 2, 1, 3)
        .reshape(seqs, count, pairs * span)
    )


def masked_scores(query_heads, key_heads, query_place, query_group, key_place, key_group):
    scores = (
        jnp.einsum("qhd,khd->hqk", query_heads, key_heads, preferred_element_type=jnp.float32)
        * SCALE
    )
    allowed = (query_group[:, None] == key_group[None, :]) & (
        key_place[None, :] <= query_place[:, None]
    )
    return jnp.where(allowed[None], scores, NEGATIVE)


def attend_forward(
    queries, keys_all, values_all, query_places, query_groups, key_places, key_groups, pairs
):
    seqs, rows, width = queries.shape
    length = keys_all.shape[1]
    span = width // pairs
    tile = min(TILE, rows)

    def one_item(item):
        query_part, key_part, value_part, index = item
        which = index // pairs
        query_place = lax.dynamic_index_in_dim(query_places, which, 0, keepdims=False)
        query_group = lax.dynamic_index_in_dim(query_groups, which, 0, keepdims=False)
        key_place = lax.dynamic_index_in_dim(key_places, which, 0, keepdims=False)
        key_group = lax.dynamic_index_in_dim(key_groups, which, 0, keepdims=False)
        key_heads = key_part.reshape(length, 2, span // 2)
        value_heads = value_part.reshape(length, 2, span // 2)
        results, tops, totals = ([], [], [])
        query_heads = query_part.reshape(tile, 2, span // 2)
        scores = masked_scores(
            query_heads, key_heads, query_place, query_group, key_place, key_group
        )
        top = jnp.max(scores, axis=-1)
        raised = jnp.exp(scores - top[..., None])
        total = jnp.sum(raised, axis=-1)
        chance = (raised / total[..., None]).astype(jnp.bfloat16)
        mixed = jnp.einsum("hqk,khd->qhd", chance, value_heads, preferred_element_type=jnp.float32)
        results.append(mixed.reshape(tile, span).astype(jnp.bfloat16))
        tops.append(top)
        totals.append(total)
        return (
            jnp.concatenate(results, axis=0),
            jnp.concatenate(tops, axis=1),
            jnp.concatenate(totals, axis=1),
        )

    items = (
        split_pairs(queries, pairs),
        split_pairs(keys_all, pairs),
        split_pairs(values_all, pairs),
        jnp.arange(seqs * pairs, dtype=jnp.int32),
    )
    mixed, tops, totals = lax.map(one_item, items)
    return (join_pairs(mixed, seqs), tops, totals)


def attend_backward(
    queries,
    keys_all,
    values_all,
    attended_slope,
    tops,
    totals,
    query_places,
    query_groups,
    key_places,
    key_groups,
    pairs,
):
    seqs, rows, width = queries.shape
    length = keys_all.shape[1]
    span = width // pairs
    tile = min(TILE, rows)

    def one_item(item):
        query_part, key_part, value_part, slope_part, top, total, index = item
        which = index // pairs
        query_place = lax.dynamic_index_in_dim(query_places, which, 0, keepdims=False)
        query_group = lax.dynamic_index_in_dim(query_groups, which, 0, keepdims=False)
        key_place = lax.dynamic_index_in_dim(key_places, which, 0, keepdims=False)
        key_group = lax.dynamic_index_in_dim(key_groups, which, 0, keepdims=False)
        key_heads = key_part.reshape(length, 2, span // 2)
        value_heads = value_part.reshape(length, 2, span // 2)
        key_total = jnp.zeros((length, 2, span // 2), jnp.float32)
        value_total = jnp.zeros((length, 2, span // 2), jnp.float32)
        query_heads = query_part.reshape(tile, 2, span // 2)
        slope_heads = slope_part.reshape(tile, 2, span // 2)
        scores = masked_scores(
            query_heads, key_heads, query_place, query_group, key_place, key_group
        )
        chance = jnp.exp(scores - top[:, 0:tile, None]) / total[:, 0:tile, None]
        chance_low = chance.astype(jnp.bfloat16)
        value_total = value_total + jnp.einsum(
            "hqk,qhd->khd", chance_low, slope_heads, preferred_element_type=jnp.float32
        )
        pulled = jnp.einsum(
            "qhd,khd->hqk", slope_heads, value_heads, preferred_element_type=jnp.float32
        )
        score_slope = (chance * (pulled - jnp.sum(chance * pulled, axis=-1, keepdims=True))).astype(
            jnp.bfloat16
        )
        query_step = (
            jnp.einsum("hqk,khd->qhd", score_slope, key_heads, preferred_element_type=jnp.float32)
            * SCALE
        )
        query_results = [query_step.reshape(tile, span).astype(jnp.bfloat16)]
        key_total = (
            key_total
            + jnp.einsum(
                "hqk,qhd->khd", score_slope, query_heads, preferred_element_type=jnp.float32
            )
            * SCALE
        )
        return (
            jnp.concatenate(query_results, axis=0),
            key_total.reshape(length, span),
            value_total.reshape(length, span),
        )

    items = (
        split_pairs(queries, pairs),
        split_pairs(keys_all, pairs),
        split_pairs(values_all, pairs),
        split_pairs(attended_slope, pairs),
        tops,
        totals,
        jnp.arange(seqs * pairs, dtype=jnp.int32),
    )
    query_slope, key_part, value_part = lax.map(one_item, items)
    return (join_pairs(query_slope, seqs), join_pairs(key_part, seqs), join_pairs(value_part, seqs))


def on_device(
    layer_input,
    cotangent,
    segments,
    slot_order,
    first_gain,
    first_shift,
    project_weight,
    project_bias,
    output_weight,
    output_bias,
    second_gain,
    second_shift,
    expand_weight,
    expand_bias,
    shrink_weight,
    shrink_bias,
):
    seqs, rows, model_width = layer_input.shape
    count = seqs * rows
    half = rows // 2
    length = rows * lax.axis_size("ctx")
    begin = lax.axis_index("ctx") * rows
    local_width = project_weight.shape[2]
    pairs = local_width // (2 * HEAD_DIM)
    (
        gain_one,
        shift_one,
        project_full,
        output_full,
        out_bias,
        gain_two,
        shift_two,
        expand_full,
        shrink_full,
        shrink_add,
    ) = (
        lax.all_gather(first_gain, ("fsdp", "ctx"), axis=0, tiled=True),
        lax.all_gather(first_shift, ("fsdp", "ctx"), axis=0, tiled=True),
        lax.all_gather(project_weight, ("fsdp", "ctx"), axis=0, tiled=True),
        lax.all_gather(output_weight, ("fsdp", "ctx"), axis=1, tiled=True),
        lax.all_gather(output_bias, ("fsdp", "ctx"), axis=0, tiled=True),
        lax.all_gather(second_gain, ("fsdp", "ctx"), axis=0, tiled=True),
        lax.all_gather(second_shift, ("fsdp", "ctx"), axis=0, tiled=True),
        lax.all_gather(expand_weight, ("fsdp", "ctx"), axis=0, tiled=True),
        lax.all_gather(shrink_weight, ("fsdp", "ctx"), axis=1, tiled=True),
        lax.all_gather(shrink_bias, ("fsdp", "ctx"), axis=0, tiled=True),
    )
    offsets = jnp.arange(half, dtype=jnp.int32)
    key_places = (slot_order[:, :, None] * half + offsets[None, None, :]).reshape(seqs, length)
    query_places = lax.dynamic_slice_in_dim(key_places, begin, rows, 1)
    query_groups = lax.dynamic_slice_in_dim(segments, begin, rows, 1)
    inputs = layer_input.reshape(count, model_width).astype(jnp.float32)
    unit_one, inverse_one = normalize_parts(inputs)
    normed_one = (unit_one * gain_one.astype(jnp.float32) + shift_one.astype(jnp.float32)).astype(
        jnp.bfloat16
    )
    project_flat = project_full.reshape(model_width, 3 * local_width)
    mixed = jnp.dot(normed_one, project_flat, preferred_element_type=jnp.float32).reshape(
        count, 3, local_width
    )
    bias_pair = project_bias.astype(jnp.float32)
    queries = (mixed[:, 0] + bias_pair[0]).astype(jnp.bfloat16).reshape(seqs, rows, local_width)
    keys = mixed[:, 1].astype(jnp.bfloat16).reshape(seqs, rows, local_width)
    values = (mixed[:, 2] + bias_pair[1]).astype(jnp.bfloat16).reshape(seqs, rows, local_width)
    keys_all, values_all = (
        lax.all_gather(keys, "ctx", axis=1, tiled=True),
        lax.all_gather(values, "ctx", axis=1, tiled=True),
    )
    attended, tops, totals = attend_forward(
        queries, keys_all, values_all, query_places, query_groups, key_places, segments, pairs
    )
    attended_flat = attended.reshape(count, local_width)
    branch = lax.psum(jnp.dot(attended_flat, output_full, preferred_element_type=jnp.float32), "tp")
    middle = inputs + branch + out_bias.astype(jnp.float32)
    unit_two, inverse_two = normalize_parts(middle)
    normed_two = (unit_two * gain_two.astype(jnp.float32) + shift_two.astype(jnp.float32)).astype(
        jnp.bfloat16
    )
    before = jnp.dot(
        normed_two, expand_full, preferred_element_type=jnp.float32
    ) + expand_bias.astype(jnp.float32)
    active_value, gelu_pull = jax.vjp(partial(jax.nn.gelu, approximate=True), before)
    active = active_value.astype(jnp.bfloat16)
    feed = lax.psum(
        jnp.dot(active, shrink_full, preferred_element_type=jnp.float32).astype(jnp.bfloat16), "tp"
    ).astype(jnp.float32)
    layer_output = (
        (middle + feed + shrink_add.astype(jnp.float32))
        .astype(jnp.bfloat16)
        .reshape(seqs, rows, model_width)
    )
    gain_back, project_again, output_back, gain_two_back, expand_back, shrink_back = (
        lax.all_gather(first_gain, ("fsdp", "ctx"), axis=0, tiled=True),
        lax.all_gather(project_weight, ("fsdp", "ctx"), axis=0, tiled=True),
        lax.all_gather(output_weight, ("fsdp", "ctx"), axis=1, tiled=True),
        lax.all_gather(second_gain, ("fsdp", "ctx"), axis=0, tiled=True),
        lax.all_gather(expand_weight, ("fsdp", "ctx"), axis=0, tiled=True),
        lax.all_gather(shrink_weight, ("fsdp", "ctx"), axis=1, tiled=True),
    )
    project_back = project_again.reshape(model_width, 3 * local_width)
    slope = cotangent.reshape(count, model_width).astype(jnp.float32)
    shrink_bias_delta = jnp.sum(slope, axis=0)
    slope_low = slope.astype(jnp.bfloat16)
    shrink_weight_delta = contract_rows(active, slope_low)
    active_slope = times_transpose(slope_low, shrink_back)
    before_slope = gelu_pull(active_slope)[0].astype(jnp.bfloat16)
    expand_bias_delta = jnp.sum(before_slope.astype(jnp.float32), axis=0)
    expand_weight_delta = contract_rows(normed_two, before_slope)
    normed_two_slope = lax.psum(
        times_transpose(before_slope, expand_back).astype(jnp.bfloat16), "tp"
    ).astype(jnp.float32)
    back_two, gain_two_delta, shift_two_delta = norm_backward(
        normed_two_slope, unit_two, inverse_two, gain_two_back.astype(jnp.float32)
    )
    middle_slope = slope + back_two
    output_bias_delta = jnp.sum(middle_slope, axis=0)
    middle_low = middle_slope.astype(jnp.bfloat16)
    output_weight_delta = contract_rows(attended_flat, middle_low)
    attended_slope = (
        times_transpose(middle_low, output_back)
        .astype(jnp.bfloat16)
        .reshape(seqs, rows, local_width)
    )
    query_slope, key_part, value_part = attend_backward(
        queries,
        keys_all,
        values_all,
        attended_slope,
        tops,
        totals,
        query_places,
        query_groups,
        key_places,
        segments,
        pairs,
    )
    key_slope, value_slope = (
        lax.psum_scatter(
            key_part.astype(jnp.bfloat16), "ctx", scatter_dimension=1, tiled=True
        ).astype(jnp.float32),
        lax.psum_scatter(
            value_part.astype(jnp.bfloat16), "ctx", scatter_dimension=1, tiled=True
        ).astype(jnp.float32),
    )
    key_low = key_slope.astype(jnp.bfloat16)
    value_low = value_slope.astype(jnp.bfloat16)
    project_slope = jnp.stack([query_slope, key_low, value_low], axis=2).reshape(
        count, 3 * local_width
    )
    project_weight_delta = contract_rows(normed_one, project_slope).reshape(
        model_width, 3, local_width
    )
    project_bias_delta = jnp.stack(
        [
            jnp.sum(query_slope.reshape(count, local_width).astype(jnp.float32), axis=0),
            jnp.sum(value_low.reshape(count, local_width).astype(jnp.float32), axis=0),
        ]
    )
    normed_one_slope = lax.psum(
        times_transpose(project_slope, project_back).astype(jnp.bfloat16), "tp"
    ).astype(jnp.float32)
    back_one, gain_one_delta, shift_one_delta = norm_backward(
        normed_one_slope, unit_one, inverse_one, gain_back.astype(jnp.float32)
    )
    input_delta = (middle_slope + back_one).reshape(seqs, rows, model_width)
    (
        part_gain_one,
        part_shift_one,
        part_project,
        part_output,
        part_out_bias,
        part_gain_two,
        part_shift_two,
        part_expand,
        part_shrink,
        part_shrink_bias,
    ) = (
        lax.psum_scatter(
            gain_one_delta.astype(jnp.bfloat16), "fsdp", scatter_dimension=0, tiled=True
        ).astype(jnp.float32),
        lax.psum_scatter(
            shift_one_delta.astype(jnp.bfloat16), "fsdp", scatter_dimension=0, tiled=True
        ).astype(jnp.float32),
        lax.psum_scatter(
            project_weight_delta.astype(jnp.bfloat16), "fsdp", scatter_dimension=0, tiled=True
        ).astype(jnp.float32),
        lax.psum_scatter(
            output_weight_delta.astype(jnp.bfloat16), "fsdp", scatter_dimension=1, tiled=True
        ).astype(jnp.float32),
        lax.psum_scatter(
            output_bias_delta.astype(jnp.bfloat16), "fsdp", scatter_dimension=0, tiled=True
        ).astype(jnp.float32),
        lax.psum_scatter(
            gain_two_delta.astype(jnp.bfloat16), "fsdp", scatter_dimension=0, tiled=True
        ).astype(jnp.float32),
        lax.psum_scatter(
            shift_two_delta.astype(jnp.bfloat16), "fsdp", scatter_dimension=0, tiled=True
        ).astype(jnp.float32),
        lax.psum_scatter(
            expand_weight_delta.astype(jnp.bfloat16), "fsdp", scatter_dimension=0, tiled=True
        ).astype(jnp.float32),
        lax.psum_scatter(
            shrink_weight_delta.astype(jnp.bfloat16), "fsdp", scatter_dimension=1, tiled=True
        ).astype(jnp.float32),
        lax.psum_scatter(
            shrink_bias_delta.astype(jnp.bfloat16), "fsdp", scatter_dimension=0, tiled=True
        ).astype(jnp.float32),
    )
    shares = (
        lax.psum_scatter(
            part_gain_one.astype(jnp.bfloat16), "ctx", scatter_dimension=0, tiled=True
        ).astype(jnp.float32),
        lax.psum_scatter(
            part_shift_one.astype(jnp.bfloat16), "ctx", scatter_dimension=0, tiled=True
        ).astype(jnp.float32),
        lax.psum_scatter(
            part_project.astype(jnp.bfloat16), "ctx", scatter_dimension=0, tiled=True
        ).astype(jnp.float32),
        lax.psum_scatter(
            part_output.astype(jnp.bfloat16), "ctx", scatter_dimension=1, tiled=True
        ).astype(jnp.float32),
        lax.psum_scatter(
            part_out_bias.astype(jnp.bfloat16), "ctx", scatter_dimension=0, tiled=True
        ).astype(jnp.float32),
        lax.psum_scatter(
            part_gain_two.astype(jnp.bfloat16), "ctx", scatter_dimension=0, tiled=True
        ).astype(jnp.float32),
        lax.psum_scatter(
            part_shift_two.astype(jnp.bfloat16), "ctx", scatter_dimension=0, tiled=True
        ).astype(jnp.float32),
        lax.psum_scatter(
            part_expand.astype(jnp.bfloat16), "ctx", scatter_dimension=0, tiled=True
        ).astype(jnp.float32),
        lax.psum_scatter(
            part_shrink.astype(jnp.bfloat16), "ctx", scatter_dimension=1, tiled=True
        ).astype(jnp.float32),
        lax.psum_scatter(
            part_shrink_bias.astype(jnp.bfloat16), "ctx", scatter_dimension=0, tiled=True
        ).astype(jnp.float32),
    )
    bias_sums = lax.psum((project_bias_delta, expand_bias_delta), ("fsdp", "ctx"))
    return (
        layer_output,
        input_delta,
        shares[0],
        shares[1],
        shares[2],
        bias_sums[0],
        shares[3],
        shares[4],
        shares[5],
        shares[6],
        shares[7],
        bias_sums[1],
        shares[8],
        shares[9],
    )


MESH = pl.DeviceIdType.MESH
VMEM_BYTES = 67043328
PIECES = 4


def dot_nn(left, right):
    return lax.dot_general(
        left, right, (((1,), (0,)), ((), ())), preferred_element_type=jnp.float32
    )


def dot_nt(left, right):
    return lax.dot_general(
        left, right, (((1,), (1,)), ((), ())), preferred_element_type=jnp.float32
    )


def remote(source, target, send, receive, device):
    return pltpu.make_async_remote_copy(
        src_ref=source,
        dst_ref=target,
        send_sem=send,
        recv_sem=receive,
        device_id=device,
        device_id_type=MESH,
    )


def aligned(index, size, unit=16):
    return pl.ds(pl.multiple_of(index * size, unit), size)


class Place:
    def __init__(self, line):
        self.line = line
        self.f = lax.axis_index("fsdp")
        self.c = lax.axis_index("ctx")
        self.t = lax.axis_index("tp")
        self.core_bit = lax.rem(self.c, 2)
        self.row_bit = self.c // 2
        self.core = self.c + 1 - 2 * self.core_bit
        self.row = lax.rem(self.c + 2, 4)
        self.other = lax.rem(self.core + 2, 4)
        self.core_device = (self.f, self.core, self.t)
        self.row_device = (self.f, self.row, self.t)
        self.tp_device = (self.f, self.c, 1 - self.t)

    def line_device(self, f):
        return (f, self.c, self.t)

    def greet(self):
        barrier = pltpu.get_barrier_semaphore()
        others = [self.core_device, self.row_device, self.tp_device]
        for step in range(1, self.line):
            others.append(self.line_device(lax.rem(self.f + step, self.line)))
        for device in others:
            pl.semaphore_signal(barrier, 1, device_id=device, device_id_type=MESH)
        pl.semaphore_wait(barrier, len(others))

    def each(self, step, action):
        if step == 0:
            action(self.f, 0)
            return

        @pl.when(self.f - step >= 0)
        def _():
            action(self.f - step, 1)

        @pl.when(self.f + step < self.line)
        def _():
            action(self.f + step, -1)

    def can_pass(self, way):
        return self.f < self.line - 1 if way > 0 else self.f > 0


class Gather:
    def __init__(self, place, group, own, full, row_first, sems):
        self.at, self.group, self.own, self.full, self.row_first = place, group, own, full, row_first
        self.line_send, self.line_recv, self.row_send, self.row_recv, self.core_send, self.core_recv = sems
        self.shard = own.shape[0]

    def part(self, f, other):
        ctx = self.at.row if other else self.at.c
        return self.full.at[aligned(f * 4 + ctx, self.shard), :]

    def line_copy(self, f, way, other=0, own=False):
        part = self.part(f, other)
        return remote(
            self.own if own else part,
            part,
            self.line_send.at[self.group, other, (way + 1) // 2, f],
            self.line_recv.at[self.group, other, f],
            self.at.line_device(self.at.f + way),
        )

    def row_copy(self, f, own=False):
        part = self.part(f, 0)
        return remote(
            self.own if own else part,
            part,
            self.row_send.at[self.group, f],
            self.row_recv.at[self.group, f],
            self.at.row_device,
        )

    def core_copy(self, f, other, own=False):
        part = self.part(f, other)
        return remote(
            self.own if own else part,
            part,
            self.core_send.at[self.group, other, f],
            self.core_recv.at[self.group, other, f],
            self.at.core_device,
        )

    def start_line(self, other=0):
        for way in (1, -1):

            @pl.when(self.at.can_pass(way))
            def _(way=way):
                self.line_copy(self.at.f, way, other, own=not other).start()

    def start_row(self):
        self.row_copy(self.at.f, own=True).start()

    def start_core(self):
        self.core_copy(self.at.f, 0, own=True).start()
        self.full[aligned(self.at.f * 4 + self.at.c, self.shard), :] = self.own[...]

    def line_step(self, step, other=0):
        def arrive(f, way):
            self.line_copy(f, 1, other).wait_recv()

            @pl.when(self.at.can_pass(way))
            def _():
                self.line_copy(f, way, other).start()

            self.core_copy(f, other).start()
            if not self.row_first:
                self.row_copy(f).start()

        self.at.each(step, arrive)

    def row_step(self, step):
        def arrive(f, _):
            self.row_copy(f).wait_recv()
            self.core_copy(f, 1).start()
            if self.row_first:
                self.start_line(1)

        self.at.each(step, arrive)

    def finish(self):
        for f in range(self.at.line):
            for other in (0, 1):
                self.core_copy(f, other).wait_recv()

    def drain(self):
        for step in range(self.at.line):
            for way in (1, -1):
                source = self.at.f - step * way
                passed = (source >= 0) & (source < self.at.line) & self.at.can_pass(way)

                @pl.when(passed)
                def _(source=source, way=way):
                    for other in range(2 if self.row_first else 1):
                        self.line_copy(source, way, other).wait_send()

        if self.row_first:
            self.row_copy(self.at.f).wait_send()
        for f in range(self.at.line):
            if not self.row_first:
                self.row_copy(f).wait_send()
            for other in (0, 1):
                self.core_copy(f, other).wait_send()


class Scatter:
    def __init__(self, place, group, shard, sems, core, row, line):
        self.place, self.group, self.shard = place, group, shard
        self.core_send, self.core_recv, self.row_send, self.row_recv, self.line_send, self.line_recv = sems
        self.core, self.row, self.line = core, row, line

    def core_copies(self):
        full, landed, _ = self.core
        at = self.place
        copies = []
        for f in range(at.line):
            for y in range(2):
                index = f * 2 + y
                copies.append(
                    remote(
                        full.at[aligned(f * 4 + 2 * y + 1 - at.core_bit, self.shard), :],
                        landed.at[pl.ds(index * self.shard, self.shard), :],
                        self.core_send.at[self.group, index],
                        self.core_recv.at[self.group, index],
                        at.core_device,
                    )
                )
        return copies

    def row_copies(self):
        summed, landed, _ = self.row
        at = self.place
        return [
            remote(
                summed.at[aligned(f * 2 + 1 - at.row_bit, self.shard), :],
                landed.at[pl.ds(f * self.shard, self.shard), :],
                self.row_send.at[self.group, f],
                self.row_recv.at[self.group, f],
                at.row_device,
            )
            for f in range(at.line)
        ]

    def line_copies(self):
        summed, landed, _ = self.line
        at = self.place
        copies = []
        for step in range(1, at.line):
            target = lax.rem(at.f + step, at.line)
            copies.append(
                remote(
                    summed.at[aligned(target, self.shard), :],
                    landed.at[pl.ds((step - 1) * self.shard, self.shard), :],
                    self.line_send.at[self.group, step],
                    self.line_recv.at[self.group, step],
                    at.line_device(target),
                )
            )
        return copies

    def start(self, stage):
        for copy in getattr(self, stage + "_copies")():
            copy.start()

    def core_finish(self):
        full, landed, summed = self.core
        at = self.place
        for index, copy in enumerate(self.core_copies()):
            copy.wait_recv()
            f, y = index // 2, index % 2
            own = full[aligned(f * 4 + 2 * y + at.core_bit, self.shard), :]
            other = landed[index * self.shard : (index + 1) * self.shard, :]
            summed[index * self.shard : (index + 1) * self.shard, :] = (
                own.astype(jnp.float32) + other.astype(jnp.float32)
            ).astype(summed.dtype)

    def row_finish(self):
        summed, landed, result = self.row
        at = self.place
        for f, copy in enumerate(self.row_copies()):
            copy.wait_recv()
            own = summed[aligned(f * 2 + at.row_bit, self.shard), :]
            other = landed[f * self.shard : (f + 1) * self.shard, :]
            result[f * self.shard : (f + 1) * self.shard, :] = (
                own.astype(jnp.float32) + other.astype(jnp.float32)
            ).astype(result.dtype)

    def line_finish(self):
        summed, landed, result = self.line
        at = self.place
        total = summed[aligned(at.f, self.shard), :].astype(jnp.float32)
        for step, copy in enumerate(self.line_copies()):
            copy.wait_recv()
            total = total + landed[step * self.shard : (step + 1) * self.shard, :].astype(jnp.float32)
        result[...] = total

    def drain(self, *stages):
        for stage in stages:
            for copy in getattr(self, stage + "_copies")():
                copy.wait_send()


def split_heads(source, store, scale):
    rows, width = source.shape
    for pair in range(width // 128):
        both = source[:, pair * 128 : (pair + 1) * 128].astype(jnp.float32) * scale
        head = lax.broadcasted_iota(jnp.int32, both.shape, 1) // HEAD_DIM
        for side in range(2):
            store[pair, side * rows : (side + 1) * rows, :] = jnp.where(
                head == side, both, 0.0
            ).astype(jnp.bfloat16)


def write_mask(r, at, key_slot, half):
    keys = aligned(key_slot, half)
    key_seg = r.seg[:, aligned(key_slot, half, 128)].astype(jnp.float32)
    key_part = jnp.broadcast_to(key_seg, (128, half)).T
    key_full = jnp.concatenate([key_part] * (half // 128), axis=1)
    shape = (half, half)
    key_place = r.order[0, key_slot] * half + lax.broadcasted_iota(jnp.int32, shape, 0)
    for part in range(2):
        query_slot = at.c * 2 + part
        query_seg = r.seg[:, aligned(query_slot, half, 128)].astype(jnp.float32)
        query_place = r.order[0, query_slot] * half + lax.broadcasted_iota(jnp.int32, shape, 1)
        allowed = (key_full == query_seg) & (key_place <= query_place)
        r.mask[keys, part * half : (part + 1) * half] = jnp.where(allowed, 0.0, NEGATIVE)


def attend_tile(r, slot, half, rows, width):
    keys = aligned(slot, half)
    mask = r.mask[keys, :]
    mask = jnp.concatenate([mask, mask], axis=1)
    for pair in range(width // 128):
        span = slice(pair * 128, (pair + 1) * 128)
        scores = dot_nt(r.kv[keys, span], r.heads[pair]) + mask
        before = r.top[pair : pair + 1, :]
        after = jnp.maximum(before, jnp.max(scores, axis=0, keepdims=True))
        raised = jnp.exp(scores - after)
        fade = jnp.exp(before - after)
        r.top[pair : pair + 1, :] = after
        r.total[pair : pair + 1, :] = r.total[pair : pair + 1, :] * fade + jnp.sum(
            raised, axis=0, keepdims=True
        )
        value = r.kv[keys, width + pair * 128 : width + (pair + 1) * 128].T
        step = dot_nn(value, raised.astype(jnp.bfloat16))
        for side in range(2):
            spot = slice((2 * pair + side) * HEAD_DIM, (2 * pair + side + 1) * HEAD_DIM)
            columns = slice(side * rows, (side + 1) * rows)
            r.mixed[spot, :] = (
                r.mixed[spot, :] * fade[:, columns]
                + step[side * HEAD_DIM : (side + 1) * HEAD_DIM, columns]
            )


def attend_finish(r, rows, width):
    for pair in range(width // 128):
        for side in range(2):
            spot = slice((2 * pair + side) * HEAD_DIM, (2 * pair + side + 1) * HEAD_DIM)
            columns = slice(side * rows, (side + 1) * rows)
            r.mixed[spot, :] = r.mixed[spot, :] / r.total[pair : pair + 1, columns]
        span = slice(pair * 128, (pair + 1) * 128)
        r.att[:, span] = r.mixed[span, :].T.astype(jnp.bfloat16)
    r.top[...] = r.top[...] + jnp.log(r.total[...])


def back_begin(r, rows, width):
    split_heads(r.att_slope, r.slopes, 1.0)
    for pair in range(width // 128):
        span = slice(pair * 128, (pair + 1) * 128)
        product = r.att_slope[:, span].astype(jnp.float32).T * r.mixed[span, :]
        for side in range(2):
            r.pull[pair : pair + 1, side * rows : (side + 1) * rows] = jnp.sum(
                product[side * HEAD_DIM : (side + 1) * HEAD_DIM, :], axis=0, keepdims=True
            )
    r.dq_sum[...] = jnp.zeros_like(r.dq_sum)


def back_tile(r, slot, target, half, rows, width):
    keys = aligned(slot, half)
    mask = r.mask[keys, :]
    mask = jnp.concatenate([mask, mask], axis=1)
    for pair in range(width // 128):
        span = slice(pair * 128, (pair + 1) * 128)
        value_span = slice(width + pair * 128, width + (pair + 1) * 128)
        key = r.kv[keys, span]
        scores = dot_nt(key, r.heads[pair]) + mask
        chance = jnp.exp(scores - r.top[pair : pair + 1, :])
        pulled = dot_nt(r.kv[keys, value_span], r.slopes[pair])
        slope = (chance * (pulled - r.pull[pair : pair + 1, :])).astype(jnp.bfloat16)
        target[:, value_span] = dot_nn(chance.astype(jnp.bfloat16), r.slopes[pair]).astype(
            jnp.bfloat16
        )
        target[:, span] = dot_nn(slope, r.heads[pair]).astype(jnp.bfloat16)
        step = dot_nn(key.T, slope)
        for side in range(2):
            spot = slice((2 * pair + side) * HEAD_DIM, (2 * pair + side + 1) * HEAD_DIM)
            r.dq_sum[spot, :] += step[
                side * HEAD_DIM : (side + 1) * HEAD_DIM, side * rows : (side + 1) * rows
            ]


def gelu_both(v):
    square = v * v
    inner = GELU_A * v * (1.0 + GELU_B * square)
    bent = jnp.tanh(inner)
    lifted = 0.5 * (1.0 + bent)
    slope = lifted + 0.5 * v * (1.0 - bent * bent) * (GELU_A * (1.0 + 3.0 * GELU_B * square))
    return (v * lifted, slope)


def wide(ref, these):
    return ref[these, :].astype(jnp.float32)


def layer_kernel(line, r):
    at = Place(line)
    shard = r.pv_own.shape[0]
    rows, model = r.x.shape
    width = r.att.shape[1]
    hidden = r.we.shape[1]
    half, some = rows // 2, rows // PIECES
    low = jnp.bfloat16
    gather_sems = (r.g_line_s, r.g_line_r, r.g_row_s, r.g_row_r, r.g_core_s, r.g_core_r)
    scatter_sems = (r.s_core_s, r.s_core_r, r.s_row_s, r.s_row_r, r.s_line_s, r.s_line_r)
    project_in = Gather(at, 0, r.pv_own, r.pv, False, gather_sems)
    output_in = Gather(at, 1, r.wo_own, r.wo, False, gather_sems)
    expand_in = Gather(at, 2, r.we_own, r.we, False, gather_sems)
    shrink_in = Gather(at, 3, r.ws_own, r.ws, True, gather_sems)

    gs, ge, gp = r.ws, r.we, r.ws.at[:, 0 : 3 * width]
    shrink = Scatter(
        at, 0, shard, scatter_sems, (gs, r.gs1, r.gs2), (r.gs2, r.gs3, r.gs4), (r.gs4, r.gs5, r.gs_out)
    )
    expand = Scatter(
        at, 1, shard, scatter_sems, (ge, r.ge1, r.ge2), (r.ge2, r.ge3, r.ge4), (r.ge4, r.ge5, r.ge_out)
    )
    output = Scatter(
        at, 2, shard, scatter_sems, (r.go, r.go1, r.go2), (r.go2, r.go3, r.go4), (r.go4, r.go5, r.go_out)
    )
    project = Scatter(
        at, 3, shard, scatter_sems, (gp, r.gp1, r.gp2), (r.gp2, r.gp3, r.gp4), (r.gp4, r.gp5, r.gp_out)
    )
    vector = Scatter(
        at, 4, shard, scatter_sems, (r.gv, r.gv1, r.gv2), (r.gv2, r.gv3, r.gv4), (r.gv4, r.gv5, r.gv_out)
    )

    def kv_row(part):
        here = r.kv.at[aligned(at.c * 2 + part, half), :]
        return remote(here, here, r.kv_s.at[0, part], r.kv_r.at[0, part], at.row_device)

    def kv_core(part, other):
        here = r.kv.at[aligned((at.row if other else at.c) * 2 + part, half), :]
        return remote(
            here, here, r.kv_s.at[1 + other, part], r.kv_r.at[1 + other, part], at.core_device
        )

    def tp_copy(kind, piece):
        source, target = (
            (r.out_send, r.out_land),
            (r.up_send, r.up_land),
            (r.feed, r.feed_land),
            (r.down_send, r.down_land),
        )[kind]
        these = aligned(piece, some)
        return remote(
            source.at[these, :],
            target.at[these, :],
            r.tp_s.at[kind, piece],
            r.tp_r.at[kind, piece],
            at.tp_device,
        )

    def slopes_of(ctx, part):
        return r.hidden.at[aligned(ctx, half), part * 2 * width : (part + 1) * 2 * width]

    def back_core(far, part):
        return remote(
            slopes_of(at.other if far else at.core, part),
            r.kv_land.at[pl.ds((2 * far + part) * half, half), :],
            r.bk_s.at[far, part],
            r.bk_r.at[far, part],
            at.core_device,
        )

    def back_row(part):
        these = pl.ds(part * half, half)
        return remote(
            r.kv_pass.at[these, :],
            r.kv_land2.at[these, :],
            r.bk_s.at[2, part],
            r.bk_r.at[2, part],
            at.row_device,
        )

    active = r.hidden.at[0:rows, :]
    before_slope = r.hidden.at[rows : 2 * rows, :]

    r.turn[...] = jnp.zeros_like(r.turn)
    for index, ref in enumerate((r.gain1, r.shift1, r.bias_o, r.gain2, r.shift2, r.bias_s)):
        r.turn[index : index + 1, 0:shard] = ref[...].astype(jnp.float32)[None, :]
    for index in range(3):
        r.pv_own[:, index * width : (index + 1) * width] = r.wp[index]
    r.pv_own[:, 3 * width :] = r.turn[...].T[0:shard, :].astype(low)
    r.ebias[...] = r.ebias_own[...].astype(jnp.float32)[None, :]
    at.greet()
    project_in.start_line()
    project_in.start_row()
    project_in.start_core()

    @pl.loop(0, PIECES)
    def _(piece):
        these = aligned(piece, some)
        r.delta[these, :] = normalize_parts(wide(r.x, these))[0]

    project_in.line_step(1)
    project_in.row_step(0)

    @pl.loop(0, 2)
    def _(slot):
        write_mask(r, at, slot, half)

    project_in.line_step(2)
    project_in.row_step(1)

    @pl.loop(2, 4)
    def _(slot):
        write_mask(r, at, slot, half)

    for step in range(3, line):
        project_in.line_step(step)
        project_in.row_step(step - 1)
    output_in.start_line()
    output_in.start_row()
    output_in.start_core()
    expand_in.start_line()
    expand_in.start_core()
    shrink_in.start_line()
    shrink_in.start_core()
    project_in.row_step(line - 1)
    project_in.finish()
    r.vec[...] = r.pv[:, 3 * width :].astype(jnp.float32).T[0:8, :]
    gain, shift = r.vec[0:1, :], r.vec[1:2, :]

    @pl.loop(0, PIECES)
    def _(piece):
        these = aligned(piece, some)
        r.normed[these, :] = (r.delta[these, :] * gain + shift).astype(low)

    bias = r.pbias[...].astype(jnp.float32)
    output_in.line_step(1)
    for part in range(2):
        left = r.normed[part * half : (part + 1) * half, :]
        here = aligned(at.c * 2 + part, half)
        r.kv[here, 0:width] = dot_nn(left, r.pv[:, width : 2 * width]).astype(low)
        r.kv[here, width:] = (dot_nn(left, r.pv[:, 2 * width : 3 * width]) + bias[1:2, :]).astype(low)
        kv_row(part).start()
        kv_core(part, 0).start()
        output_in.line_step(2 + part)
        output_in.row_step(part)
    shrink_in.start_row()
    expand_in.start_row()
    r.att[...] = (dot_nn(r.normed[...], r.pv[:, 0:width]) + bias[0:1, :]).astype(low)
    split_heads(r.att, r.heads, SCALE)
    r.top[...] = jnp.full_like(r.top, NEGATIVE)
    r.total[...] = jnp.zeros_like(r.total)
    r.mixed[...] = jnp.zeros_like(r.mixed)

    @pl.loop(4, 8)
    def _(slot):
        write_mask(r, at, slot, half)

    @pl.loop(0, 8)
    def _(tile):
        @pl.when(tile == 2)
        def _():
            for part in range(2):
                kv_core(part, 0).wait_recv()
            for weight in (expand_in, shrink_in):
                weight.line_step(1)

        for part in range(2):

            @pl.when(tile == 4 + 2 * part)
            def _(part=part):
                kv_row(part).wait_recv()
                kv_core(part, 1).start()
                for weight in (expand_in, shrink_in):
                    weight.line_step(2 + part)

            @pl.when(tile == 5 + 2 * part)
            def _(part=part):
                kv_core(part, 1).wait_recv()

        far = jnp.where(lax.rem(tile, 2) == 0, at.row, at.other)
        ctx = jnp.where(tile < 2, at.c, jnp.where(tile < 4, at.core, far))
        part = jnp.where(tile < 4, lax.rem(tile, 2), (tile - 4) // 2)
        attend_tile(r, ctx * 2 + part, half, rows, width)

    attend_finish(r, rows, width)
    for step in range(2, line):
        output_in.row_step(step)
    output_in.finish()

    @pl.loop(0, PIECES)
    def _(piece):
        these = aligned(piece, some)
        r.out_send[these, :] = dot_nt(r.att[these, :], r.wo[...]).astype(low)
        tp_copy(0, piece).start()

    shrink_in.row_step(0)
    for step in range(line):
        expand_in.row_step(step)
        if step + 1 < line:
            shrink_in.line_step(step + 1, 1)
    shrink_in.finish()
    expand_in.finish()
    out_bias, gain2, shift2 = r.vec[2:3, :], r.vec[3:4, :], r.vec[4:5, :]

    @pl.loop(0, PIECES)
    def _(piece):
        these = aligned(piece, some)
        tp_copy(0, piece).wait_recv()
        middle = wide(r.x, these) + (wide(r.out_send, these) + wide(r.out_land, these)) + out_bias
        r.mid[these, :] = middle
        unit, _ = normalize_parts(middle)
        normed = (unit * gain2 + shift2).astype(low)
        r.normed2[these, :] = normed
        for column in range(0, hidden, 512):
            span = slice(column, column + 512)
            value, slope = gelu_both(dot_nn(normed, r.we[:, span]) + r.ebias[:, span])
            active[these, span] = value.astype(low)
            before_slope[these, span] = (dot_nn(r.ct[these, :], r.ws[:, span]) * slope).astype(low)
        r.up_send[these, :] = dot_nt(before_slope[these, :], r.we[...]).astype(low)
        tp_copy(1, piece).start()

    @pl.loop(0, PIECES)
    def _(piece):
        these = aligned(piece, some)
        r.feed[these, :] = dot_nt(active[these, :], r.ws[...]).astype(low)
        tp_copy(2, piece).start()

    for weight in (shrink_in, expand_in):
        weight.drain()
    r.turned[...] = r.ct[...].T
    for column in range(0, hidden, 512):
        span = slice(column, column + 512)
        gs[:, span] = dot_nn(r.turned[...], active[:, span]).astype(low)
    shrink.start("core")
    r.turned[...] = r.normed2[...].T
    for column in range(0, hidden, 512):
        span = slice(column, column + 512)
        ge[:, span] = dot_nn(r.turned[...], before_slope[:, span]).astype(low)
    expand.start("core")
    shrink.core_finish()
    shrink.start("row")
    r.bsum[...] = jnp.sum(before_slope[...].astype(jnp.float32), axis=0, keepdims=True)
    expand.core_finish()
    expand.start("row")
    r.vsum[...] = jnp.zeros_like(r.vsum)

    @pl.loop(0, PIECES)
    def _(piece):
        these = aligned(piece, some)
        tp_copy(1, piece).wait_recv()
        upstream = wide(r.up_send, these) + wide(r.up_land, these)
        unit, inverse = normalize_parts(r.mid[these, :])
        back, gain_delta, shift_delta = norm_backward(upstream, unit, inverse, gain2)
        slope = wide(r.ct, these)
        middle_slope = slope + back
        r.mids[these, :] = middle_slope
        r.vsum[2:3, :] += jnp.sum(middle_slope, axis=0, keepdims=True)
        r.vsum[3:4, :] += gain_delta[None]
        r.vsum[4:5, :] += shift_delta[None]
        r.vsum[5:6, :] += jnp.sum(slope, axis=0, keepdims=True)
        rounded = middle_slope.astype(low)
        r.normed2[these, :] = rounded
        r.att_slope[these, :] = dot_nn(rounded, r.wo[...]).astype(low)

    back_begin(r, rows, width)
    r.turned[...] = r.normed2[...].T
    r.go[...] = dot_nn(r.turned[...], r.att[...]).astype(low)
    output.start("core")
    shrink.row_finish()
    shrink.start("line")

    @pl.loop(0, 8)
    def _(tile):
        pair = tile // 2
        ctx = jnp.where(
            pair < 2, jnp.where(pair == 0, at.other, at.row), jnp.where(pair == 2, at.core, at.c)
        )
        part = lax.rem(tile, 2)
        back_tile(r, ctx * 2 + part, r.tile, half, rows, width)
        for index in range(2):

            @pl.when(part == index)
            def _(index=index):
                slopes_of(ctx, index)[...] = r.tile[...]

        for index in range(2):

            @pl.when(tile == index)
            def _(index=index):
                back_core(1, index).start()

            @pl.when(tile == 2 + index)
            def _(index=index):
                back_core(1, index).wait_recv()
                landed = r.kv_land[(2 + index) * half : (3 + index) * half, :]
                r.kv_pass[index * half : (index + 1) * half, :] = (
                    r.tile[...].astype(jnp.float32) + landed.astype(jnp.float32)
                ).astype(low)
                back_row(index).start()

            @pl.when(tile == 4 + index)
            def _(index=index):
                back_core(0, index).start()

        @pl.when(tile == 3)
        def _():
            output.core_finish()
            output.start("row")

        @pl.when(tile == 5)
        def _():
            expand.row_finish()
            expand.start("line")

    for pair in range(width // 128):
        span = slice(pair * 128, (pair + 1) * 128)
        r.dq[:, span] = (r.dq_sum[span, :] * SCALE).T.astype(low)

    @pl.loop(0, PIECES)
    def _(piece):
        these = aligned(piece, some)
        r.delta[these, :] = dot_nt(r.dq[these, :], r.pv[:, 0:width])

    shrink.drain("core")
    r.turned[...] = r.normed[...].T
    gp[:, 0:width] = dot_nn(r.turned[...], r.dq[...]).astype(low)
    shrink_bias = r.vec[5:6, :]

    @pl.loop(0, PIECES)
    def _(piece):
        these = aligned(piece, some)
        tp_copy(2, piece).wait_recv()
        feed = (wide(r.feed, these) + wide(r.feed_land, these)).astype(low)
        r.out[these, :] = (r.mid[these, :] + feed.astype(jnp.float32) + shrink_bias).astype(low)

    for part in range(2):
        back_core(0, part).wait_recv()
        back_row(part).wait_recv()
        these = slice(part * half, (part + 1) * half)
        total = slopes_of(at.c, part)[...].astype(jnp.float32)
        total = total + wide(r.kv_land, slice(part * half, (part + 1) * half))
        total = total + wide(r.kv_land2, these)
        r.kv_low[these, :] = total.astype(low)
        for step in range(PIECES // 2):
            piece = part * (PIECES // 2) + step
            these = slice(piece * some, (piece + 1) * some)
            r.down_send[these, :] = (
                r.delta[these, :] + dot_nt(r.kv_low[these, :], r.pv[:, width : 3 * width])
            ).astype(low)
            tp_copy(3, piece).start()
    for piece in range(2):
        span = slice((1 + piece) * width, (2 + piece) * width)
        gp[:, span] = dot_nn(r.turned[...], r.kv_low[:, piece * width : (piece + 1) * width]).astype(low)
    project.start("core")
    bias_row = jnp.concatenate(
        [
            r.bsum[...],
            jnp.sum(r.dq[...].astype(jnp.float32), axis=0, keepdims=True),
            jnp.sum(r.kv_low[:, width:].astype(jnp.float32), axis=0, keepdims=True),
        ],
        axis=1,
    )
    r.bias_pack[...] = jnp.zeros_like(r.bias_pack)
    for index in range(bias_row.shape[1] // 128):
        r.bias_pack[0, index : index + 1, :] = bias_row[:, index * 128 : (index + 1) * 128]

    def bias_copy(stage):
        device = (at.core_device, at.row_device)[stage]
        return remote(
            r.bias_pack.at[stage], r.bias_land.at[stage], r.b_s.at[0, stage], r.b_r.at[0, stage], device
        )

    def bias_line_copy(step):
        target = lax.rem(at.f + step, line)
        return remote(
            r.bias_pack.at[2],
            r.bias_line.at[at.f],
            r.b_s.at[1, step],
            r.b_r.at[1, step],
            at.line_device(target),
        )

    bias_copy(0).start()
    output.row_finish()
    output.start("line")
    project.core_finish()
    project.start("row")
    bias_copy(0).wait_recv()
    r.bias_pack[1, :, :] = r.bias_pack[0, :, :] + r.bias_land[0, :, :]
    bias_copy(1).start()
    shrink.line_finish()
    bias_copy(1).wait_recv()
    r.bias_pack[2, :, :] = r.bias_pack[1, :, :] + r.bias_land[1, :, :]
    for step in range(1, line):
        bias_line_copy(step).start()
    project.row_finish()
    project.start("line")
    expand.line_finish()
    r.turn_wide[...] = jnp.zeros_like(r.turn_wide)
    r.turn_wide[0:8, :] = r.vsum[...]

    @pl.loop(0, PIECES)
    def _(piece):
        these = aligned(piece, some)
        tp_copy(3, piece).wait_recv()
        upstream = wide(r.down_send, these) + wide(r.down_land, these)
        unit, inverse = normalize_parts(wide(r.x, these))
        slope, gain_delta, shift_delta = norm_backward(upstream, unit, inverse, gain)
        r.delta[these, :] = r.mids[these, :] + slope
        r.turn_wide[0:1, :] += gain_delta[None]
        r.turn_wide[1:2, :] += shift_delta[None]

    r.gv[...] = r.turn_wide[...].T.astype(low)
    vector.start("core")
    output.line_finish()
    vector.core_finish()
    vector.start("row")
    vector.row_finish()
    vector.start("line")
    for step in range(1, line):
        source = lax.rem(at.f + line - step, line)
        remote(
            r.bias_pack.at[2], r.bias_line.at[source], r.b_s.at[1, step], r.b_r.at[1, step], at.row_device
        ).wait_recv()
    r.bias_line[at.f, :, :] = r.bias_pack[2, :, :]
    total = r.bias_line[0, :, :]
    for f in range(1, line):
        total = total + r.bias_line[f, :, :]
    r.bias_out[...] = total
    project.line_finish()
    vector.line_finish()
    project_in.drain()
    output_in.drain()
    for part in range(2):
        kv_row(part).wait_send()
        back_row(part).wait_send()
        for index in range(2):
            kv_core(part, index).wait_send()
            back_core(index, part).wait_send()
    for kind in range(4):
        for piece in range(PIECES):
            tp_copy(kind, piece).wait_send()
    for stage in range(2):
        bias_copy(stage).wait_send()
    for step in range(1, line):
        bias_line_copy(step).wait_send()
    shrink.drain("row", "line")
    for gradient in (expand, output, project, vector):
        gradient.drain("core", "row", "line")


def finish_kernel(r):
    r.out_end[0] = r.out[...]
    r.delta_end[0] = r.delta[...]
    r.gs_end[...] = r.gs[...]
    r.ge_end[...] = r.ge[...]
    r.go_end[...] = r.go[...]
    width = r.go.shape[1]
    for index in range(3):
        r.gp_end[index] = r.gp[:, index * width : (index + 1) * width]
    vectors = r.gv[...].T
    shard = r.gv.shape[0]
    for index in range(6):
        r["gv%d" % index][...] = vectors[index, 0:shard]
    hidden = r.ebias.shape[0]
    for index in range(hidden // 128):
        r.ebias[pl.ds(index * 128, 128)] = r.biases[index, :]
    each = width // 128
    for index in range(2 * each):
        row, column = index // each, index % each
        place = hidden // 128 + index
        r.pbias[row : row + 1, column * 128 : (column + 1) * 128] = r.biases[place : place + 1, :]


class Refs(dict):
    __getattr__ = dict.__getitem__


def call(kernel, ins, outs, scratch, smem=(), identity=None):
    names = [*ins, *outs, *scratch]
    params = dict(vmem_limit_bytes=VMEM_BYTES)
    if identity is not None:
        params.update(collective_id=identity, has_side_effects=True)
    results = pl.pallas_call(
        lambda *refs: kernel(Refs(zip(names, refs))),
        out_shape=[jax.ShapeDtypeStruct(shape, dtype) for shape, dtype in outs.values()],
        in_specs=[
            pl.BlockSpec(memory_space=pltpu.SMEM if name in smem else pltpu.VMEM) for name in ins
        ],
        out_specs=[pl.BlockSpec(memory_space=pltpu.VMEM)] * len(outs),
        scratch_shapes=[
            pltpu.VMEM(*spec) if isinstance(spec, tuple) else spec for spec in scratch.values()
        ],
        compiler_params=pltpu.CompilerParams(**params),
    )(*ins.values())
    return Refs(zip(outs, results))


def by_kernels(
    layer_input,
    cotangent,
    segments,
    slot_order,
    first_gain,
    first_shift,
    project_weight,
    project_bias,
    output_weight,
    output_bias,
    second_gain,
    second_shift,
    expand_weight,
    expand_bias,
    shrink_weight,
    shrink_bias,
):
    low, full = jnp.bfloat16, jnp.float32
    line = lax.axis_size("fsdp")
    _, rows, model = layer_input.shape
    length = segments.shape[1]
    shard, _, width = project_weight.shape
    hidden = expand_weight.shape[1]
    pairs = width // 128
    half = rows // 2
    packed = 3 * width + 128
    two, one = 2 * line * shard, line * shard
    less = one - shard
    bias_rows = -(-(hidden + 2 * width) // 1024) * 8
    dma = lambda *shape: pltpu.SemaphoreType.DMA(shape)

    def stages(name, columns):
        sizes = (two, two, one, one, less)
        return {"%s%d" % (name, index + 1): ((size, columns), low) for index, size in enumerate(sizes)}

    done = call(
        partial(layer_kernel, line),
        dict(
            x=layer_input.reshape(rows, model),
            ct=cotangent.reshape(rows, model),
            seg=segments,
            order=slot_order,
            gain1=first_gain,
            shift1=first_shift,
            bias_o=output_bias,
            gain2=second_gain,
            shift2=second_shift,
            bias_s=shrink_bias,
            wp=project_weight.transpose(1, 0, 2),
            pbias=project_bias,
            wo_own=output_weight.T,
            we_own=expand_weight,
            ws_own=shrink_weight.T,
            ebias_own=expand_bias,
        ),
        dict(
            out=((rows, model), low),
            delta=((rows, model), full),
            gs_out=((shard, hidden), full),
            ge_out=((shard, hidden), full),
            go_out=((shard, width), full),
            gp_out=((shard, 3 * width), full),
            gv_out=((shard, 128), full),
            bias_out=((bias_rows, 128), full),
        ),
        dict(
            pv_own=((shard, packed), low),
            pv=((model, packed), low),
            wo=((model, width), low),
            we=((model, hidden), low),
            ws=((model, hidden), low),
            kv=((length, 2 * width), low),
            vec=((8, model), full),
            ebias=((1, hidden), full),
            turn=((128, 128), full),
            turn_wide=((128, model), full),
            normed=((rows, model), low),
            normed2=((rows, model), low),
            turned=((model, rows), low),
            mask=((length, rows), full),
            heads=((pairs, 2 * rows, 128), low),
            slopes=((pairs, 2 * rows, 128), low),
            top=((8, 2 * rows), full),
            total=((8, 2 * rows), full),
            pull=((8, 2 * rows), full),
            mixed=((width, rows), full),
            dq_sum=((width, rows), full),
            att=((rows, width), low),
            att_slope=((rows, width), low),
            dq=((rows, width), low),
            tile=((half, 2 * width), low),
            mid=((rows, model), full),
            mids=((rows, model), full),
            hidden=((2 * rows, hidden), low),
            out_send=((rows, model), low),
            out_land=((rows, model), low),
            up_send=((rows, model), low),
            up_land=((rows, model), low),
            feed=((rows, model), low),
            feed_land=((rows, model), low),
            down_send=((rows, model), low),
            down_land=((rows, model), low),
            kv_land=((2 * rows, 2 * width), low),
            kv_pass=((rows, 2 * width), low),
            kv_land2=((rows, 2 * width), low),
            kv_low=((rows, 2 * width), low),
            bsum=((1, hidden), full),
            vsum=((8, model), full),
            go=((model, width), low),
            gv=((model, 128), low),
            **stages("gs", hidden),
            **stages("ge", hidden),
            **stages("go", width),
            **stages("gp", 3 * width),
            **stages("gv", 128),
            bias_pack=((3, bias_rows, 128), full),
            bias_land=((2, bias_rows, 128), full),
            bias_line=((line, bias_rows, 128), full),
            g_line_s=dma(4, 2, 2, line),
            g_line_r=dma(4, 2, line),
            g_row_s=dma(4, line),
            g_row_r=dma(4, line),
            g_core_s=dma(4, 2, line),
            g_core_r=dma(4, 2, line),
            s_core_s=dma(5, 2 * line),
            s_core_r=dma(5, 2 * line),
            s_row_s=dma(5, line),
            s_row_r=dma(5, line),
            s_line_s=dma(5, line),
            s_line_r=dma(5, line),
            kv_s=dma(3, 2),
            kv_r=dma(3, 2),
            tp_s=dma(4, PIECES),
            tp_r=dma(4, PIECES),
            bk_s=dma(3, 2),
            bk_r=dma(3, 2),
            b_s=dma(2, line),
            b_r=dma(2, line),
        ),
        smem=("order",),
        identity=0,
    )
    end = call(
        finish_kernel,
        dict(
            out=done.out,
            delta=done.delta,
            gs=done.gs_out,
            ge=done.ge_out,
            go=done.go_out,
            gp=done.gp_out,
            gv=done.gv_out,
            biases=done.bias_out,
        ),
        dict(
            out_end=(layer_input.shape, low),
            delta_end=(layer_input.shape, full),
            gs_end=((shard, hidden), full),
            ge_end=((shard, hidden), full),
            go_end=((shard, width), full),
            gp_end=((3, shard, width), full),
            **{"gv%d" % index: ((shard,), full) for index in range(6)},
            ebias=((hidden,), full),
            pbias=((2, width), full),
        ),
        {},
    )
    return (
        end.out_end,
        end.delta_end,
        end.gv0,
        end.gv1,
        end.gp_end.transpose(1, 0, 2),
        end.pbias,
        end.go_end.T,
        end.gv2,
        end.gv3,
        end.gv4,
        end.ge_end,
        end.ebias,
        end.gs_end.T,
        end.gv5,
    )


def solution(mesh):
    n_ctx, n_tp = mesh.shape["ctx"], mesh.shape["tp"]

    def choose(layer_input, *others):
        seqs, rows, model = layer_input.shape
        whole_tiles = model % (16 * n_ctx * mesh.shape["fsdp"]) == 0 and rows % 256 == 0
        if seqs == 1 and n_ctx == 4 and n_tp == 2 and whole_tiles:
            return by_kernels(layer_input, *others)
        return on_device(layer_input, *others)

    return jax.shard_map(
        choose,
        mesh=mesh,
        in_specs=(
            P("fsdp", "ctx", None),
            P("fsdp", "ctx", None),
            P("fsdp", None),
            P("fsdp", None),
            P(("fsdp", "ctx")),
            P(("fsdp", "ctx")),
            P(("fsdp", "ctx"), None, "tp"),
            P(None, "tp"),
            P("tp", ("fsdp", "ctx")),
            P(("fsdp", "ctx")),
            P(("fsdp", "ctx")),
            P(("fsdp", "ctx")),
            P(("fsdp", "ctx"), "tp"),
            P("tp"),
            P("tp", ("fsdp", "ctx")),
            P(("fsdp", "ctx")),
        ),
        out_specs=(
            P("fsdp", "ctx", None),
            P("fsdp", "ctx", None),
            P(("fsdp", "ctx")),
            P(("fsdp", "ctx")),
            P(("fsdp", "ctx"), None, "tp"),
            P(None, "tp"),
            P("tp", ("fsdp", "ctx")),
            P(("fsdp", "ctx")),
            P(("fsdp", "ctx")),
            P(("fsdp", "ctx")),
            P(("fsdp", "ctx"), "tp"),
            P("tp"),
            P("tp", ("fsdp", "ctx")),
            P(("fsdp", "ctx")),
        ),
        check_vma=False,
    )
```

```python
from functools import partial

import jax
import jax.numpy as jnp
from jax import lax
from jax.experimental import pallas as pl
from jax.experimental.pallas import tpu as pltpu
from jax.sharding import PartitionSpec as P

HEAD_DIM = 64


EPSILON = 1e-05
SCALE = 0.125
NEGATIVE = -1000000000.0
TILE = 512
GELU_A = 0.7978845608028654
GELU_B = 0.044715


def contract_rows(left, right):
    return lax.dot_general(
        left, right, (((0,), (0,)), ((), ())), preferred_element_type=jnp.float32
    )


def times_transpose(left, right):
    return lax.dot_general(
        left, right, (((1,), (1,)), ((), ())), preferred_element_type=jnp.float32
    )


def normalize_parts(rows):
    mean = jnp.mean(rows, axis=-1, keepdims=True)
    centred = rows - mean
    spread = jnp.mean(centred * centred, axis=-1, keepdims=True)
    inverse = lax.rsqrt(spread + EPSILON)
    return (centred * inverse, inverse)


def norm_backward(upstream, unit, inverse, gain):
    scaled = upstream * gain
    back = inverse * (
        scaled
        - jnp.mean(scaled, axis=-1, keepdims=True)
        - unit * jnp.mean(scaled * unit, axis=-1, keepdims=True)
    )
    return (back, jnp.sum(upstream * unit, axis=0), jnp.sum(upstream, axis=0))


def split_pairs(array, pairs):
    seqs, count, width = array.shape
    span = width // pairs
    return (
        array.reshape(seqs, count, pairs, span)
        .transpose(0, 2, 1, 3)
        .reshape(seqs * pairs, count, span)
    )


def join_pairs(array, seqs):
    items, count, span = array.shape
    pairs = items // seqs
    return (
        array.reshape(seqs, pairs, count, span)
        .transpose(0, 2, 1, 3)
        .reshape(seqs, count, pairs * span)
    )


def masked_scores(query_heads, key_heads, query_place, query_group, key_place, key_group):
    scores = (
        jnp.einsum("qhd,khd->hqk", query_heads, key_heads, preferred_element_type=jnp.float32)
        * SCALE
    )
    allowed = (query_group[:, None] == key_group[None, :]) & (
        key_place[None, :] <= query_place[:, None]
    )
    return jnp.where(allowed[None], scores, NEGATIVE)


def attend_forward(
    queries, keys_all, values_all, query_places, query_groups, key_places, key_groups, pairs
):
    seqs, rows, width = queries.shape
    length = keys_all.shape[1]
    span = width // pairs
    tile = min(TILE, rows)

    def one_item(item):
        query_part, key_part, value_part, index = item
        which = index // pairs
        query_place = lax.dynamic_index_in_dim(query_places, which, 0, keepdims=False)
        query_group = lax.dynamic_index_in_dim(query_groups, which, 0, keepdims=False)
        key_place = lax.dynamic_index_in_dim(key_places, which, 0, keepdims=False)
        key_group = lax.dynamic_index_in_dim(key_groups, which, 0, keepdims=False)
        key_heads = key_part.reshape(length, 2, span // 2)
        value_heads = value_part.reshape(length, 2, span // 2)
        results, tops, totals = ([], [], [])
        query_heads = query_part.reshape(tile, 2, span // 2)
        scores = masked_scores(
            query_heads, key_heads, query_place, query_group, key_place, key_group
        )
        top = jnp.max(scores, axis=-1)
        raised = jnp.exp(scores - top[..., None])
        total = jnp.sum(raised, axis=-1)
        chance = (raised / total[..., None]).astype(jnp.bfloat16)
        mixed = jnp.einsum("hqk,khd->qhd", chance, value_heads, preferred_element_type=jnp.float32)
        results.append(mixed.reshape(tile, span).astype(jnp.bfloat16))
        tops.append(top)
        totals.append(total)
        return (
            jnp.concatenate(results, axis=0),
            jnp.concatenate(tops, axis=1),
            jnp.concatenate(totals, axis=1),
        )

    items = (
        split_pairs(queries, pairs),
        split_pairs(keys_all, pairs),
        split_pairs(values_all, pairs),
        jnp.arange(seqs * pairs, dtype=jnp.int32),
    )
    mixed, tops, totals = lax.map(one_item, items)
    return (join_pairs(mixed, seqs), tops, totals)


def attend_backward(
    queries,
    keys_all,
    values_all,
    attended_slope,
    tops,
    totals,
    query_places,
    query_groups,
    key_places,
    key_groups,
    pairs,
):
    seqs, rows, width = queries.shape
    length = keys_all.shape[1]
    span = width // pairs
    tile = min(TILE, rows)

    def one_item(item):
        query_part, key_part, value_part, slope_part, top, total, index = item
        which = index // pairs
        query_place = lax.dynamic_index_in_dim(query_places, which, 0, keepdims=False)
        query_group = lax.dynamic_index_in_dim(query_groups, which, 0, keepdims=False)
        key_place = lax.dynamic_index_in_dim(key_places, which, 0, keepdims=False)
        key_group = lax.dynamic_index_in_dim(key_groups, which, 0, keepdims=False)
        key_heads = key_part.reshape(length, 2, span // 2)
        value_heads = value_part.reshape(length, 2, span // 2)
        key_total = jnp.zeros((length, 2, span // 2), jnp.float32)
        value_total = jnp.zeros((length, 2, span // 2), jnp.float32)
        query_heads = query_part.reshape(tile, 2, span // 2)
        slope_heads = slope_part.reshape(tile, 2, span // 2)
        scores = masked_scores(
            query_heads, key_heads, query_place, query_group, key_place, key_group
        )
        chance = jnp.exp(scores - top[:, 0:tile, None]) / total[:, 0:tile, None]
        chance_low = chance.astype(jnp.bfloat16)
        value_total = value_total + jnp.einsum(
            "hqk,qhd->khd", chance_low, slope_heads, preferred_element_type=jnp.float32
        )
        pulled = jnp.einsum(
            "qhd,khd->hqk", slope_heads, value_heads, preferred_element_type=jnp.float32
        )
        score_slope = (chance * (pulled - jnp.sum(chance * pulled, axis=-1, keepdims=True))).astype(
            jnp.bfloat16
        )
        query_step = (
            jnp.einsum("hqk,khd->qhd", score_slope, key_heads, preferred_element_type=jnp.float32)
            * SCALE
        )
        query_results = [query_step.reshape(tile, span).astype(jnp.bfloat16)]
        key_total = (
            key_total
            + jnp.einsum(
                "hqk,qhd->khd", score_slope, query_heads, preferred_element_type=jnp.float32
            )
            * SCALE
        )
        return (
            jnp.concatenate(query_results, axis=0),
            key_total.reshape(length, span),
            value_total.reshape(length, span),
        )

    items = (
        split_pairs(queries, pairs),
        split_pairs(keys_all, pairs),
        split_pairs(values_all, pairs),
        split_pairs(attended_slope, pairs),
        tops,
        totals,
        jnp.arange(seqs * pairs, dtype=jnp.int32),
    )
    query_slope, key_part, value_part = lax.map(one_item, items)
    return (join_pairs(query_slope, seqs), join_pairs(key_part, seqs), join_pairs(value_part, seqs))


def on_device(
    layer_input,
    cotangent,
    segments,
    slot_order,
    first_gain,
    first_shift,
    project_weight,
    project_bias,
    output_weight,
    output_bias,
    second_gain,
    second_shift,
    expand_weight,
    expand_bias,
    shrink_weight,
    shrink_bias,
):
    seqs, rows, model_width = layer_input.shape
    count = seqs * rows
    half = rows // 2
    length = rows * lax.axis_size("ctx")
    begin = lax.axis_index("ctx") * rows
    local_width = project_weight.shape[2]
    pairs = local_width // (2 * HEAD_DIM)
    (
        gain_one,
        shift_one,
        project_full,
        output_full,
        out_bias,
        gain_two,
        shift_two,
        expand_full,
        shrink_full,
        shrink_add,
    ) = (
        lax.all_gather(first_gain, ("fsdp", "ctx"), axis=0, tiled=True),
        lax.all_gather(first_shift, ("fsdp", "ctx"), axis=0, tiled=True),
        lax.all_gather(project_weight, ("fsdp", "ctx"), axis=0, tiled=True),
        lax.all_gather(output_weight, ("fsdp", "ctx"), axis=1, tiled=True),
        lax.all_gather(output_bias, ("fsdp", "ctx"), axis=0, tiled=True),
        lax.all_gather(second_gain, ("fsdp", "ctx"), axis=0, tiled=True),
        lax.all_gather(second_shift, ("fsdp", "ctx"), axis=0, tiled=True),
        lax.all_gather(expand_weight, ("fsdp", "ctx"), axis=0, tiled=True),
        lax.all_gather(shrink_weight, ("fsdp", "ctx"), axis=1, tiled=True),
        lax.all_gather(shrink_bias, ("fsdp", "ctx"), axis=0, tiled=True),
    )
    offsets = jnp.arange(half, dtype=jnp.int32)
    key_places = (slot_order[:, :, None] * half + offsets[None, None, :]).reshape(seqs, length)
    query_places = lax.dynamic_slice_in_dim(key_places, begin, rows, 1)
    query_groups = lax.dynamic_slice_in_dim(segments, begin, rows, 1)
    inputs = layer_input.reshape(count, model_width).astype(jnp.float32)
    unit_one, inverse_one = normalize_parts(inputs)
    normed_one = (unit_one * gain_one.astype(jnp.float32) + shift_one.astype(jnp.float32)).astype(
        jnp.bfloat16
    )
    project_flat = project_full.reshape(model_width, 3 * local_width)
    mixed = jnp.dot(normed_one, project_flat, preferred_element_type=jnp.float32).reshape(
        count, 3, local_width
    )
    bias_pair = project_bias.astype(jnp.float32)
    queries = (mixed[:, 0] + bias_pair[0]).astype(jnp.bfloat16).reshape(seqs, rows, local_width)
    keys = mixed[:, 1].astype(jnp.bfloat16).reshape(seqs, rows, local_width)
    values = (mixed[:, 2] + bias_pair[1]).astype(jnp.bfloat16).reshape(seqs, rows, local_width)
    keys_all, values_all = (
        lax.all_gather(keys, "ctx", axis=1, tiled=True),
        lax.all_gather(values, "ctx", axis=1, tiled=True),
    )
    attended, tops, totals = attend_forward(
        queries, keys_all, values_all, query_places, query_groups, key_places, segments, pairs
    )
    attended_flat = attended.reshape(count, local_width)
    branch = lax.psum(jnp.dot(attended_flat, output_full, preferred_element_type=jnp.float32), "tp")
    middle = inputs + branch + out_bias.astype(jnp.float32)
    unit_two, inverse_two = normalize_parts(middle)
    normed_two = (unit_two * gain_two.astype(jnp.float32) + shift_two.astype(jnp.float32)).astype(
        jnp.bfloat16
    )
    before = jnp.dot(
        normed_two, expand_full, preferred_element_type=jnp.float32
    ) + expand_bias.astype(jnp.float32)
    active_value, gelu_pull = jax.vjp(partial(jax.nn.gelu, approximate=True), before)
    active = active_value.astype(jnp.bfloat16)
    feed = lax.psum(
        jnp.dot(active, shrink_full, preferred_element_type=jnp.float32).astype(jnp.bfloat16), "tp"
    ).astype(jnp.float32)
    layer_output = (
        (middle + feed + shrink_add.astype(jnp.float32))
        .astype(jnp.bfloat16)
        .reshape(seqs, rows, model_width)
    )
    gain_back, project_again, output_back, gain_two_back, expand_back, shrink_back = (
        lax.all_gather(first_gain, ("fsdp", "ctx"), axis=0, tiled=True),
        lax.all_gather(project_weight, ("fsdp", "ctx"), axis=0, tiled=True),
        lax.all_gather(output_weight, ("fsdp", "ctx"), axis=1, tiled=True),
        lax.all_gather(second_gain, ("fsdp", "ctx"), axis=0, tiled=True),
        lax.all_gather(expand_weight, ("fsdp", "ctx"), axis=0, tiled=True),
        lax.all_gather(shrink_weight, ("fsdp", "ctx"), axis=1, tiled=True),
    )
    project_back = project_again.reshape(model_width, 3 * local_width)
    slope = cotangent.reshape(count, model_width).astype(jnp.float32)
    shrink_bias_delta = jnp.sum(slope, axis=0)
    slope_low = slope.astype(jnp.bfloat16)
    shrink_weight_delta = contract_rows(active, slope_low)
    active_slope = times_transpose(slope_low, shrink_back)
    before_slope = gelu_pull(active_slope)[0].astype(jnp.bfloat16)
    expand_bias_delta = jnp.sum(before_slope.astype(jnp.float32), axis=0)
    expand_weight_delta = contract_rows(normed_two, before_slope)
    normed_two_slope = lax.psum(
        times_transpose(before_slope, expand_back).astype(jnp.bfloat16), "tp"
    ).astype(jnp.float32)
    back_two, gain_two_delta, shift_two_delta = norm_backward(
        normed_two_slope, unit_two, inverse_two, gain_two_back.astype(jnp.float32)
    )
    middle_slope = slope + back_two
    output_bias_delta = jnp.sum(middle_slope, axis=0)
    middle_low = middle_slope.astype(jnp.bfloat16)
    output_weight_delta = contract_rows(attended_flat, middle_low)
    attended_slope = (
        times_transpose(middle_low, output_back)
        .astype(jnp.bfloat16)
        .reshape(seqs, rows, local_width)
    )
    query_slope, key_part, value_part = attend_backward(
        queries,
        keys_all,
        values_all,
        attended_slope,
        tops,
        totals,
        query_places,
        query_groups,
        key_places,
        segments,
        pairs,
    )
    key_slope, value_slope = (
        lax.psum_scatter(
            key_part.astype(jnp.bfloat16), "ctx", scatter_dimension=1, tiled=True
        ).astype(jnp.float32),
        lax.psum_scatter(
            value_part.astype(jnp.bfloat16), "ctx", scatter_dimension=1, tiled=True
        ).astype(jnp.float32),
    )
    key_low = key_slope.astype(jnp.bfloat16)
    value_low = value_slope.astype(jnp.bfloat16)
    project_slope = jnp.stack([query_slope, key_low, value_low], axis=2).reshape(
        count, 3 * local_width
    )
    project_weight_delta = contract_rows(normed_one, project_slope).reshape(
        model_width, 3, local_width
    )
    project_bias_delta = jnp.stack(
        [
            jnp.sum(query_slope.reshape(count, local_width).astype(jnp.float32), axis=0),
            jnp.sum(value_low.reshape(count, local_width).astype(jnp.float32), axis=0),
        ]
    )
    normed_one_slope = lax.psum(
        times_transpose(project_slope, project_back).astype(jnp.bfloat16), "tp"
    ).astype(jnp.float32)
    back_one, gain_one_delta, shift_one_delta = norm_backward(
        normed_one_slope, unit_one, inverse_one, gain_back.astype(jnp.float32)
    )
    input_delta = (middle_slope + back_one).reshape(seqs, rows, model_width)
    (
        part_gain_one,
        part_shift_one,
        part_project,
        part_output,
        part_out_bias,
        part_gain_two,
        part_shift_two,
        part_expand,
        part_shrink,
        part_shrink_bias,
    ) = (
        lax.psum_scatter(
            gain_one_delta.astype(jnp.bfloat16), "fsdp", scatter_dimension=0, tiled=True
        ).astype(jnp.float32),
        lax.psum_scatter(
            shift_one_delta.astype(jnp.bfloat16), "fsdp", scatter_dimension=0, tiled=True
        ).astype(jnp.float32),
        lax.psum_scatter(
            project_weight_delta.astype(jnp.bfloat16), "fsdp", scatter_dimension=0, tiled=True
        ).astype(jnp.float32),
        lax.psum_scatter(
            output_weight_delta.astype(jnp.bfloat16), "fsdp", scatter_dimension=1, tiled=True
        ).astype(jnp.float32),
        lax.psum_scatter(
            output_bias_delta.astype(jnp.bfloat16), "fsdp", scatter_dimension=0, tiled=True
        ).astype(jnp.float32),
        lax.psum_scatter(
            gain_two_delta.astype(jnp.bfloat16), "fsdp", scatter_dimension=0, tiled=True
        ).astype(jnp.float32),
        lax.psum_scatter(
            shift_two_delta.astype(jnp.bfloat16), "fsdp", scatter_dimension=0, tiled=True
        ).astype(jnp.float32),
        lax.psum_scatter(
            expand_weight_delta.astype(jnp.bfloat16), "fsdp", scatter_dimension=0, tiled=True
        ).astype(jnp.float32),
        lax.psum_scatter(
            shrink_weight_delta.astype(jnp.bfloat16), "fsdp", scatter_dimension=1, tiled=True
        ).astype(jnp.float32),
        lax.psum_scatter(
            shrink_bias_delta.astype(jnp.bfloat16), "fsdp", scatter_dimension=0, tiled=True
        ).astype(jnp.float32),
    )
    shares = (
        lax.psum_scatter(
            part_gain_one.astype(jnp.bfloat16), "ctx", scatter_dimension=0, tiled=True
        ).astype(jnp.float32),
        lax.psum_scatter(
            part_shift_one.astype(jnp.bfloat16), "ctx", scatter_dimension=0, tiled=True
        ).astype(jnp.float32),
        lax.psum_scatter(
            part_project.astype(jnp.bfloat16), "ctx", scatter_dimension=0, tiled=True
        ).astype(jnp.float32),
        lax.psum_scatter(
            part_output.astype(jnp.bfloat16), "ctx", scatter_dimension=1, tiled=True
        ).astype(jnp.float32),
        lax.psum_scatter(
            part_out_bias.astype(jnp.bfloat16), "ctx", scatter_dimension=0, tiled=True
        ).astype(jnp.float32),
        lax.psum_scatter(
            part_gain_two.astype(jnp.bfloat16), "ctx", scatter_dimension=0, tiled=True
        ).astype(jnp.float32),
        lax.psum_scatter(
            part_shift_two.astype(jnp.bfloat16), "ctx", scatter_dimension=0, tiled=True
        ).astype(jnp.float32),
        lax.psum_scatter(
            part_expand.astype(jnp.bfloat16), "ctx", scatter_dimension=0, tiled=True
        ).astype(jnp.float32),
        lax.psum_scatter(
            part_shrink.astype(jnp.bfloat16), "ctx", scatter_dimension=1, tiled=True
        ).astype(jnp.float32),
        lax.psum_scatter(
            part_shrink_bias.astype(jnp.bfloat16), "ctx", scatter_dimension=0, tiled=True
        ).astype(jnp.float32),
    )
    bias_sums = lax.psum((project_bias_delta, expand_bias_delta), ("fsdp", "ctx"))
    return (
        layer_output,
        input_delta,
        shares[0],
        shares[1],
        shares[2],
        bias_sums[0],
        shares[3],
        shares[4],
        shares[5],
        shares[6],
        shares[7],
        bias_sums[1],
        shares[8],
        shares[9],
    )


MESH = pl.DeviceIdType.MESH
VMEM_BYTES = 67043328
PIECES = 4


def dot_nn(left, right):
    return lax.dot_general(
        left, right, (((1,), (0,)), ((), ())), preferred_element_type=jnp.float32
    )


def dot_nt(left, right):
    return lax.dot_general(
        left, right, (((1,), (1,)), ((), ())), preferred_element_type=jnp.float32
    )


def remote(source, target, send, receive, device):
    return pltpu.make_async_remote_copy(
        src_ref=source,
        dst_ref=target,
        send_sem=send,
        recv_sem=receive,
        device_id=device,
        device_id_type=MESH,
    )


def aligned(index, size, unit=16):
    return pl.ds(pl.multiple_of(index * size, unit), size)


class Place:
    def __init__(self, line):
        self.line = line
        self.f = lax.axis_index("fsdp")
        self.c = lax.axis_index("ctx")
        self.t = lax.axis_index("tp")
        self.core_bit = lax.rem(self.c, 2)
        self.row_bit = self.c // 2
        self.core = self.c + 1 - 2 * self.core_bit
        self.row = lax.rem(self.c + 2, 4)
        self.other = lax.rem(self.core + 2, 4)
        self.core_device = (self.f, self.core, self.t)
        self.row_device = (self.f, self.row, self.t)
        self.tp_device = (self.f, self.c, 1 - self.t)

    def line_device(self, f):
        return (f, self.c, self.t)

    def greet(self):
        barrier = pltpu.get_barrier_semaphore()
        others = [self.core_device, self.row_device, self.tp_device]
        for step in range(1, self.line):
            others.append(self.line_device(lax.rem(self.f + step, self.line)))
        for device in others:
            pl.semaphore_signal(barrier, 1, device_id=device, device_id_type=MESH)
        pl.semaphore_wait(barrier, len(others))

    def each(self, step, action):
        if step == 0:
            action(self.f, 0)
            return

        @pl.when(self.f - step >= 0)
        def _():
            action(self.f - step, 1)

        @pl.when(self.f + step < self.line)
        def _():
            action(self.f + step, -1)

    def can_pass(self, way):
        return self.f < self.line - 1 if way > 0 else self.f > 0


class Gather:
    def __init__(self, place, group, own, full, row_first, direct, sems):
        self.at, self.group, self.own, self.full = place, group, own, full
        self.row_first, self.direct = row_first, direct
        self.line_send, self.line_recv, self.row_send, self.row_recv, self.core_send, self.core_recv = sems
        self.shard = own.shape[0]

    def part(self, f, other):
        ctx = self.at.row if other else self.at.c
        return self.full.at[aligned(f * 4 + ctx, self.shard), :]

    def line_copy(self, f, way, other=0, own=False):
        part = self.part(f, other)
        return remote(
            self.own if own else part,
            part,
            self.line_send.at[self.group, other, (way + 1) // 2, f],
            self.line_recv.at[self.group, other, f],
            self.at.line_device(self.at.f + way),
        )

    def direct_copy(self, step, other):
        part = self.part(self.at.f, other)
        return remote(
            part if other else self.own,
            part,
            self.line_send.at[self.group, other, 0, step],
            self.line_recv.at[self.group, other, self.at.f],
            self.at.line_device(lax.rem(self.at.f + step, self.at.line)),
        )

    def row_copy(self, f, own=False):
        part = self.part(f, 0)
        return remote(
            self.own if own else part,
            part,
            self.row_send.at[self.group, f],
            self.row_recv.at[self.group, f],
            self.at.row_device,
        )

    def core_copy(self, f, other, own=False):
        part = self.part(f, other)
        return remote(
            self.own if own else part,
            part,
            self.core_send.at[self.group, other, f],
            self.core_recv.at[self.group, other, f],
            self.at.core_device,
        )

    def start_line(self, other=0):
        if self.direct:
            for step in range(1, self.at.line):
                self.direct_copy(step, other).start()
            return
        for way in (1, -1):

            @pl.when(self.at.can_pass(way))
            def _(way=way):
                self.line_copy(self.at.f, way, other, own=not other).start()

    def start_row(self):
        self.row_copy(self.at.f, own=True).start()

    def start_core(self):
        self.core_copy(self.at.f, 0, own=True).start()
        self.full[aligned(self.at.f * 4 + self.at.c, self.shard), :] = self.own[...]

    def line_step(self, step, other=0):
        def arrive(f, way):
            self.line_copy(f, 1, other).wait_recv()
            if not self.direct:

                @pl.when(self.at.can_pass(way))
                def _():
                    self.line_copy(f, way, other).start()

            self.core_copy(f, other).start()
            if not self.row_first:
                self.row_copy(f).start()

        self.at.each(step, arrive)

    def row_step(self, step):
        def arrive(f, _):
            self.row_copy(f).wait_recv()
            self.core_copy(f, 1).start()
            if self.row_first:
                self.start_line(1)

        self.at.each(step, arrive)

    def finish(self):
        for f in range(self.at.line):
            for other in (0, 1):
                self.core_copy(f, other).wait_recv()

    def drain(self):
        for step in range(1, self.at.line if self.direct else 0):
            for other in range(2 if self.row_first else 1):
                self.direct_copy(step, other).wait_send()
        for step in range(0 if self.direct else self.at.line):
            for way in (1, -1):
                source = self.at.f - step * way
                passed = (source >= 0) & (source < self.at.line) & self.at.can_pass(way)

                @pl.when(passed)
                def _(source=source, way=way):
                    for other in range(2 if self.row_first else 1):
                        self.line_copy(source, way, other).wait_send()

        if self.row_first:
            self.row_copy(self.at.f).wait_send()
        for f in range(self.at.line):
            if not self.row_first:
                self.row_copy(f).wait_send()
            for other in (0, 1):
                self.core_copy(f, other).wait_send()


class Scatter:
    def __init__(self, place, group, shard, sems, core, row, line, line_first=False):
        self.place, self.group, self.shard = place, group, shard
        self.core_send, self.core_recv, self.row_send, self.row_recv, self.line_send, self.line_recv = sems
        self.core, self.row, self.line = core, row, line
        self.row_blocks = 1 if line_first else place.line
        self.line_unit = 2 * shard if line_first else shard

    def core_copies(self):
        full, landed, _ = self.core
        at = self.place
        copies = []
        for f in range(at.line):
            for y in range(2):
                index = f * 2 + y
                copies.append(
                    remote(
                        full.at[aligned(f * 4 + 2 * y + 1 - at.core_bit, self.shard), :],
                        landed.at[pl.ds(index * self.shard, self.shard), :],
                        self.core_send.at[self.group, index],
                        self.core_recv.at[self.group, index],
                        at.core_device,
                    )
                )
        return copies

    def row_copies(self):
        summed, landed, _ = self.row
        at = self.place
        return [
            remote(
                summed.at[aligned(f * 2 + 1 - at.row_bit, self.shard), :],
                landed.at[pl.ds(f * self.shard, self.shard), :],
                self.row_send.at[self.group, f],
                self.row_recv.at[self.group, f],
                at.row_device,
            )
            for f in range(self.row_blocks)
        ]

    def line_copies(self):
        summed, landed, _ = self.line
        at = self.place
        copies = []
        for step in range(1, at.line):
            target = lax.rem(at.f + step, at.line)
            copies.append(
                remote(
                    summed.at[aligned(target, self.line_unit), :],
                    landed.at[pl.ds((step - 1) * self.line_unit, self.line_unit), :],
                    self.line_send.at[self.group, step],
                    self.line_recv.at[self.group, step],
                    at.line_device(target),
                )
            )
        return copies

    def start(self, stage):
        for copy in getattr(self, stage + "_copies")():
            copy.start()

    def core_finish(self):
        full, landed, summed = self.core
        at = self.place
        for index, copy in enumerate(self.core_copies()):
            copy.wait_recv()
            f, y = index // 2, index % 2
            own = full[aligned(f * 4 + 2 * y + at.core_bit, self.shard), :]
            other = landed[index * self.shard : (index + 1) * self.shard, :]
            summed[index * self.shard : (index + 1) * self.shard, :] = (
                own.astype(jnp.float32) + other.astype(jnp.float32)
            ).astype(summed.dtype)

    def row_finish(self):
        summed, landed, result = self.row
        at = self.place
        for f, copy in enumerate(self.row_copies()):
            copy.wait_recv()
            own = summed[aligned(f * 2 + at.row_bit, self.shard), :]
            other = landed[f * self.shard : (f + 1) * self.shard, :]
            result[f * self.shard : (f + 1) * self.shard, :] = (
                own.astype(jnp.float32) + other.astype(jnp.float32)
            ).astype(result.dtype)

    def line_finish(self):
        summed, landed, result = self.line
        at = self.place
        total = summed[aligned(at.f, self.line_unit), :].astype(jnp.float32)
        for step, copy in enumerate(self.line_copies()):
            copy.wait_recv()
            total = total + landed[step * self.line_unit : (step + 1) * self.line_unit, :].astype(jnp.float32)
        result[...] = total.astype(result.dtype)

    def drain(self, *stages):
        for stage in stages:
            for copy in getattr(self, stage + "_copies")():
                copy.wait_send()


def split_heads(source, store, scale):
    rows, width = source.shape
    for pair in range(width // 128):
        both = source[:, pair * 128 : (pair + 1) * 128].astype(jnp.float32) * scale
        head = lax.broadcasted_iota(jnp.int32, both.shape, 1) // HEAD_DIM
        for side in range(2):
            store[pair, side * rows : (side + 1) * rows, :] = jnp.where(
                head == side, both, 0.0
            ).astype(jnp.bfloat16)


def write_mask(r, at, key_slot, half):
    keys = aligned(key_slot, half)
    key_seg = r.seg[:, aligned(key_slot, half, 128)].astype(jnp.float32)
    key_part = jnp.broadcast_to(key_seg, (128, half)).T
    key_full = jnp.concatenate([key_part] * (half // 128), axis=1)
    shape = (half, half)
    key_place = r.order[0, key_slot] * half + lax.broadcasted_iota(jnp.int32, shape, 0)
    for part in range(2):
        query_slot = at.c * 2 + part
        query_seg = r.seg[:, aligned(query_slot, half, 128)].astype(jnp.float32)
        query_place = r.order[0, query_slot] * half + lax.broadcasted_iota(jnp.int32, shape, 1)
        allowed = (key_full == query_seg) & (key_place <= query_place)
        r.mask[keys, part * half : (part + 1) * half] = jnp.where(allowed, 0.0, NEGATIVE)


def attend_tile(r, slot, half, rows, width):
    keys = aligned(slot, half)
    mask = r.mask[keys, :]
    mask = jnp.concatenate([mask, mask], axis=1)
    for pair in range(width // 128):
        span = slice(pair * 128, (pair + 1) * 128)
        scores = dot_nt(r.kv[keys, span], r.heads[pair]) + mask
        before = r.top[pair : pair + 1, :]
        after = jnp.maximum(before, jnp.max(scores, axis=0, keepdims=True))
        raised = jnp.exp(scores - after)
        fade = jnp.exp(before - after)
        r.top[pair : pair + 1, :] = after
        r.total[pair : pair + 1, :] = r.total[pair : pair + 1, :] * fade + jnp.sum(
            raised, axis=0, keepdims=True
        )
        value = r.kv[keys, width + pair * 128 : width + (pair + 1) * 128].T
        step = dot_nn(value, raised.astype(jnp.bfloat16))
        for side in range(2):
            spot = slice((2 * pair + side) * HEAD_DIM, (2 * pair + side + 1) * HEAD_DIM)
            columns = slice(side * rows, (side + 1) * rows)
            r.mixed[spot, :] = (
                r.mixed[spot, :] * fade[:, columns]
                + step[side * HEAD_DIM : (side + 1) * HEAD_DIM, columns]
            )


def attend_finish(r, rows, width):
    for pair in range(width // 128):
        for side in range(2):
            spot = slice((2 * pair + side) * HEAD_DIM, (2 * pair + side + 1) * HEAD_DIM)
            columns = slice(side * rows, (side + 1) * rows)
            r.mixed[spot, :] = r.mixed[spot, :] / r.total[pair : pair + 1, columns]
        span = slice(pair * 128, (pair + 1) * 128)
        r.att[:, span] = r.mixed[span, :].T.astype(jnp.bfloat16)
    r.top[...] = r.top[...] + jnp.log(r.total[...])


def back_begin(r, rows, width):
    split_heads(r.att_slope, r.slopes, 1.0)
    for pair in range(width // 128):
        span = slice(pair * 128, (pair + 1) * 128)
        product = r.att_slope[:, span].astype(jnp.float32).T * r.mixed[span, :]
        for side in range(2):
            r.pull[pair : pair + 1, side * rows : (side + 1) * rows] = jnp.sum(
                product[side * HEAD_DIM : (side + 1) * HEAD_DIM, :], axis=0, keepdims=True
            )
    r.dq_sum[...] = jnp.zeros_like(r.dq_sum)


def back_tile(r, slot, target, half, rows, width):
    keys = aligned(slot, half)
    mask = r.mask[keys, :]
    mask = jnp.concatenate([mask, mask], axis=1)
    for pair in range(width // 128):
        span = slice(pair * 128, (pair + 1) * 128)
        value_span = slice(width + pair * 128, width + (pair + 1) * 128)
        key = r.kv[keys, span]
        scores = dot_nt(key, r.heads[pair]) + mask
        chance = jnp.exp(scores - r.top[pair : pair + 1, :])
        pulled = dot_nt(r.kv[keys, value_span], r.slopes[pair])
        slope = (chance * (pulled - r.pull[pair : pair + 1, :])).astype(jnp.bfloat16)
        target[:, value_span] = dot_nn(chance.astype(jnp.bfloat16), r.slopes[pair]).astype(
            jnp.bfloat16
        )
        target[:, span] = dot_nn(slope, r.heads[pair]).astype(jnp.bfloat16)
        step = dot_nn(key.T, slope)
        for side in range(2):
            spot = slice((2 * pair + side) * HEAD_DIM, (2 * pair + side + 1) * HEAD_DIM)
            r.dq_sum[spot, :] += step[
                side * HEAD_DIM : (side + 1) * HEAD_DIM, side * rows : (side + 1) * rows
            ]


def gelu_both(v):
    square = v * v
    inner = GELU_A * v * (1.0 + GELU_B * square)
    bent = jnp.tanh(inner)
    lifted = 0.5 * (1.0 + bent)
    slope = lifted + 0.5 * v * (1.0 - bent * bent) * (GELU_A * (1.0 + 3.0 * GELU_B * square))
    return (v * lifted, slope)


def wide(ref, these):
    return ref[these, :].astype(jnp.float32)


def layer_kernel(line, r):
    at = Place(line)
    shard = r.pv_own.shape[0]
    rows, model = r.x.shape
    width = r.att.shape[1]
    hidden = r.we.shape[1]
    half, some = rows // 2, rows // PIECES
    low = jnp.bfloat16
    gather_sems = (r.g_line_s, r.g_line_r, r.g_row_s, r.g_row_r, r.g_core_s, r.g_core_r)
    scatter_sems = (r.s_core_s, r.s_core_r, r.s_row_s, r.s_row_r, r.s_line_s, r.s_line_r)
    project_in = Gather(at, 0, r.pv_own, r.pv, False, False, gather_sems)
    output_in = Gather(at, 1, r.wo_own, r.wo, False, False, gather_sems)
    expand_in = Gather(at, 2, r.we_own, r.we, False, True, gather_sems)
    shrink_in = Gather(at, 3, r.ws_own, r.ws, True, True, gather_sems)

    gs, ge = r.ws, r.we
    shrink = Scatter(
        at, 0, shard, scatter_sems, (gs, r.gs1, r.gs2), (r.gs4, r.gs5, r.gs_out), (r.gs2, r.gs3, r.gs4), True
    )
    expand = Scatter(
        at, 1, shard, scatter_sems, (ge, r.ge1, r.ge2), (r.ge2, r.ge3, r.ge4), (r.ge4, r.ge5, r.ge_out)
    )
    output = Scatter(
        at, 2, shard, scatter_sems, (r.go, r.go1, r.go2), (r.go2, r.go3, r.go4), (r.go4, r.go5, r.go_out)
    )
    project = []
    for index in range(3):
        span = slice(index * width, (index + 1) * width)
        landed1, summed1, landed2, summed2, landed3 = [r["gp%d%d" % (index, stage)] for stage in range(1, 6)]
        project.append(
            Scatter(
                at,
                3 + index,
                shard,
                scatter_sems,
                (r.ws.at[:, span], landed1, summed1),
                (summed1, landed2, summed2),
                (summed2, landed3, r.gp_out.at[:, span]),
            )
        )
    vector = Scatter(
        at, 6, shard, scatter_sems, (r.gv, r.gv1, r.gv2), (r.gv2, r.gv3, r.gv4), (r.gv4, r.gv5, r.gv_out)
    )

    def kv_row(part):
        here = r.kv.at[aligned(at.c * 2 + part, half), :]
        return remote(here, here, r.kv_s.at[0, part], r.kv_r.at[0, part], at.row_device)

    def kv_core(part, other):
        here = r.kv.at[aligned((at.row if other else at.c) * 2 + part, half), :]
        return remote(
            here, here, r.kv_s.at[1 + other, part], r.kv_r.at[1 + other, part], at.core_device
        )

    def tp_copy(kind, piece):
        source, target = (
            (r.att, r.att_land),
            (r.up_send, r.up_land),
            (r.feed, r.feed_land),
            (r.down_send, r.down_land),
        )[kind]
        these = aligned(piece, some)
        return remote(
            source.at[these, :],
            target.at[these, :],
            r.tp_s.at[kind, piece],
            r.tp_r.at[kind, piece],
            at.tp_device,
        )

    wo_copy = remote(r.wo, r.wo_land, r.wo_s.at[0], r.wo_r.at[0], at.tp_device)

    def slopes_of(ctx, part):
        return r.hidden.at[aligned(ctx, half), part * 2 * width : (part + 1) * 2 * width]

    def back_core(far, part):
        return remote(
            slopes_of(at.other if far else at.core, part),
            r.kv_land.at[pl.ds((2 * far + part) * half, half), :],
            r.bk_s.at[far, part],
            r.bk_r.at[far, part],
            at.core_device,
        )

    def back_row(part):
        these = pl.ds(part * half, half)
        return remote(
            r.kv_pass.at[these, :],
            r.kv_land2.at[these, :],
            r.bk_s.at[2, part],
            r.bk_r.at[2, part],
            at.row_device,
        )

    active = r.hidden.at[0:rows, :]
    before_slope = r.hidden.at[rows : 2 * rows, :]

    r.turn[...] = jnp.zeros_like(r.turn)
    for index, ref in enumerate((r.gain1, r.shift1, r.bias_o, r.gain2, r.shift2, r.bias_s)):
        r.turn[index : index + 1, 0:shard] = ref[...].astype(jnp.float32)[None, :]
    for index in range(3):
        r.pv_own[:, index * width : (index + 1) * width] = r.wp[index]
    r.pv_own[:, 3 * width :] = r.turn[...].T[0:shard, :].astype(low)
    r.ebias[...] = r.ebias_own[...].astype(jnp.float32)[None, :]
    at.greet()
    for weight in (project_in, output_in):
        weight.start_line()
        weight.start_row()
        weight.start_core()

    @pl.loop(0, PIECES)
    def _(piece):
        these = aligned(piece, some)
        r.delta[these, :] = normalize_parts(wide(r.x, these))[0]

    for step in range(1, line):
        project_in.line_step(step)
        output_in.line_step(step)
        if step == line - 2:
            expand_in.start_line()
            shrink_in.start_line()
        project_in.row_step(step - 1)

        if step < line - 1:
            for slot in range(4 * step - 4, min(4 * step, 8)):
                write_mask(r, at, slot, half)
    shrink_in.start_row()
    shrink_in.start_core()
    expand_in.start_row()
    expand_in.start_core()
    project_in.row_step(line - 1)
    project_in.finish()
    r.vec[...] = r.pv[:, 3 * width :].astype(jnp.float32).T[0:8, :]
    gain, shift = r.vec[0:1, :], r.vec[1:2, :]

    @pl.loop(0, PIECES)
    def _(piece):
        these = aligned(piece, some)
        r.normed[these, :] = (r.delta[these, :] * gain + shift).astype(low)

    bias = r.pbias[...].astype(jnp.float32)
    for part in range(2):
        left = r.normed[part * half : (part + 1) * half, :]
        here = aligned(at.c * 2 + part, half)
        r.kv[here, 0:width] = dot_nn(left, r.pv[:, width : 2 * width]).astype(low)
        r.kv[here, width:] = (dot_nn(left, r.pv[:, 2 * width : 3 * width]) + bias[1:2, :]).astype(low)
        kv_row(part).start()
        kv_core(part, 0).start()
    shrink_in.row_step(0)
    r.att[...] = (dot_nn(r.normed[...], r.pv[:, 0:width]) + bias[0:1, :]).astype(low)
    split_heads(r.att, r.heads, SCALE)
    r.top[...] = jnp.full_like(r.top, NEGATIVE)
    r.total[...] = jnp.zeros_like(r.total)
    r.mixed[...] = jnp.zeros_like(r.mixed)
    for step in range(line):
        output_in.row_step(step)
    output_in.finish()
    wo_copy.start()

    @pl.loop(0, 8)
    def _(tile):
        @pl.when(tile == 2)
        def _():
            for part in range(2):
                kv_core(part, 0).wait_recv()

        for step in range(1, line):

            @pl.when(tile == step)
            def _(step=step):
                expand_in.line_step(step)

        for part in range(2):

            @pl.when(tile == 4 + 2 * part)
            def _(part=part):
                kv_row(part).wait_recv()
                kv_core(part, 1).start()

            @pl.when(tile == 5 + 2 * part)
            def _(part=part):
                kv_core(part, 1).wait_recv()

        far = jnp.where(lax.rem(tile, 2) == 0, at.row, at.other)
        ctx = jnp.where(tile < 2, at.c, jnp.where(tile < 4, at.core, far))
        part = jnp.where(tile < 4, lax.rem(tile, 2), (tile - 4) // 2)
        attend_tile(r, ctx * 2 + part, half, rows, width)

    attend_finish(r, rows, width)
    for piece in range(PIECES):
        tp_copy(0, piece).start()
    expand_in.row_step(0)
    for step in range(1, line):
        shrink_in.line_step(step, 0)
        expand_in.row_step(step)
        shrink_in.line_step(step, 1)
    shrink_in.finish()
    expand_in.finish()
    wo_copy.wait_recv()
    out_bias, gain2, shift2 = r.vec[2:3, :], r.vec[3:4, :], r.vec[4:5, :]

    @pl.loop(0, PIECES)
    def _(piece):
        these = aligned(piece, some)
        tp_copy(0, piece).wait_recv()
        branch = dot_nt(r.att[these, :], r.wo[...]) + dot_nt(r.att_land[these, :], r.wo_land[...])
        middle = wide(r.x, these) + branch + out_bias
        r.mid[these, :] = middle
        unit, _ = normalize_parts(middle)
        normed = (unit * gain2 + shift2).astype(low)
        r.normed2[these, :] = normed
        for column in range(0, hidden, 512):
            span = slice(column, column + 512)
            value, slope = gelu_both(dot_nn(normed, r.we[:, span]) + r.ebias[:, span])
            active[these, span] = value.astype(low)
            before_slope[these, span] = (dot_nn(r.ct[these, :], r.ws[:, span]) * slope).astype(low)
        r.up_send[these, :] = dot_nt(before_slope[these, :], r.we[...]).astype(low)
        tp_copy(1, piece).start()

    @pl.loop(0, PIECES)
    def _(piece):
        these = aligned(piece, some)
        r.feed[these, :] = dot_nt(active[these, :], r.ws[...]).astype(low)
        tp_copy(2, piece).start()

    for weight in (shrink_in, expand_in):
        weight.drain()
    r.turned[...] = r.ct[...].T
    for column in range(0, hidden, 512):
        span = slice(column, column + 512)
        gs[:, span] = dot_nn(r.turned[...], active[:, span]).astype(low)
    shrink.start("core")
    r.turned[...] = r.normed2[...].T
    for column in range(0, hidden, 512):
        span = slice(column, column + 512)
        ge[:, span] = dot_nn(r.turned[...], before_slope[:, span]).astype(low)
    expand.start("core")
    shrink.core_finish()
    shrink.start("line")
    r.bsum[...] = jnp.sum(before_slope[...].astype(jnp.float32), axis=0, keepdims=True)
    expand.core_finish()
    expand.start("row")
    r.vsum[...] = jnp.zeros_like(r.vsum)

    @pl.loop(0, PIECES)
    def _(piece):
        these = aligned(piece, some)
        tp_copy(1, piece).wait_recv()
        upstream = wide(r.up_send, these) + wide(r.up_land, these)
        unit, inverse = normalize_parts(r.mid[these, :])
        back, gain_delta, shift_delta = norm_backward(upstream, unit, inverse, gain2)
        slope = wide(r.ct, these)
        middle_slope = slope + back
        r.mids[these, :] = middle_slope
        r.vsum[2:3, :] += jnp.sum(middle_slope, axis=0, keepdims=True)
        r.vsum[3:4, :] += gain_delta[None]
        r.vsum[4:5, :] += shift_delta[None]
        r.vsum[5:6, :] += jnp.sum(slope, axis=0, keepdims=True)
        rounded = middle_slope.astype(low)
        r.normed2[these, :] = rounded
        r.att_slope[these, :] = dot_nn(rounded, r.wo[...]).astype(low)

    back_begin(r, rows, width)
    r.turned[...] = r.normed2[...].T
    r.go[...] = dot_nn(r.turned[...], r.att[...]).astype(low)
    output.start("core")

    @pl.loop(0, 8)
    def _(tile):
        pair = tile // 2
        ctx = jnp.where(
            pair < 2, jnp.where(pair == 0, at.other, at.row), jnp.where(pair == 2, at.core, at.c)
        )
        part = lax.rem(tile, 2)
        back_tile(r, ctx * 2 + part, r.tile, half, rows, width)
        for index in range(2):

            @pl.when(part == index)
            def _(index=index):
                slopes_of(ctx, index)[...] = r.tile[...]

        for index in range(2):

            @pl.when(tile == index)
            def _(index=index):
                back_core(1, index).start()

            @pl.when(tile == 2 + index)
            def _(index=index):
                back_core(1, index).wait_recv()
                landed = r.kv_land[(2 + index) * half : (3 + index) * half, :]
                r.kv_pass[index * half : (index + 1) * half, :] = (
                    r.tile[...].astype(jnp.float32) + landed.astype(jnp.float32)
                ).astype(low)
                back_row(index).start()

            @pl.when(tile == 4 + index)
            def _(index=index):
                back_core(0, index).start()

        @pl.when(tile == 1)
        def _():
            output.core_finish()
            output.start("row")

        @pl.when(tile == 6)
        def _():
            expand.row_finish()
            expand.start("line")

        @pl.when(tile == 7)
        def _():
            output.row_finish()
            output.start("line")

    for pair in range(width // 128):
        span = slice(pair * 128, (pair + 1) * 128)
        r.dq[:, span] = (r.dq_sum[span, :] * SCALE).T.astype(low)

    @pl.loop(0, PIECES)
    def _(piece):
        these = aligned(piece, some)
        r.delta[these, :] = dot_nt(r.dq[these, :], r.pv[:, 0:width])

    shrink.drain("core")
    r.turned[...] = r.normed[...].T
    r.ws[:, 0:width] = dot_nn(r.turned[...], r.dq[...]).astype(low)
    project[0].start("core")
    shrink.line_finish()
    shrink.start("row")
    shrink_bias = r.vec[5:6, :]

    @pl.loop(0, PIECES)
    def _(piece):
        these = aligned(piece, some)
        tp_copy(2, piece).wait_recv()
        feed = (wide(r.feed, these) + wide(r.feed_land, these)).astype(low)
        r.out[these, :] = (r.mid[these, :] + feed.astype(jnp.float32) + shrink_bias).astype(low)

    project[0].core_finish()
    project[0].start("row")
    for part in range(2):
        back_core(0, part).wait_recv()
        back_row(part).wait_recv()
        these = slice(part * half, (part + 1) * half)
        total = slopes_of(at.c, part)[...].astype(jnp.float32)
        total = total + wide(r.kv_land, slice(part * half, (part + 1) * half))
        total = total + wide(r.kv_land2, these)
        r.kv_low[these, :] = total.astype(low)
        for step in range(PIECES // 2):
            piece = part * (PIECES // 2) + step
            these = slice(piece * some, (piece + 1) * some)
            r.down_send[these, :] = (
                r.delta[these, :] + dot_nt(r.kv_low[these, :], r.pv[:, width : 3 * width])
            ).astype(low)
            tp_copy(3, piece).start()
    for piece in range(2):
        span = slice((1 + piece) * width, (2 + piece) * width)
        slopes = r.kv_low[:, piece * width : (piece + 1) * width]
        r.ws[:, span] = dot_nn(r.turned[...], slopes).astype(low)
        project[1 + piece].start("core")
    bias_row = jnp.concatenate(
        [
            r.bsum[...],
            jnp.sum(r.dq[...].astype(jnp.float32), axis=0, keepdims=True),
            jnp.sum(r.kv_low[:, width:].astype(jnp.float32), axis=0, keepdims=True),
        ],
        axis=1,
    )
    r.bias_pack[...] = jnp.zeros_like(r.bias_pack)
    for index in range(bias_row.shape[1] // 128):
        r.bias_pack[0, index : index + 1, :] = bias_row[:, index * 128 : (index + 1) * 128]

    def bias_copy(stage):
        device = (at.core_device, at.row_device)[stage]
        return remote(
            r.bias_pack.at[stage], r.bias_land.at[stage], r.b_s.at[0, stage], r.b_r.at[0, stage], device
        )

    def bias_line_copy(step):
        target = lax.rem(at.f + step, line)
        return remote(
            r.bias_pack.at[2],
            r.bias_line.at[at.f],
            r.b_s.at[1, step],
            r.b_r.at[1, step],
            at.line_device(target),
        )

    bias_copy(0).start()
    for piece in (1, 2):
        project[piece].core_finish()
        project[piece].start("row")
    bias_copy(0).wait_recv()
    r.bias_pack[1, :, :] = r.bias_pack[0, :, :] + r.bias_land[0, :, :]
    bias_copy(1).start()
    project[0].row_finish()
    project[0].start("line")
    shrink.row_finish()
    expand.line_finish()
    bias_copy(1).wait_recv()
    r.bias_pack[2, :, :] = r.bias_pack[1, :, :] + r.bias_land[1, :, :]
    for step in range(1, line):
        bias_line_copy(step).start()
    output.line_finish()
    project[1].row_finish()
    project[1].start("line")
    r.turn_wide[...] = jnp.zeros_like(r.turn_wide)
    r.turn_wide[0:8, :] = r.vsum[...]

    @pl.loop(0, PIECES)
    def _(piece):
        these = aligned(piece, some)
        tp_copy(3, piece).wait_recv()
        upstream = wide(r.down_send, these) + wide(r.down_land, these)
        unit, inverse = normalize_parts(wide(r.x, these))
        slope, gain_delta, shift_delta = norm_backward(upstream, unit, inverse, gain)
        r.delta[these, :] = r.mids[these, :] + slope
        r.turn_wide[0:1, :] += gain_delta[None]
        r.turn_wide[1:2, :] += shift_delta[None]

    r.gv[...] = r.turn_wide[...].T.astype(low)
    vector.start("core")
    project[2].row_finish()
    project[2].start("line")
    vector.core_finish()
    vector.start("row")
    vector.row_finish()
    vector.start("line")
    for step in range(1, line):
        source = lax.rem(at.f + line - step, line)
        remote(
            r.bias_pack.at[2], r.bias_line.at[source], r.b_s.at[1, step], r.b_r.at[1, step], at.row_device
        ).wait_recv()
    r.bias_line[at.f, :, :] = r.bias_pack[2, :, :]
    total = r.bias_line[0, :, :]
    for f in range(1, line):
        total = total + r.bias_line[f, :, :]
    r.bias_out[...] = total
    for piece in project:
        piece.line_finish()
    vector.line_finish()
    project_in.drain()
    output_in.drain()
    wo_copy.wait_send()
    for part in range(2):
        kv_row(part).wait_send()
        back_row(part).wait_send()
        for index in range(2):
            kv_core(part, index).wait_send()
            back_core(index, part).wait_send()
    for kind in range(4):
        for piece in range(PIECES):
            tp_copy(kind, piece).wait_send()
    for stage in range(2):
        bias_copy(stage).wait_send()
    for step in range(1, line):
        bias_line_copy(step).wait_send()
    shrink.drain("row", "line")
    for gradient in (expand, output, *project, vector):
        gradient.drain("core", "row", "line")


def finish_kernel(r):
    r.out_end[0] = r.out[...]
    r.delta_end[0] = r.delta[...]
    r.gs_end[...] = r.gs[...]
    r.ge_end[...] = r.ge[...]
    r.go_end[...] = r.go[...]
    width = r.go.shape[1]
    for index in range(3):
        r.gp_end[index] = r.gp[:, index * width : (index + 1) * width]
    vectors = r.gv[...].T
    shard = r.gv.shape[0]
    for index in range(6):
        r["gv%d" % index][...] = vectors[index, 0:shard]
    hidden = r.ebias.shape[0]
    for index in range(hidden // 128):
        r.ebias[pl.ds(index * 128, 128)] = r.biases[index, :]
    each = width // 128
    for index in range(2 * each):
        row, column = index // each, index % each
        place = hidden // 128 + index
        r.pbias[row : row + 1, column * 128 : (column + 1) * 128] = r.biases[place : place + 1, :]


class Refs(dict):
    __getattr__ = dict.__getitem__


def call(kernel, ins, outs, scratch, smem=(), identity=None):
    names = [*ins, *outs, *scratch]
    params = dict(vmem_limit_bytes=VMEM_BYTES)
    if identity is not None:
        params.update(collective_id=identity, has_side_effects=True)
    results = pl.pallas_call(
        lambda *refs: kernel(Refs(zip(names, refs))),
        out_shape=[jax.ShapeDtypeStruct(shape, dtype) for shape, dtype in outs.values()],
        in_specs=[
            pl.BlockSpec(memory_space=pltpu.SMEM if name in smem else pltpu.VMEM) for name in ins
        ],
        out_specs=[pl.BlockSpec(memory_space=pltpu.VMEM)] * len(outs),
        scratch_shapes=[
            pltpu.VMEM(*spec) if isinstance(spec, tuple) else spec for spec in scratch.values()
        ],
        compiler_params=pltpu.CompilerParams(**params),
    )(*ins.values())
    return Refs(zip(outs, results))


def by_kernels(
    layer_input,
    cotangent,
    segments,
    slot_order,
    first_gain,
    first_shift,
    project_weight,
    project_bias,
    output_weight,
    output_bias,
    second_gain,
    second_shift,
    expand_weight,
    expand_bias,
    shrink_weight,
    shrink_bias,
):
    low, full = jnp.bfloat16, jnp.float32
    line = lax.axis_size("fsdp")
    _, rows, model = layer_input.shape
    length = segments.shape[1]
    shard, _, width = project_weight.shape
    hidden = expand_weight.shape[1]
    pairs = width // 128
    half = rows // 2
    packed = 3 * width + 128
    two, one = 2 * line * shard, line * shard
    less = one - shard
    bias_rows = -(-(hidden + 2 * width) // 1024) * 8
    dma = lambda *shape: pltpu.SemaphoreType.DMA(shape)

    def stages(name, columns, sizes=(two, two, one, one, less)):
        return {"%s%d" % (name, index + 1): ((size, columns), low) for index, size in enumerate(sizes)}

    done = call(
        partial(layer_kernel, line),
        dict(
            x=layer_input.reshape(rows, model),
            ct=cotangent.reshape(rows, model),
            seg=segments,
            order=slot_order,
            gain1=first_gain,
            shift1=first_shift,
            bias_o=output_bias,
            gain2=second_gain,
            shift2=second_shift,
            bias_s=shrink_bias,
            wp=project_weight.transpose(1, 0, 2),
            pbias=project_bias,
            wo_own=output_weight.T,
            we_own=expand_weight,
            ws_own=shrink_weight.T,
            ebias_own=expand_bias,
        ),
        dict(
            out=((rows, model), low),
            delta=((rows, model), full),
            gs_out=((shard, hidden), full),
            ge_out=((shard, hidden), full),
            go_out=((shard, width), full),
            gp_out=((shard, 3 * width), full),
            gv_out=((shard, 128), full),
            bias_out=((bias_rows, 128), full),
        ),
        dict(
            pv_own=((shard, packed), low),
            pv=((model, packed), low),
            wo=((model, width), low),
            we=((model, hidden), low),
            ws=((model, hidden), low),
            kv=((length, 2 * width), low),
            vec=((8, model), full),
            ebias=((1, hidden), full),
            turn=((128, 128), full),
            turn_wide=((128, model), full),
            normed=((rows, model), low),
            normed2=((rows, model), low),
            turned=((model, rows), low),
            mask=((length, rows), full),
            heads=((pairs, 2 * rows, 128), low),
            slopes=((pairs, 2 * rows, 128), low),
            top=((8, 2 * rows), full),
            total=((8, 2 * rows), full),
            pull=((8, 2 * rows), full),
            mixed=((width, rows), full),
            dq_sum=((width, rows), full),
            att=((rows, width), low),
            att_slope=((rows, width), low),
            dq=((rows, width), low),
            tile=((half, 2 * width), low),
            mid=((rows, model), full),
            mids=((rows, model), full),
            hidden=((2 * rows, hidden), low),
            att_land=((rows, width), low),
            wo_land=((model, width), low),
            up_send=((rows, model), low),
            up_land=((rows, model), low),
            feed=((rows, model), low),
            feed_land=((rows, model), low),
            down_send=((rows, model), low),
            down_land=((rows, model), low),
            kv_land=((2 * rows, 2 * width), low),
            kv_pass=((rows, 2 * width), low),
            kv_land2=((rows, 2 * width), low),
            kv_low=((rows, 2 * width), low),
            bsum=((1, hidden), full),
            vsum=((8, model), full),
            go=((model, width), low),
            gv=((model, 128), low),
            **stages("gs", hidden, (two, two, 2 * less, 2 * shard, shard)),
            **stages("ge", hidden),
            **stages("go", width),
            **stages("gp0", width),
            **stages("gp1", width),
            **stages("gp2", width),
            **stages("gv", 128),
            bias_pack=((3, bias_rows, 128), full),
            bias_land=((2, bias_rows, 128), full),
            bias_line=((line, bias_rows, 128), full),
            g_line_s=dma(4, 2, 2, line),
            g_line_r=dma(4, 2, line),
            g_row_s=dma(4, line),
            g_row_r=dma(4, line),
            g_core_s=dma(4, 2, line),
            g_core_r=dma(4, 2, line),
            s_core_s=dma(7, 2 * line),
            s_core_r=dma(7, 2 * line),
            s_row_s=dma(7, line),
            s_row_r=dma(7, line),
            s_line_s=dma(7, line),
            s_line_r=dma(7, line),
            wo_s=dma(1),
            wo_r=dma(1),
            kv_s=dma(3, 2),
            kv_r=dma(3, 2),
            tp_s=dma(4, PIECES),
            tp_r=dma(4, PIECES),
            bk_s=dma(3, 2),
            bk_r=dma(3, 2),
            b_s=dma(2, line),
            b_r=dma(2, line),
        ),
        smem=("order",),
        identity=0,
    )
    end = call(
        finish_kernel,
        dict(
            out=done.out,
            delta=done.delta,
            gs=done.gs_out,
            ge=done.ge_out,
            go=done.go_out,
            gp=done.gp_out,
            gv=done.gv_out,
            biases=done.bias_out,
        ),
        dict(
            out_end=(layer_input.shape, low),
            delta_end=(layer_input.shape, full),
            gs_end=((shard, hidden), full),
            ge_end=((shard, hidden), full),
            go_end=((shard, width), full),
            gp_end=((3, shard, width), full),
            **{"gv%d" % index: ((shard,), full) for index in range(6)},
            ebias=((hidden,), full),
            pbias=((2, width), full),
        ),
        {},
    )
    return (
        end.out_end,
        end.delta_end,
        end.gv0,
        end.gv1,
        end.gp_end.transpose(1, 0, 2),
        end.pbias,
        end.go_end.T,
        end.gv2,
        end.gv3,
        end.gv4,
        end.ge_end,
        end.ebias,
        end.gs_end.T,
        end.gv5,
    )


def solution(mesh):
    n_ctx, n_tp = mesh.shape["ctx"], mesh.shape["tp"]

    def choose(layer_input, *others):
        seqs, rows, model = layer_input.shape
        whole_tiles = model % (16 * n_ctx * mesh.shape["fsdp"]) == 0 and rows % 256 == 0
        if seqs == 1 and n_ctx == 4 and n_tp == 2 and whole_tiles:
            return by_kernels(layer_input, *others)
        return on_device(layer_input, *others)

    return jax.shard_map(
        choose,
        mesh=mesh,
        in_specs=(
            P("fsdp", "ctx", None),
            P("fsdp", "ctx", None),
            P("fsdp", None),
            P("fsdp", None),
            P(("fsdp", "ctx")),
            P(("fsdp", "ctx")),
            P(("fsdp", "ctx"), None, "tp"),
            P(None, "tp"),
            P("tp", ("fsdp", "ctx")),
            P(("fsdp", "ctx")),
            P(("fsdp", "ctx")),
            P(("fsdp", "ctx")),
            P(("fsdp", "ctx"), "tp"),
            P("tp"),
            P("tp", ("fsdp", "ctx")),
            P(("fsdp", "ctx")),
        ),
        out_specs=(
            P("fsdp", "ctx", None),
            P("fsdp", "ctx", None),
            P(("fsdp", "ctx")),
            P(("fsdp", "ctx")),
            P(("fsdp", "ctx"), None, "tp"),
            P(None, "tp"),
            P("tp", ("fsdp", "ctx")),
            P(("fsdp", "ctx")),
            P(("fsdp", "ctx")),
            P(("fsdp", "ctx")),
            P(("fsdp", "ctx"), "tp"),
            P("tp"),
            P("tp", ("fsdp", "ctx")),
            P(("fsdp", "ctx")),
        ),
        check_vma=False,
    )
```

```python
from functools import partial

import jax
import jax.numpy as jnp
from jax import lax
from jax.experimental import pallas as pl
from jax.experimental.pallas import tpu as pltpu
from jax.sharding import PartitionSpec as P

HEAD_DIM = 64


EPSILON = 1e-05
SCALE = 0.125
NEGATIVE = -1000000000.0
TILE = 512
GELU_A = 0.7978845608028654
GELU_B = 0.044715


def contract_rows(left, right):
    return lax.dot_general(
        left, right, (((0,), (0,)), ((), ())), preferred_element_type=jnp.float32
    )


def times_transpose(left, right):
    return lax.dot_general(
        left, right, (((1,), (1,)), ((), ())), preferred_element_type=jnp.float32
    )


def normalize_parts(rows):
    mean = jnp.mean(rows, axis=-1, keepdims=True)
    centred = rows - mean
    spread = jnp.mean(centred * centred, axis=-1, keepdims=True)
    inverse = lax.rsqrt(spread + EPSILON)
    return (centred * inverse, inverse)


def norm_backward(upstream, unit, inverse, gain):
    scaled = upstream * gain
    back = inverse * (
        scaled
        - jnp.mean(scaled, axis=-1, keepdims=True)
        - unit * jnp.mean(scaled * unit, axis=-1, keepdims=True)
    )
    return (back, jnp.sum(upstream * unit, axis=0), jnp.sum(upstream, axis=0))


def split_pairs(array, pairs):
    seqs, count, width = array.shape
    span = width // pairs
    return (
        array.reshape(seqs, count, pairs, span)
        .transpose(0, 2, 1, 3)
        .reshape(seqs * pairs, count, span)
    )


def join_pairs(array, seqs):
    items, count, span = array.shape
    pairs = items // seqs
    return (
        array.reshape(seqs, pairs, count, span)
        .transpose(0, 2, 1, 3)
        .reshape(seqs, count, pairs * span)
    )


def masked_scores(query_heads, key_heads, query_place, query_group, key_place, key_group):
    scores = (
        jnp.einsum("qhd,khd->hqk", query_heads, key_heads, preferred_element_type=jnp.float32)
        * SCALE
    )
    allowed = (query_group[:, None] == key_group[None, :]) & (
        key_place[None, :] <= query_place[:, None]
    )
    return jnp.where(allowed[None], scores, NEGATIVE)


def attend_forward(
    queries, keys_all, values_all, query_places, query_groups, key_places, key_groups, pairs
):
    seqs, rows, width = queries.shape
    length = keys_all.shape[1]
    span = width // pairs
    tile = min(TILE, rows)

    def one_item(item):
        query_part, key_part, value_part, index = item
        which = index // pairs
        query_place = lax.dynamic_index_in_dim(query_places, which, 0, keepdims=False)
        query_group = lax.dynamic_index_in_dim(query_groups, which, 0, keepdims=False)
        key_place = lax.dynamic_index_in_dim(key_places, which, 0, keepdims=False)
        key_group = lax.dynamic_index_in_dim(key_groups, which, 0, keepdims=False)
        key_heads = key_part.reshape(length, 2, span // 2)
        value_heads = value_part.reshape(length, 2, span // 2)
        results, tops, totals = ([], [], [])
        query_heads = query_part.reshape(tile, 2, span // 2)
        scores = masked_scores(
            query_heads, key_heads, query_place, query_group, key_place, key_group
        )
        top = jnp.max(scores, axis=-1)
        raised = jnp.exp(scores - top[..., None])
        total = jnp.sum(raised, axis=-1)
        chance = (raised / total[..., None]).astype(jnp.bfloat16)
        mixed = jnp.einsum("hqk,khd->qhd", chance, value_heads, preferred_element_type=jnp.float32)
        results.append(mixed.reshape(tile, span).astype(jnp.bfloat16))
        tops.append(top)
        totals.append(total)
        return (
            jnp.concatenate(results, axis=0),
            jnp.concatenate(tops, axis=1),
            jnp.concatenate(totals, axis=1),
        )

    items = (
        split_pairs(queries, pairs),
        split_pairs(keys_all, pairs),
        split_pairs(values_all, pairs),
        jnp.arange(seqs * pairs, dtype=jnp.int32),
    )
    mixed, tops, totals = lax.map(one_item, items)
    return (join_pairs(mixed, seqs), tops, totals)


def attend_backward(
    queries,
    keys_all,
    values_all,
    attended_slope,
    tops,
    totals,
    query_places,
    query_groups,
    key_places,
    key_groups,
    pairs,
):
    seqs, rows, width = queries.shape
    length = keys_all.shape[1]
    span = width // pairs
    tile = min(TILE, rows)

    def one_item(item):
        query_part, key_part, value_part, slope_part, top, total, index = item
        which = index // pairs
        query_place = lax.dynamic_index_in_dim(query_places, which, 0, keepdims=False)
        query_group = lax.dynamic_index_in_dim(query_groups, which, 0, keepdims=False)
        key_place = lax.dynamic_index_in_dim(key_places, which, 0, keepdims=False)
        key_group = lax.dynamic_index_in_dim(key_groups, which, 0, keepdims=False)
        key_heads = key_part.reshape(length, 2, span // 2)
        value_heads = value_part.reshape(length, 2, span // 2)
        key_total = jnp.zeros((length, 2, span // 2), jnp.float32)
        value_total = jnp.zeros((length, 2, span // 2), jnp.float32)
        query_heads = query_part.reshape(tile, 2, span // 2)
        slope_heads = slope_part.reshape(tile, 2, span // 2)
        scores = masked_scores(
            query_heads, key_heads, query_place, query_group, key_place, key_group
        )
        chance = jnp.exp(scores - top[:, 0:tile, None]) / total[:, 0:tile, None]
        chance_low = chance.astype(jnp.bfloat16)
        value_total = value_total + jnp.einsum(
            "hqk,qhd->khd", chance_low, slope_heads, preferred_element_type=jnp.float32
        )
        pulled = jnp.einsum(
            "qhd,khd->hqk", slope_heads, value_heads, preferred_element_type=jnp.float32
        )
        score_slope = (chance * (pulled - jnp.sum(chance * pulled, axis=-1, keepdims=True))).astype(
            jnp.bfloat16
        )
        query_step = (
            jnp.einsum("hqk,khd->qhd", score_slope, key_heads, preferred_element_type=jnp.float32)
            * SCALE
        )
        query_results = [query_step.reshape(tile, span).astype(jnp.bfloat16)]
        key_total = (
            key_total
            + jnp.einsum(
                "hqk,qhd->khd", score_slope, query_heads, preferred_element_type=jnp.float32
            )
            * SCALE
        )
        return (
            jnp.concatenate(query_results, axis=0),
            key_total.reshape(length, span),
            value_total.reshape(length, span),
        )

    items = (
        split_pairs(queries, pairs),
        split_pairs(keys_all, pairs),
        split_pairs(values_all, pairs),
        split_pairs(attended_slope, pairs),
        tops,
        totals,
        jnp.arange(seqs * pairs, dtype=jnp.int32),
    )
    query_slope, key_part, value_part = lax.map(one_item, items)
    return (join_pairs(query_slope, seqs), join_pairs(key_part, seqs), join_pairs(value_part, seqs))


def on_device(
    layer_input,
    cotangent,
    segments,
    slot_order,
    first_gain,
    first_shift,
    project_weight,
    project_bias,
    output_weight,
    output_bias,
    second_gain,
    second_shift,
    expand_weight,
    expand_bias,
    shrink_weight,
    shrink_bias,
):
    seqs, rows, model_width = layer_input.shape
    count = seqs * rows
    half = rows // 2
    length = rows * lax.axis_size("ctx")
    begin = lax.axis_index("ctx") * rows
    local_width = project_weight.shape[2]
    pairs = local_width // (2 * HEAD_DIM)
    (
        gain_one,
        shift_one,
        project_full,
        output_full,
        out_bias,
        gain_two,
        shift_two,
        expand_full,
        shrink_full,
        shrink_add,
    ) = (
        lax.all_gather(first_gain, ("fsdp", "ctx"), axis=0, tiled=True),
        lax.all_gather(first_shift, ("fsdp", "ctx"), axis=0, tiled=True),
        lax.all_gather(project_weight, ("fsdp", "ctx"), axis=0, tiled=True),
        lax.all_gather(output_weight, ("fsdp", "ctx"), axis=1, tiled=True),
        lax.all_gather(output_bias, ("fsdp", "ctx"), axis=0, tiled=True),
        lax.all_gather(second_gain, ("fsdp", "ctx"), axis=0, tiled=True),
        lax.all_gather(second_shift, ("fsdp", "ctx"), axis=0, tiled=True),
        lax.all_gather(expand_weight, ("fsdp", "ctx"), axis=0, tiled=True),
        lax.all_gather(shrink_weight, ("fsdp", "ctx"), axis=1, tiled=True),
        lax.all_gather(shrink_bias, ("fsdp", "ctx"), axis=0, tiled=True),
    )
    offsets = jnp.arange(half, dtype=jnp.int32)
    key_places = (slot_order[:, :, None] * half + offsets[None, None, :]).reshape(seqs, length)
    query_places = lax.dynamic_slice_in_dim(key_places, begin, rows, 1)
    query_groups = lax.dynamic_slice_in_dim(segments, begin, rows, 1)
    inputs = layer_input.reshape(count, model_width).astype(jnp.float32)
    unit_one, inverse_one = normalize_parts(inputs)
    normed_one = (unit_one * gain_one.astype(jnp.float32) + shift_one.astype(jnp.float32)).astype(
        jnp.bfloat16
    )
    project_flat = project_full.reshape(model_width, 3 * local_width)
    mixed = jnp.dot(normed_one, project_flat, preferred_element_type=jnp.float32).reshape(
        count, 3, local_width
    )
    bias_pair = project_bias.astype(jnp.float32)
    queries = (mixed[:, 0] + bias_pair[0]).astype(jnp.bfloat16).reshape(seqs, rows, local_width)
    keys = mixed[:, 1].astype(jnp.bfloat16).reshape(seqs, rows, local_width)
    values = (mixed[:, 2] + bias_pair[1]).astype(jnp.bfloat16).reshape(seqs, rows, local_width)
    keys_all, values_all = (
        lax.all_gather(keys, "ctx", axis=1, tiled=True),
        lax.all_gather(values, "ctx", axis=1, tiled=True),
    )
    attended, tops, totals = attend_forward(
        queries, keys_all, values_all, query_places, query_groups, key_places, segments, pairs
    )
    attended_flat = attended.reshape(count, local_width)
    branch = lax.psum(jnp.dot(attended_flat, output_full, preferred_element_type=jnp.float32), "tp")
    middle = inputs + branch + out_bias.astype(jnp.float32)
    unit_two, inverse_two = normalize_parts(middle)
    normed_two = (unit_two * gain_two.astype(jnp.float32) + shift_two.astype(jnp.float32)).astype(
        jnp.bfloat16
    )
    before = jnp.dot(
        normed_two, expand_full, preferred_element_type=jnp.float32
    ) + expand_bias.astype(jnp.float32)
    active_value, gelu_pull = jax.vjp(partial(jax.nn.gelu, approximate=True), before)
    active = active_value.astype(jnp.bfloat16)
    feed = lax.psum(
        jnp.dot(active, shrink_full, preferred_element_type=jnp.float32).astype(jnp.bfloat16), "tp"
    ).astype(jnp.float32)
    layer_output = (
        (middle + feed + shrink_add.astype(jnp.float32))
        .astype(jnp.bfloat16)
        .reshape(seqs, rows, model_width)
    )
    gain_back, project_again, output_back, gain_two_back, expand_back, shrink_back = (
        lax.all_gather(first_gain, ("fsdp", "ctx"), axis=0, tiled=True),
        lax.all_gather(project_weight, ("fsdp", "ctx"), axis=0, tiled=True),
        lax.all_gather(output_weight, ("fsdp", "ctx"), axis=1, tiled=True),
        lax.all_gather(second_gain, ("fsdp", "ctx"), axis=0, tiled=True),
        lax.all_gather(expand_weight, ("fsdp", "ctx"), axis=0, tiled=True),
        lax.all_gather(shrink_weight, ("fsdp", "ctx"), axis=1, tiled=True),
    )
    project_back = project_again.reshape(model_width, 3 * local_width)
    slope = cotangent.reshape(count, model_width).astype(jnp.float32)
    shrink_bias_delta = jnp.sum(slope, axis=0)
    slope_low = slope.astype(jnp.bfloat16)
    shrink_weight_delta = contract_rows(active, slope_low)
    active_slope = times_transpose(slope_low, shrink_back)
    before_slope = gelu_pull(active_slope)[0].astype(jnp.bfloat16)
    expand_bias_delta = jnp.sum(before_slope.astype(jnp.float32), axis=0)
    expand_weight_delta = contract_rows(normed_two, before_slope)
    normed_two_slope = lax.psum(
        times_transpose(before_slope, expand_back).astype(jnp.bfloat16), "tp"
    ).astype(jnp.float32)
    back_two, gain_two_delta, shift_two_delta = norm_backward(
        normed_two_slope, unit_two, inverse_two, gain_two_back.astype(jnp.float32)
    )
    middle_slope = slope + back_two
    output_bias_delta = jnp.sum(middle_slope, axis=0)
    middle_low = middle_slope.astype(jnp.bfloat16)
    output_weight_delta = contract_rows(attended_flat, middle_low)
    attended_slope = (
        times_transpose(middle_low, output_back)
        .astype(jnp.bfloat16)
        .reshape(seqs, rows, local_width)
    )
    query_slope, key_part, value_part = attend_backward(
        queries,
        keys_all,
        values_all,
        attended_slope,
        tops,
        totals,
        query_places,
        query_groups,
        key_places,
        segments,
        pairs,
    )
    key_slope, value_slope = (
        lax.psum_scatter(
            key_part.astype(jnp.bfloat16), "ctx", scatter_dimension=1, tiled=True
        ).astype(jnp.float32),
        lax.psum_scatter(
            value_part.astype(jnp.bfloat16), "ctx", scatter_dimension=1, tiled=True
        ).astype(jnp.float32),
    )
    key_low = key_slope.astype(jnp.bfloat16)
    value_low = value_slope.astype(jnp.bfloat16)
    project_slope = jnp.stack([query_slope, key_low, value_low], axis=2).reshape(
        count, 3 * local_width
    )
    project_weight_delta = contract_rows(normed_one, project_slope).reshape(
        model_width, 3, local_width
    )
    project_bias_delta = jnp.stack(
        [
            jnp.sum(query_slope.reshape(count, local_width).astype(jnp.float32), axis=0),
            jnp.sum(value_low.reshape(count, local_width).astype(jnp.float32), axis=0),
        ]
    )
    normed_one_slope = lax.psum(
        times_transpose(project_slope, project_back).astype(jnp.bfloat16), "tp"
    ).astype(jnp.float32)
    back_one, gain_one_delta, shift_one_delta = norm_backward(
        normed_one_slope, unit_one, inverse_one, gain_back.astype(jnp.float32)
    )
    input_delta = (middle_slope + back_one).reshape(seqs, rows, model_width)
    (
        part_gain_one,
        part_shift_one,
        part_project,
        part_output,
        part_out_bias,
        part_gain_two,
        part_shift_two,
        part_expand,
        part_shrink,
        part_shrink_bias,
    ) = (
        lax.psum_scatter(
            gain_one_delta.astype(jnp.bfloat16), "fsdp", scatter_dimension=0, tiled=True
        ).astype(jnp.float32),
        lax.psum_scatter(
            shift_one_delta.astype(jnp.bfloat16), "fsdp", scatter_dimension=0, tiled=True
        ).astype(jnp.float32),
        lax.psum_scatter(
            project_weight_delta.astype(jnp.bfloat16), "fsdp", scatter_dimension=0, tiled=True
        ).astype(jnp.float32),
        lax.psum_scatter(
            output_weight_delta.astype(jnp.bfloat16), "fsdp", scatter_dimension=1, tiled=True
        ).astype(jnp.float32),
        lax.psum_scatter(
            output_bias_delta.astype(jnp.bfloat16), "fsdp", scatter_dimension=0, tiled=True
        ).astype(jnp.float32),
        lax.psum_scatter(
            gain_two_delta.astype(jnp.bfloat16), "fsdp", scatter_dimension=0, tiled=True
        ).astype(jnp.float32),
        lax.psum_scatter(
            shift_two_delta.astype(jnp.bfloat16), "fsdp", scatter_dimension=0, tiled=True
        ).astype(jnp.float32),
        lax.psum_scatter(
            expand_weight_delta.astype(jnp.bfloat16), "fsdp", scatter_dimension=0, tiled=True
        ).astype(jnp.float32),
        lax.psum_scatter(
            shrink_weight_delta.astype(jnp.bfloat16), "fsdp", scatter_dimension=1, tiled=True
        ).astype(jnp.float32),
        lax.psum_scatter(
            shrink_bias_delta.astype(jnp.bfloat16), "fsdp", scatter_dimension=0, tiled=True
        ).astype(jnp.float32),
    )
    shares = (
        lax.psum_scatter(
            part_gain_one.astype(jnp.bfloat16), "ctx", scatter_dimension=0, tiled=True
        ).astype(jnp.float32),
        lax.psum_scatter(
            part_shift_one.astype(jnp.bfloat16), "ctx", scatter_dimension=0, tiled=True
        ).astype(jnp.float32),
        lax.psum_scatter(
            part_project.astype(jnp.bfloat16), "ctx", scatter_dimension=0, tiled=True
        ).astype(jnp.float32),
        lax.psum_scatter(
            part_output.astype(jnp.bfloat16), "ctx", scatter_dimension=1, tiled=True
        ).astype(jnp.float32),
        lax.psum_scatter(
            part_out_bias.astype(jnp.bfloat16), "ctx", scatter_dimension=0, tiled=True
        ).astype(jnp.float32),
        lax.psum_scatter(
            part_gain_two.astype(jnp.bfloat16), "ctx", scatter_dimension=0, tiled=True
        ).astype(jnp.float32),
        lax.psum_scatter(
            part_shift_two.astype(jnp.bfloat16), "ctx", scatter_dimension=0, tiled=True
        ).astype(jnp.float32),
        lax.psum_scatter(
            part_expand.astype(jnp.bfloat16), "ctx", scatter_dimension=0, tiled=True
        ).astype(jnp.float32),
        lax.psum_scatter(
            part_shrink.astype(jnp.bfloat16), "ctx", scatter_dimension=1, tiled=True
        ).astype(jnp.float32),
        lax.psum_scatter(
            part_shrink_bias.astype(jnp.bfloat16), "ctx", scatter_dimension=0, tiled=True
        ).astype(jnp.float32),
    )
    bias_sums = lax.psum((project_bias_delta, expand_bias_delta), ("fsdp", "ctx"))
    return (
        layer_output,
        input_delta,
        shares[0],
        shares[1],
        shares[2],
        bias_sums[0],
        shares[3],
        shares[4],
        shares[5],
        shares[6],
        shares[7],
        bias_sums[1],
        shares[8],
        shares[9],
    )


MESH = pl.DeviceIdType.MESH
VMEM_BYTES = 67043328
PIECES = 4


def dot_nn(left, right):
    return lax.dot_general(
        left, right, (((1,), (0,)), ((), ())), preferred_element_type=jnp.float32
    )


def dot_nt(left, right):
    return lax.dot_general(
        left, right, (((1,), (1,)), ((), ())), preferred_element_type=jnp.float32
    )


def remote(source, target, send, receive, device):
    return pltpu.make_async_remote_copy(
        src_ref=source,
        dst_ref=target,
        send_sem=send,
        recv_sem=receive,
        device_id=device,
        device_id_type=MESH,
    )


def aligned(index, size, unit=16):
    return pl.ds(pl.multiple_of(index * size, unit), size)


class Place:
    def __init__(self, line):
        self.line = line
        self.f = lax.axis_index("fsdp")
        self.c = lax.axis_index("ctx")
        self.t = lax.axis_index("tp")
        self.core_bit = lax.rem(self.c, 2)
        self.row_bit = self.c // 2
        self.core = self.c + 1 - 2 * self.core_bit
        self.row = lax.rem(self.c + 2, 4)
        self.other = lax.rem(self.core + 2, 4)
        self.core_device = (self.f, self.core, self.t)
        self.row_device = (self.f, self.row, self.t)
        self.tp_device = (self.f, self.c, 1 - self.t)
        self.ctx_devices = (self.core_device, self.row_device, (self.f, self.other, self.t))

    def line_device(self, f):
        return (f, self.c, self.t)

    def greet(self):
        barrier = pltpu.get_barrier_semaphore()
        others = [*self.ctx_devices, self.tp_device]
        for step in range(1, self.line):
            others.append(self.line_device(lax.rem(self.f + step, self.line)))
        for device in others:
            pl.semaphore_signal(barrier, 1, device_id=device, device_id_type=MESH)
        pl.semaphore_wait(barrier, len(others))

    def each(self, step, action):
        if step == 0:
            action(self.f, 0)
            return

        @pl.when(self.f - step >= 0)
        def _():
            action(self.f - step, 1)

        @pl.when(self.f + step < self.line)
        def _():
            action(self.f + step, -1)

    def can_pass(self, way):
        return self.f < self.line - 1 if way > 0 else self.f > 0


class Gather:
    def __init__(self, place, group, own, full, row_first, direct, sems):
        self.at, self.group, self.own, self.full = place, group, own, full
        self.row_first, self.direct = row_first, direct
        self.line_send, self.line_recv, self.row_send, self.row_recv, self.core_send, self.core_recv = sems
        self.shard = own.shape[0]

    def part(self, f, other):
        ctx = self.at.row if other else self.at.c
        return self.full.at[aligned(f * 4 + ctx, self.shard), :]

    def line_copy(self, f, way, other=0, own=False):
        part = self.part(f, other)
        return remote(
            self.own if own else part,
            part,
            self.line_send.at[self.group, other, (way + 1) // 2, f],
            self.line_recv.at[self.group, other, f],
            self.at.line_device(self.at.f + way),
        )

    def direct_copy(self, step, other):
        part = self.part(self.at.f, other)
        return remote(
            part if other else self.own,
            part,
            self.line_send.at[self.group, other, 0, step],
            self.line_recv.at[self.group, other, self.at.f],
            self.at.line_device(lax.rem(self.at.f + step, self.at.line)),
        )

    def row_copy(self, f, own=False):
        part = self.part(f, 0)
        return remote(
            self.own if own else part,
            part,
            self.row_send.at[self.group, f],
            self.row_recv.at[self.group, f],
            self.at.row_device,
        )

    def core_copy(self, f, other, own=False):
        part = self.part(f, other)
        return remote(
            self.own if own else part,
            part,
            self.core_send.at[self.group, other, f],
            self.core_recv.at[self.group, other, f],
            self.at.core_device,
        )

    def start_line(self, other=0):
        if self.direct:
            for step in range(1, self.at.line):
                self.direct_copy(step, other).start()
            return
        for way in (1, -1):

            @pl.when(self.at.can_pass(way))
            def _(way=way):
                self.line_copy(self.at.f, way, other, own=not other).start()

    def start_row(self):
        self.row_copy(self.at.f, own=True).start()

    def start_core(self):
        self.core_copy(self.at.f, 0, own=True).start()
        self.full[aligned(self.at.f * 4 + self.at.c, self.shard), :] = self.own[...]

    def line_step(self, step, other=0):
        def arrive(f, way):
            self.line_copy(f, 1, other).wait_recv()
            if not self.direct:

                @pl.when(self.at.can_pass(way))
                def _():
                    self.line_copy(f, way, other).start()

            self.core_copy(f, other).start()
            if not self.row_first:
                self.row_copy(f).start()

        self.at.each(step, arrive)

    def row_step(self, step):
        def arrive(f, _):
            self.row_copy(f).wait_recv()
            self.core_copy(f, 1).start()
            if self.row_first:
                self.start_line(1)

        self.at.each(step, arrive)

    def finish(self):
        for f in range(self.at.line):
            for other in (0, 1):
                self.core_copy(f, other).wait_recv()

    def drain(self):
        for step in range(1, self.at.line if self.direct else 0):
            for other in range(2 if self.row_first else 1):
                self.direct_copy(step, other).wait_send()
        for step in range(0 if self.direct else self.at.line):
            for way in (1, -1):
                source = self.at.f - step * way
                passed = (source >= 0) & (source < self.at.line) & self.at.can_pass(way)

                @pl.when(passed)
                def _(source=source, way=way):
                    for other in range(2 if self.row_first else 1):
                        self.line_copy(source, way, other).wait_send()

        if self.row_first:
            self.row_copy(self.at.f).wait_send()
        for f in range(self.at.line):
            if not self.row_first:
                self.row_copy(f).wait_send()
            for other in (0, 1):
                self.core_copy(f, other).wait_send()


class Scatter:
    def __init__(self, place, group, shard, sems, core, row, line, line_first=False):
        self.place, self.group, self.shard = place, group, shard
        self.core_send, self.core_recv, self.row_send, self.row_recv, self.line_send, self.line_recv = sems
        self.core, self.row, self.line = core, row, line
        self.row_blocks = 1 if line_first else place.line
        self.line_unit = 2 * shard if line_first else shard

    def core_copies(self):
        full, landed, _ = self.core
        at = self.place
        copies = []
        for f in range(at.line):
            for y in range(2):
                index = f * 2 + y
                copies.append(
                    remote(
                        full.at[aligned(f * 4 + 2 * y + 1 - at.core_bit, self.shard), :],
                        landed.at[pl.ds(index * self.shard, self.shard), :],
                        self.core_send.at[self.group, index],
                        self.core_recv.at[self.group, index],
                        at.core_device,
                    )
                )
        return copies

    def row_copies(self):
        summed, landed, _ = self.row
        at = self.place
        return [
            remote(
                summed.at[aligned(f * 2 + 1 - at.row_bit, self.shard), :],
                landed.at[pl.ds(f * self.shard, self.shard), :],
                self.row_send.at[self.group, f],
                self.row_recv.at[self.group, f],
                at.row_device,
            )
            for f in range(self.row_blocks)
        ]

    def line_copies(self):
        summed, landed, _ = self.line
        at = self.place
        copies = []
        for step in range(1, at.line):
            target = lax.rem(at.f + step, at.line)
            copies.append(
                remote(
                    summed.at[aligned(target, self.line_unit), :],
                    landed.at[pl.ds((step - 1) * self.line_unit, self.line_unit), :],
                    self.line_send.at[self.group, step],
                    self.line_recv.at[self.group, step],
                    at.line_device(target),
                )
            )
        return copies

    def start(self, stage):
        for copy in getattr(self, stage + "_copies")():
            copy.start()

    def core_finish(self):
        full, landed, summed = self.core
        at = self.place
        for index, copy in enumerate(self.core_copies()):
            copy.wait_recv()
            f, y = index // 2, index % 2
            own = full[aligned(f * 4 + 2 * y + at.core_bit, self.shard), :]
            other = landed[index * self.shard : (index + 1) * self.shard, :]
            summed[index * self.shard : (index + 1) * self.shard, :] = (
                own.astype(jnp.float32) + other.astype(jnp.float32)
            ).astype(summed.dtype)

    def row_finish(self):
        summed, landed, result = self.row
        at = self.place
        for f, copy in enumerate(self.row_copies()):
            copy.wait_recv()
            own = summed[aligned(f * 2 + at.row_bit, self.shard), :]
            other = landed[f * self.shard : (f + 1) * self.shard, :]
            result[f * self.shard : (f + 1) * self.shard, :] = (
                own.astype(jnp.float32) + other.astype(jnp.float32)
            ).astype(result.dtype)

    def line_finish(self):
        summed, landed, result = self.line
        at = self.place
        total = summed[aligned(at.f, self.line_unit), :].astype(jnp.float32)
        for step, copy in enumerate(self.line_copies()):
            copy.wait_recv()
            total = total + landed[step * self.line_unit : (step + 1) * self.line_unit, :].astype(jnp.float32)
        result[...] = total.astype(result.dtype)

    def drain(self, *stages):
        for stage in stages:
            for copy in getattr(self, stage + "_copies")():
                copy.wait_send()


class Total:
    def __init__(self, place, group, pack, landed, lines, sems):
        self.at, self.group, self.pack, self.landed, self.lines = place, group, pack, landed, lines
        self.send, self.recv = sems

    def ctx_copies(self):
        return [
            remote(
                self.pack.at[0],
                self.landed.at[role],
                self.send.at[self.group, 0, role],
                self.recv.at[self.group, 0, role],
                device,
            )
            for role, device in enumerate(self.at.ctx_devices)
        ]

    def line_copy(self, step, source):
        return remote(
            self.pack.at[1],
            self.lines.at[source],
            self.send.at[self.group, 1, step],
            self.recv.at[self.group, 1, step],
            self.at.line_device(lax.rem(self.at.f + step, self.at.line)),
        )

    def start(self):
        for copy in self.ctx_copies():
            copy.start()

    def pass_on(self):
        for copy in self.ctx_copies():
            copy.wait_recv()
        near = self.pack[0] + self.landed[0]
        self.pack[1] = near + (self.landed[1] + self.landed[2])
        for step in range(1, self.at.line):
            self.line_copy(step, self.at.f).start()

    def finish(self):
        for step in range(1, self.at.line):
            self.line_copy(step, lax.rem(self.at.f + self.at.line - step, self.at.line)).wait_recv()
        self.lines[self.at.f] = self.pack[1]
        total = self.lines[0]
        for f in range(1, self.at.line):
            total = total + self.lines[f]
        return total

    def drain(self):
        for copy in self.ctx_copies():
            copy.wait_send()
        for step in range(1, self.at.line):
            self.line_copy(step, self.at.f).wait_send()


def split_heads(source, store, scale):
    rows, width = source.shape
    for pair in range(width // 128):
        both = source[:, pair * 128 : (pair + 1) * 128].astype(jnp.float32) * scale
        head = lax.broadcasted_iota(jnp.int32, both.shape, 1) // HEAD_DIM
        for side in range(2):
            store[pair, side * rows : (side + 1) * rows, :] = jnp.where(
                head == side, both, 0.0
            ).astype(jnp.bfloat16)


def write_mask(r, at, key_slot, half):
    keys = aligned(key_slot, half)
    key_seg = r.seg[:, aligned(key_slot, half, 128)].astype(jnp.float32)
    key_part = jnp.broadcast_to(key_seg, (128, half)).T
    key_full = jnp.concatenate([key_part] * (half // 128), axis=1)
    shape = (half, half)
    key_place = r.order[0, key_slot] * half + lax.broadcasted_iota(jnp.int32, shape, 0)
    for part in range(2):
        query_slot = at.c * 2 + part
        query_seg = r.seg[:, aligned(query_slot, half, 128)].astype(jnp.float32)
        query_place = r.order[0, query_slot] * half + lax.broadcasted_iota(jnp.int32, shape, 1)
        allowed = (key_full == query_seg) & (key_place <= query_place)
        r.mask[keys, part * half : (part + 1) * half] = jnp.where(allowed, 0.0, NEGATIVE)


def attend_tile(r, slot, half, rows, width):
    keys = aligned(slot, half)
    mask = r.mask[keys, :]
    mask = jnp.concatenate([mask, mask], axis=1)
    for pair in range(width // 128):
        span = slice(pair * 128, (pair + 1) * 128)
        scores = dot_nt(r.kv[keys, span], r.heads[pair]) + mask
        before = r.top[pair : pair + 1, :]
        after = jnp.maximum(before, jnp.max(scores, axis=0, keepdims=True))
        raised = jnp.exp(scores - after)
        fade = jnp.exp(before - after)
        r.top[pair : pair + 1, :] = after
        r.total[pair : pair + 1, :] = r.total[pair : pair + 1, :] * fade + jnp.sum(
            raised, axis=0, keepdims=True
        )
        value = r.kv[keys, width + pair * 128 : width + (pair + 1) * 128].T
        step = dot_nn(value, raised.astype(jnp.bfloat16))
        for side in range(2):
            spot = slice((2 * pair + side) * HEAD_DIM, (2 * pair + side + 1) * HEAD_DIM)
            columns = slice(side * rows, (side + 1) * rows)
            r.mixed[spot, :] = (
                r.mixed[spot, :] * fade[:, columns]
                + step[side * HEAD_DIM : (side + 1) * HEAD_DIM, columns]
            )


def attend_finish(r, rows, width):
    for pair in range(width // 128):
        for side in range(2):
            spot = slice((2 * pair + side) * HEAD_DIM, (2 * pair + side + 1) * HEAD_DIM)
            columns = slice(side * rows, (side + 1) * rows)
            r.mixed[spot, :] = r.mixed[spot, :] / r.total[pair : pair + 1, columns]
        span = slice(pair * 128, (pair + 1) * 128)
        r.att[:, span] = r.mixed[span, :].T.astype(jnp.bfloat16)
    r.top[...] = r.top[...] + jnp.log(r.total[...])


def back_begin(r, rows, width):
    split_heads(r.att_slope, r.slopes, 1.0)
    for pair in range(width // 128):
        span = slice(pair * 128, (pair + 1) * 128)
        product = r.att_slope[:, span].astype(jnp.float32).T * r.mixed[span, :]
        for side in range(2):
            r.pull[pair : pair + 1, side * rows : (side + 1) * rows] = jnp.sum(
                product[side * HEAD_DIM : (side + 1) * HEAD_DIM, :], axis=0, keepdims=True
            )
    r.dq_sum[...] = jnp.zeros_like(r.dq_sum)


def back_tile(r, slot, target, half, rows, width):
    keys = aligned(slot, half)
    mask = r.mask[keys, :]
    mask = jnp.concatenate([mask, mask], axis=1)
    for pair in range(width // 128):
        span = slice(pair * 128, (pair + 1) * 128)
        value_span = slice(width + pair * 128, width + (pair + 1) * 128)
        key = r.kv[keys, span]
        scores = dot_nt(key, r.heads[pair]) + mask
        chance = jnp.exp(scores - r.top[pair : pair + 1, :])
        pulled = dot_nt(r.kv[keys, value_span], r.slopes[pair])
        slope = (chance * (pulled - r.pull[pair : pair + 1, :])).astype(jnp.bfloat16)
        target[:, value_span] = dot_nn(chance.astype(jnp.bfloat16), r.slopes[pair]).astype(
            jnp.bfloat16
        )
        target[:, span] = dot_nn(slope, r.heads[pair]).astype(jnp.bfloat16)
        step = dot_nn(key.T, slope)
        for side in range(2):
            spot = slice((2 * pair + side) * HEAD_DIM, (2 * pair + side + 1) * HEAD_DIM)
            r.dq_sum[spot, :] += step[
                side * HEAD_DIM : (side + 1) * HEAD_DIM, side * rows : (side + 1) * rows
            ]


def gelu_both(v):
    square = v * v
    inner = GELU_A * v * (1.0 + GELU_B * square)
    bent = jnp.tanh(inner)
    lifted = 0.5 * (1.0 + bent)
    slope = lifted + 0.5 * v * (1.0 - bent * bent) * (GELU_A * (1.0 + 3.0 * GELU_B * square))
    return (v * lifted, slope)


def wide(ref, these):
    return ref[these, :].astype(jnp.float32)


def layer_kernel(line, r):
    at = Place(line)
    shard = r.pv_own.shape[0]
    rows, model = r.x.shape
    width = r.att.shape[1]
    hidden = r.we.shape[1]
    half, some = rows // 2, rows // PIECES
    low = jnp.bfloat16
    gather_sems = (r.g_line_s, r.g_line_r, r.g_row_s, r.g_row_r, r.g_core_s, r.g_core_r)
    scatter_sems = (r.s_core_s, r.s_core_r, r.s_row_s, r.s_row_r, r.s_line_s, r.s_line_r)
    project_in = Gather(at, 0, r.pv_own, r.pv, False, False, gather_sems)
    output_in = Gather(at, 1, r.wo_own, r.wo, False, False, gather_sems)
    expand_in = Gather(at, 2, r.we_own, r.we, False, True, gather_sems)
    shrink_in = Gather(at, 3, r.ws_own, r.ws, True, True, gather_sems)

    gs, ge = r.ws, r.we
    shrink = Scatter(
        at, 0, shard, scatter_sems, (gs, r.gs1, r.gs2), (r.gs4, r.gs5, r.gs_out), (r.gs2, r.gs3, r.gs4), True
    )
    expand = Scatter(
        at, 1, shard, scatter_sems, (ge, r.ge1, r.ge2), (r.ge2, r.ge3, r.ge4), (r.ge4, r.ge5, r.ge_out)
    )
    output = Scatter(
        at, 2, shard, scatter_sems, (r.go, r.go1, r.go2), (r.go2, r.go3, r.go4), (r.go4, r.go5, r.go_out)
    )
    project = []
    for index in range(3):
        span = slice(index * width, (index + 1) * width)
        landed1, summed1, landed2, summed2, landed3 = [r["gp%d%d" % (index, stage)] for stage in range(1, 6)]
        project.append(
            Scatter(
                at,
                3 + index,
                shard,
                scatter_sems,
                (r.ws.at[:, span], landed1, summed1),
                (summed1, landed2, summed2),
                (summed2, landed3, r.gp_out.at[:, span]),
            )
        )
    vector = Scatter(
        at, 6, shard, scatter_sems, (r.gv, r.gv1, r.gv2), (r.gv2, r.gv3, r.gv4), (r.gv4, r.gv5, r.gv_out)
    )

    biases = Total(at, 0, r.bias_pack, r.bias_land, r.bias_line, (r.b_s, r.b_r))
    gains = Total(at, 1, r.gain_pack, r.gain_land, r.gain_line, (r.b_s, r.b_r))

    def kv_row(part):
        here = r.kv.at[aligned(at.c * 2 + part, half), :]
        return remote(here, here, r.kv_s.at[0, part], r.kv_r.at[0, part], at.row_device)

    def kv_core(part, other):
        here = r.kv.at[aligned((at.row if other else at.c) * 2 + part, half), :]
        return remote(
            here, here, r.kv_s.at[1 + other, part], r.kv_r.at[1 + other, part], at.core_device
        )

    def tp_copy(kind, piece):
        source, target = (
            (r.att, r.att_land),
            (r.up_send, r.up_land),
            (r.feed, r.feed_land),
            (r.down_send, r.down_land),
        )[kind]
        these = aligned(piece, some)
        return remote(
            source.at[these, :],
            target.at[these, :],
            r.tp_s.at[kind, piece],
            r.tp_r.at[kind, piece],
            at.tp_device,
        )

    wo_copy = remote(r.wo, r.wo_land, r.wo_s.at[0], r.wo_r.at[0], at.tp_device)

    def slopes_of(ctx, part):
        return r.hidden.at[aligned(ctx, half), part * 2 * width : (part + 1) * 2 * width]

    def back_core(far, part):
        return remote(
            slopes_of(at.other if far else at.core, part),
            r.kv_land.at[pl.ds((2 * far + part) * half, half), :],
            r.bk_s.at[far, part],
            r.bk_r.at[far, part],
            at.core_device,
        )

    def back_row(part):
        these = pl.ds(part * half, half)
        return remote(
            r.kv_pass.at[these, :],
            r.kv_land2.at[these, :],
            r.bk_s.at[2, part],
            r.bk_r.at[2, part],
            at.row_device,
        )

    active = r.hidden.at[0:rows, :]
    before_slope = r.hidden.at[rows : 2 * rows, :]

    r.turn[...] = jnp.zeros_like(r.turn)
    for index, ref in enumerate((r.gain1, r.shift1, r.bias_o, r.gain2, r.shift2, r.bias_s)):
        r.turn[index : index + 1, 0:shard] = ref[...].astype(jnp.float32)[None, :]
    for index in range(3):
        r.pv_own[:, index * width : (index + 1) * width] = r.wp[index]
    r.pv_own[:, 3 * width :] = r.turn[...].T[0:shard, :].astype(low)
    r.ebias[...] = r.ebias_own[...].astype(jnp.float32)[None, :]
    at.greet()
    for weight in (project_in, output_in):
        weight.start_line()
        weight.start_row()
        weight.start_core()

    @pl.loop(0, PIECES)
    def _(piece):
        these = aligned(piece, some)
        r.delta[these, :] = normalize_parts(wide(r.x, these))[0]

    for step in range(1, line):
        for weight in (project_in, output_in):
            weight.line_step(step)
        if step == line - 2:
            expand_in.start_line()
            shrink_in.start_line()
        project_in.row_step(step - 1)

        if step < line - 1:
            for slot in range(4 * step - 4, min(4 * step, 8)):
                write_mask(r, at, slot, half)
    shrink_in.start_row()
    shrink_in.start_core()
    expand_in.start_row()
    expand_in.start_core()
    project_in.row_step(line - 1)
    project_in.finish()
    r.vec[...] = r.pv[:, 3 * width :].astype(jnp.float32).T[0:8, :]
    gain, shift = r.vec[0:1, :], r.vec[1:2, :]

    @pl.loop(0, PIECES)
    def _(piece):
        these = aligned(piece, some)
        r.normed[these, :] = (r.delta[these, :] * gain + shift).astype(low)

    bias = r.pbias[...].astype(jnp.float32)
    for part in range(2):
        left = r.normed[part * half : (part + 1) * half, :]
        here = aligned(at.c * 2 + part, half)
        r.kv[here, 0:width] = dot_nn(left, r.pv[:, width : 2 * width]).astype(low)
        r.kv[here, width:] = (dot_nn(left, r.pv[:, 2 * width : 3 * width]) + bias[1:2, :]).astype(low)
        kv_row(part).start()
        kv_core(part, 0).start()
    shrink_in.row_step(0)
    r.att[...] = (dot_nn(r.normed[...], r.pv[:, 0:width]) + bias[0:1, :]).astype(low)
    split_heads(r.att, r.heads, SCALE)
    r.top[...] = jnp.full_like(r.top, NEGATIVE)
    r.total[...] = jnp.zeros_like(r.total)
    r.mixed[...] = jnp.zeros_like(r.mixed)
    for step in range(line):
        output_in.row_step(step)
    output_in.finish()
    wo_copy.start()

    @pl.loop(0, 8)
    def _(tile):
        @pl.when(tile == 2)
        def _():
            for part in range(2):
                kv_core(part, 0).wait_recv()

        for step in range(1, line):

            @pl.when(tile == step)
            def _(step=step):
                expand_in.line_step(step)

        for part in range(2):

            @pl.when(tile == 4 + 2 * part)
            def _(part=part):
                kv_row(part).wait_recv()
                kv_core(part, 1).start()

            @pl.when(tile == 5 + 2 * part)
            def _(part=part):
                kv_core(part, 1).wait_recv()

        far = jnp.where(lax.rem(tile, 2) == 0, at.row, at.other)
        ctx = jnp.where(tile < 2, at.c, jnp.where(tile < 4, at.core, far))
        part = jnp.where(tile < 4, lax.rem(tile, 2), (tile - 4) // 2)
        attend_tile(r, ctx * 2 + part, half, rows, width)

    attend_finish(r, rows, width)
    for piece in range(PIECES):
        tp_copy(0, piece).start()
    expand_in.row_step(0)
    for step in range(1, line):
        shrink_in.line_step(step, 0)
        expand_in.row_step(step)
        shrink_in.line_step(step, 1)
    shrink_in.finish()
    expand_in.finish()
    wo_copy.wait_recv()
    out_bias, gain2, shift2 = r.vec[2:3, :], r.vec[3:4, :], r.vec[4:5, :]

    def feed_forward(these):
        branch = dot_nt(r.att[these, :], r.wo[...]) + dot_nt(r.att_land[these, :], r.wo_land[...])
        middle = wide(r.x, these) + branch + out_bias
        r.mid[these, :] = middle
        unit, _ = normalize_parts(middle)
        normed = (unit * gain2 + shift2).astype(low)
        r.normed2[these, :] = normed
        for column in range(0, hidden, 512):
            span = slice(column, column + 512)
            value, slope = gelu_both(dot_nn(normed, r.we[:, span]) + r.ebias[:, span])
            active[these, span] = value.astype(low)
            before_slope[these, span] = (dot_nn(r.ct[these, :], r.ws[:, span]) * slope).astype(low)
        r.up_send[these, :] = dot_nt(before_slope[these, :], r.we[...]).astype(low)

    @pl.loop(0, PIECES // 2)
    def _(piece):
        tp_copy(0, piece).wait_recv()
        feed_forward(aligned(piece, some))
        tp_copy(1, piece).start()

    for piece in range(PIECES // 2, PIECES):
        tp_copy(0, piece).wait_recv()
    feed_forward(slice(half, rows))
    for piece in range(PIECES // 2, PIECES):
        tp_copy(1, piece).start()
    r.feed[...] = dot_nt(active[...], r.ws[...]).astype(low)
    for piece in range(PIECES):
        tp_copy(2, piece).start()
    for weight in (shrink_in, expand_in):
        weight.drain()
    r.turned[...] = r.ct[...].T
    for column in range(0, hidden, 512):
        span = slice(column, column + 512)
        gs[:, span] = dot_nn(r.turned[...], active[:, span]).astype(low)
    shrink.start("core")
    r.turned[...] = r.normed2[...].T
    for column in range(0, hidden, 512):
        span = slice(column, column + 512)
        ge[:, span] = dot_nn(r.turned[...], before_slope[:, span]).astype(low)
    expand.start("core")
    shrink.core_finish()
    shrink.start("line")
    r.bsum[...] = jnp.sum(before_slope[...].astype(jnp.float32), axis=0, keepdims=True)
    expand.core_finish()
    expand.start("row")
    r.vsum[...] = jnp.zeros_like(r.vsum)

    @pl.loop(0, PIECES)
    def _(piece):
        these = aligned(piece, some)
        tp_copy(1, piece).wait_recv()
        upstream = wide(r.up_send, these) + wide(r.up_land, these)
        unit, inverse = normalize_parts(r.mid[these, :])
        back, gain_delta, shift_delta = norm_backward(upstream, unit, inverse, gain2)
        slope = wide(r.ct, these)
        middle_slope = slope + back
        r.mids[these, :] = middle_slope
        r.vsum[2:3, :] += jnp.sum(middle_slope, axis=0, keepdims=True)
        r.vsum[3:4, :] += gain_delta[None]
        r.vsum[4:5, :] += shift_delta[None]
        r.vsum[5:6, :] += jnp.sum(slope, axis=0, keepdims=True)
        rounded = middle_slope.astype(low)
        r.normed2[these, :] = rounded
        r.att_slope[these, :] = dot_nn(rounded, r.wo[...]).astype(low)

    r.turn_wide[...] = jnp.zeros_like(r.turn_wide)
    r.turn_wide[0:8, :] = r.vsum[...]
    r.gv[...] = r.turn_wide[...].T.astype(low)
    vector.start("core")
    back_begin(r, rows, width)
    r.turned[...] = r.normed2[...].T
    r.go[...] = dot_nn(r.turned[...], r.att[...]).astype(low)
    output.start("core")

    @pl.loop(0, 8)
    def _(tile):
        odd = lax.rem(tile, 2)
        far = jnp.where(odd == 0, at.other, at.row)
        ctx = jnp.where(tile < 4, far, jnp.where(tile < 6, at.core, at.c))
        part = jnp.where(tile < 4, tile // 2, odd)
        back_tile(r, ctx * 2 + part, r.tile, half, rows, width)
        for index in range(2):

            @pl.when(part == index)
            def _(index=index):
                slopes_of(ctx, index)[...] = r.tile[...]

        for index in range(2):

            @pl.when(tile == 2 * index)
            def _(index=index):
                back_core(1, index).start()

            @pl.when(tile == 2 * index + 1)
            def _(index=index):
                back_core(1, index).wait_recv()
                landed = r.kv_land[(2 + index) * half : (3 + index) * half, :]
                r.kv_pass[index * half : (index + 1) * half, :] = (
                    r.tile[...].astype(jnp.float32) + landed.astype(jnp.float32)
                ).astype(low)
                back_row(index).start()

            @pl.when(tile == 4 + index)
            def _(index=index):
                back_core(0, index).start()

        @pl.when(tile == 1)
        def _():
            output.core_finish()
            output.start("row")
            vector.core_finish()
            vector.start("row")

        @pl.when(tile == 4)
        def _():
            expand.row_finish()
            expand.start("line")

    for pair in range(width // 128):
        span = slice(pair * 128, (pair + 1) * 128)
        r.dq[:, span] = (r.dq_sum[span, :] * SCALE).T.astype(low)

    r.delta[...] = dot_nt(r.dq[...], r.pv[:, 0:width])

    def down(part):
        back_core(0, part).wait_recv()
        back_row(part).wait_recv()
        these = slice(part * half, (part + 1) * half)
        total = slopes_of(at.c, part)[...].astype(jnp.float32)
        total = total + wide(r.kv_land, these) + wide(r.kv_land2, these)
        r.kv_low[these, :] = total.astype(low)
        r.down_send[these, :] = (
            r.delta[these, :] + dot_nt(r.kv_low[these, :], r.pv[:, width : 3 * width])
        ).astype(low)
        for step in range(PIECES // 2):
            tp_copy(3, part * (PIECES // 2) + step).start()

    down(0)
    shrink.drain("core")
    r.turned[...] = r.normed[...].T
    r.ws[:, 0:width] = dot_nn(r.turned[...], r.dq[...]).astype(low)
    project[0].start("core")
    shrink.line_finish()
    shrink.start("row")
    shrink_bias = r.vec[5:6, :]

    @pl.loop(0, PIECES)
    def _(piece):
        these = aligned(piece, some)
        tp_copy(2, piece).wait_recv()
        feed = (wide(r.feed, these) + wide(r.feed_land, these)).astype(low)
        r.out[these, :] = (r.mid[these, :] + feed.astype(jnp.float32) + shrink_bias).astype(low)

    project[0].core_finish()
    project[0].start("row")
    output.row_finish()
    output.start("line")
    vector.row_finish()
    vector.start("line")
    down(1)
    for piece in range(2):
        span = slice((1 + piece) * width, (2 + piece) * width)
        slopes = r.kv_low[:, piece * width : (piece + 1) * width]
        r.ws[:, span] = dot_nn(r.turned[...], slopes).astype(low)
        project[1 + piece].start("core")
    bias_row = jnp.concatenate(
        [
            r.bsum[...],
            jnp.sum(r.dq[...].astype(jnp.float32), axis=0, keepdims=True),
            jnp.sum(r.kv_low[:, width:].astype(jnp.float32), axis=0, keepdims=True),
        ],
        axis=1,
    )
    r.bias_pack[...] = jnp.zeros_like(r.bias_pack)
    for index in range(bias_row.shape[1] // 128):
        r.bias_pack[0, index : index + 1, :] = bias_row[:, index * 128 : (index + 1) * 128]

    biases.start()
    for piece in (1, 2):
        project[piece].core_finish()
        project[piece].start("row")
    project[0].row_finish()
    project[0].start("line")
    biases.pass_on()
    shrink.row_finish()
    expand.line_finish()
    output.line_finish()
    vector.line_finish()
    project[1].row_finish()
    project[1].start("line")
    r.gain_pack[0] = jnp.zeros_like(r.gain_pack[0])

    @pl.loop(0, PIECES)
    def _(piece):
        these = aligned(piece, some)
        tp_copy(3, piece).wait_recv()
        upstream = wide(r.down_send, these) + wide(r.down_land, these)
        unit, inverse = normalize_parts(wide(r.x, these))
        slope, gain_delta, shift_delta = norm_backward(upstream, unit, inverse, gain)
        r.delta[these, :] = r.mids[these, :] + slope
        r.gain_pack[0, 0:1, :] += gain_delta[None]
        r.gain_pack[0, 1:2, :] += shift_delta[None]

    gains.start()
    project[2].row_finish()
    project[2].start("line")
    gains.pass_on()
    r.turn_wide[0:8, :] = jnp.zeros_like(r.vsum)
    r.bias_out[...] = biases.finish()
    for piece in project:
        piece.line_finish()
    r.turn_wide[0:2, :] = gains.finish()
    r.gain_full[...] = r.turn_wide[...].T
    r.gv_out[...] = r.gv_out[...] + r.gain_full[aligned(at.f * 4 + at.c, shard), :]
    project_in.drain()
    output_in.drain()
    wo_copy.wait_send()
    for part in range(2):
        kv_row(part).wait_send()
        back_row(part).wait_send()
        for index in range(2):
            kv_core(part, index).wait_send()
            back_core(index, part).wait_send()
    for kind in range(4):
        for piece in range(PIECES):
            tp_copy(kind, piece).wait_send()
    biases.drain()
    gains.drain()
    shrink.drain("row", "line")
    for gradient in (expand, output, *project, vector):
        gradient.drain("core", "row", "line")


def finish_kernel(r):
    r.out_end[0] = r.out[...]
    r.delta_end[0] = r.delta[...]
    r.gs_end[...] = r.gs[...]
    r.ge_end[...] = r.ge[...]
    r.go_end[...] = r.go[...]
    width = r.go.shape[1]
    for index in range(3):
        r.gp_end[index] = r.gp[:, index * width : (index + 1) * width]
    vectors = r.gv[...].T
    shard = r.gv.shape[0]
    for index in range(6):
        r["gv%d" % index][...] = vectors[index, 0:shard]
    hidden = r.ebias.shape[0]
    for index in range(hidden // 128):
        r.ebias[pl.ds(index * 128, 128)] = r.biases[index, :]
    each = width // 128
    for index in range(2 * each):
        row, column = index // each, index % each
        place = hidden // 128 + index
        r.pbias[row : row + 1, column * 128 : (column + 1) * 128] = r.biases[place : place + 1, :]


class Refs(dict):
    __getattr__ = dict.__getitem__


def call(kernel, ins, outs, scratch, smem=(), identity=None):
    names = [*ins, *outs, *scratch]
    params = dict(vmem_limit_bytes=VMEM_BYTES)
    if identity is not None:
        params.update(collective_id=identity, has_side_effects=True)
    results = pl.pallas_call(
        lambda *refs: kernel(Refs(zip(names, refs))),
        out_shape=[jax.ShapeDtypeStruct(shape, dtype) for shape, dtype in outs.values()],
        in_specs=[
            pl.BlockSpec(memory_space=pltpu.SMEM if name in smem else pltpu.VMEM) for name in ins
        ],
        out_specs=[pl.BlockSpec(memory_space=pltpu.VMEM)] * len(outs),
        scratch_shapes=[
            pltpu.VMEM(*spec) if isinstance(spec, tuple) else spec for spec in scratch.values()
        ],
        compiler_params=pltpu.CompilerParams(**params),
    )(*ins.values())
    return Refs(zip(outs, results))


def by_kernels(
    layer_input,
    cotangent,
    segments,
    slot_order,
    first_gain,
    first_shift,
    project_weight,
    project_bias,
    output_weight,
    output_bias,
    second_gain,
    second_shift,
    expand_weight,
    expand_bias,
    shrink_weight,
    shrink_bias,
):
    low, full = jnp.bfloat16, jnp.float32
    line = lax.axis_size("fsdp")
    _, rows, model = layer_input.shape
    length = segments.shape[1]
    shard, _, width = project_weight.shape
    hidden = expand_weight.shape[1]
    pairs = width // 128
    half = rows // 2
    packed = 3 * width + 128
    two, one = 2 * line * shard, line * shard
    less = one - shard
    bias_rows = -(-(hidden + 2 * width) // 1024) * 8
    dma = lambda *shape: pltpu.SemaphoreType.DMA(shape)

    def stages(name, columns, sizes=(two, two, one, one, less)):
        return {"%s%d" % (name, index + 1): ((size, columns), low) for index, size in enumerate(sizes)}

    done = call(
        partial(layer_kernel, line),
        dict(
            x=layer_input.reshape(rows, model),
            ct=cotangent.reshape(rows, model),
            seg=segments,
            order=slot_order,
            gain1=first_gain,
            shift1=first_shift,
            bias_o=output_bias,
            gain2=second_gain,
            shift2=second_shift,
            bias_s=shrink_bias,
            wp=project_weight.transpose(1, 0, 2),
            pbias=project_bias,
            wo_own=output_weight.T,
            we_own=expand_weight,
            ws_own=shrink_weight.T,
            ebias_own=expand_bias,
        ),
        dict(
            out=((rows, model), low),
            delta=((rows, model), full),
            gs_out=((shard, hidden), full),
            ge_out=((shard, hidden), full),
            go_out=((shard, width), full),
            gp_out=((shard, 3 * width), full),
            gv_out=((shard, 128), full),
            bias_out=((bias_rows, 128), full),
        ),
        dict(
            pv_own=((shard, packed), low),
            pv=((model, packed), low),
            wo=((model, width), low),
            we=((model, hidden), low),
            ws=((model, hidden), low),
            kv=((length, 2 * width), low),
            vec=((8, model), full),
            ebias=((1, hidden), full),
            turn=((128, 128), full),
            turn_wide=((128, model), full),
            normed=((rows, model), low),
            normed2=((rows, model), low),
            turned=((model, rows), low),
            mask=((length, rows), full),
            heads=((pairs, 2 * rows, 128), low),
            slopes=((pairs, 2 * rows, 128), low),
            top=((8, 2 * rows), full),
            total=((8, 2 * rows), full),
            pull=((8, 2 * rows), full),
            mixed=((width, rows), full),
            dq_sum=((width, rows), full),
            att=((rows, width), low),
            att_slope=((rows, width), low),
            dq=((rows, width), low),
            tile=((half, 2 * width), low),
            mid=((rows, model), full),
            mids=((rows, model), full),
            hidden=((2 * rows, hidden), low),
            att_land=((rows, width), low),
            wo_land=((model, width), low),
            up_send=((rows, model), low),
            up_land=((rows, model), low),
            feed=((rows, model), low),
            feed_land=((rows, model), low),
            down_send=((rows, model), low),
            down_land=((rows, model), low),
            kv_land=((2 * rows, 2 * width), low),
            kv_pass=((rows, 2 * width), low),
            kv_land2=((rows, 2 * width), low),
            kv_low=((rows, 2 * width), low),
            bsum=((1, hidden), full),
            vsum=((8, model), full),
            go=((model, width), low),
            gv=((model, 128), low),
            **stages("gs", hidden, (two, two, 2 * less, 2 * shard, shard)),
            **stages("ge", hidden),
            **stages("go", width),
            **stages("gp0", width),
            **stages("gp1", width),
            **stages("gp2", width),
            **stages("gv", 128),
            bias_pack=((2, bias_rows, 128), full),
            bias_land=((3, bias_rows, 128), full),
            gain_pack=((2, 2, model), full),
            gain_land=((3, 2, model), full),
            gain_line=((line, 2, model), full),
            gain_full=((model, 128), full),
            bias_line=((line, bias_rows, 128), full),
            g_line_s=dma(5, 2, 2, line),
            g_line_r=dma(5, 2, line),
            g_row_s=dma(5, line),
            g_row_r=dma(5, line),
            g_core_s=dma(5, 2, line),
            g_core_r=dma(5, 2, line),
            s_core_s=dma(7, 2 * line),
            s_core_r=dma(7, 2 * line),
            s_row_s=dma(7, line),
            s_row_r=dma(7, line),
            s_line_s=dma(7, line),
            s_line_r=dma(7, line),
            wo_s=dma(1),
            wo_r=dma(1),
            kv_s=dma(3, 2),
            kv_r=dma(3, 2),
            tp_s=dma(4, PIECES),
            tp_r=dma(4, PIECES),
            bk_s=dma(3, 2),
            bk_r=dma(3, 2),
            b_s=dma(2, 2, max(line, 3)),
            b_r=dma(2, 2, max(line, 3)),
        ),
        smem=("order",),
        identity=0,
    )
    end = call(
        finish_kernel,
        dict(
            out=done.out,
            delta=done.delta,
            gs=done.gs_out,
            ge=done.ge_out,
            go=done.go_out,
            gp=done.gp_out,
            gv=done.gv_out,
            biases=done.bias_out,
        ),
        dict(
            out_end=(layer_input.shape, low),
            delta_end=(layer_input.shape, full),
            gs_end=((shard, hidden), full),
            ge_end=((shard, hidden), full),
            go_end=((shard, width), full),
            gp_end=((3, shard, width), full),
            **{"gv%d" % index: ((shard,), full) for index in range(6)},
            ebias=((hidden,), full),
            pbias=((2, width), full),
        ),
        {},
    )
    return (
        end.out_end,
        end.delta_end,
        end.gv0,
        end.gv1,
        end.gp_end.transpose(1, 0, 2),
        end.pbias,
        end.go_end.T,
        end.gv2,
        end.gv3,
        end.gv4,
        end.ge_end,
        end.ebias,
        end.gs_end.T,
        end.gv5,
    )


def solution(mesh):
    n_ctx, n_tp = mesh.shape["ctx"], mesh.shape["tp"]

    def choose(layer_input, *others):
        seqs, rows, model = layer_input.shape
        whole_tiles = model % (16 * n_ctx * mesh.shape["fsdp"]) == 0 and rows % 256 == 0
        if seqs == 1 and n_ctx == 4 and n_tp == 2 and whole_tiles:
            return by_kernels(layer_input, *others)
        return on_device(layer_input, *others)

    return jax.shard_map(
        choose,
        mesh=mesh,
        in_specs=(
            P("fsdp", "ctx", None),
            P("fsdp", "ctx", None),
            P("fsdp", None),
            P("fsdp", None),
            P(("fsdp", "ctx")),
            P(("fsdp", "ctx")),
            P(("fsdp", "ctx"), None, "tp"),
            P(None, "tp"),
            P("tp", ("fsdp", "ctx")),
            P(("fsdp", "ctx")),
            P(("fsdp", "ctx")),
            P(("fsdp", "ctx")),
            P(("fsdp", "ctx"), "tp"),
            P("tp"),
            P("tp", ("fsdp", "ctx")),
            P(("fsdp", "ctx")),
        ),
        out_specs=(
            P("fsdp", "ctx", None),
            P("fsdp", "ctx", None),
            P(("fsdp", "ctx")),
            P(("fsdp", "ctx")),
            P(("fsdp", "ctx"), None, "tp"),
            P(None, "tp"),
            P("tp", ("fsdp", "ctx")),
            P(("fsdp", "ctx")),
            P(("fsdp", "ctx")),
            P(("fsdp", "ctx")),
            P(("fsdp", "ctx"), "tp"),
            P("tp"),
            P("tp", ("fsdp", "ctx")),
            P(("fsdp", "ctx")),
        ),
        check_vma=False,
    )
```
